32 devices in a mesh: dp: 8 (over z, x), mp: 4 (over y, core).
Axes of the slice: x: 2, y: 2, z: 4, core: 2. Of those that a mesh axis runs over, the one named last changes fastest.
Arguments:
- block_input: bfloat16 [16384, 768], P('dp'), may hold values from -6 to 6
- segment_ids: int32 [16, 1024], P('dp'), may hold values from 0 to 7, never falling along the last dimension, each value on 1 to 256 neighbouring positions
- group_ids: int32 [16, 1024], P('dp'), may hold values from 0 to 3
- padding: int32 [16, 1024], P('dp'), may hold values 0 or 1
- ln1_gain: float32 [768], replicated, may hold values from 0.25 to 1.75
- ln1_bias: float32 [768], replicated, may hold values from -4 to 4
- w_qkv: bfloat16 [768, 3, 768], P(None, None, 'mp'), may hold values from -0.21875 to 0.21875
- b_qv: float32 [2, 768], P(None, 'mp'), may hold values from -1.5 to 1.5
- w_out: bfloat16 [768, 768], P('mp'), may hold values from -1.75 to 1.75
- b_out: float32 [768], replicated, may hold values from -4 to 4
- ln2_gain: float32 [768], replicated, may hold values from 0.25 to 1.75
- ln2_bias: float32 [768], replicated, may hold values from -4 to 4
- w_up: bfloat16 [768, 3072], P(None, 'mp'), may hold values from -0.21875 to 0.21875
- b_up: float32 [3072], P('mp'), may hold values from -6 to 6
- w_down: bfloat16 [3072, 768], P('mp'), may hold values from -0.15625 to 0.15625
- b_down: float32 [768], replicated, may hold values from -4 to 4
- cotangent: bfloat16 [16384, 768], P('dp'), may hold values from -6 to 6
Outputs:
- block_output: bfloat16 [16384, 768], P('dp')
- input_grad: float32 [16384, 768], P('dp')
- grad_ln1_gain: float32 [768], P('dp')
- grad_ln1_bias: float32 [768], P('dp')
- grad_w_qkv: float32 [768, 3, 768], P('dp', None, 'mp')
- grad_b_qv: float32 [2, 768], P(None, ('mp', 'dp'))
- grad_w_out: float32 [768, 768], P('mp', 'dp')
- grad_b_out: float32 [768], P('dp')
- grad_ln2_gain: float32 [768], P('dp')
- grad_ln2_bias: float32 [768], P('dp')
- grad_w_up: float32 [768, 3072], P('dp', 'mp')
- grad_b_up: float32 [3072], P(('mp', 'dp'))
- grad_w_down: float32 [3072, 768], P('mp', 'dp')
- grad_b_down: float32 [768], P('dp')
The draws below stay inside these ranges and needn't reach their ends.
Inputs may be any that keep to these rules, and one draw needn't show every extreme that they name: `segment_ids`: along each sequence the segment numbers never fall; a segment holds at most 256 tokens.
All inputs are finite; a program needn't handle non-finite values. No bound on the sum of `padding` on one device may be relied on, other than what follows from the above.
Results may differ from the reference program's by a relative error of at most 0.018.
Values may be sent and summed in bfloat16 or wider, within the bound.
No kernel may reach another device: no remote copies, remote signals or barrier semaphores. Data moves between devices by JAX's collectives and lax.ppermute only.
A program may use at most 128 MiB of HBM per device.

```python
import math
import jax
import jax.numpy as jnp
import numpy as np
from jax import lax

D = 768
HEADS = 12
HD = 64
FF = 3072
LEN = 1024
SEQS = 16
TOKENS = 16384
N_MP = 4


def touch_ends(entries, rng, least, largest):
    longest = entries.shape.index(max(entries.shape))
    spots = []
    for shift in (0, 1):
        where = [jax.random.randint(jax.random.fold_in(rng, axis), (), 0, length) for axis, length in enumerate(entries.shape)]
        where[longest] = (where[longest] + shift) % entries.shape[longest]
        spots.append(tuple(where))
    return entries.at[spots[0]].set(least).at[spots[1]].set(largest)


def strengthened(values, stream_key, source, target, parts, factor):
    owner, partner = [(jnp.arange(values.shape[dim]) // (values.shape[dim] // parts)).reshape([-1 if axis == dim else 1 for axis in range(values.ndim)]) for dim in (source, target)]
    chosen = jax.random.permutation(stream_key, parts)[partner]
    strong = (owner == chosen) | (owner == (partner + parts // 2) % parts)
    return jnp.where(strong, factor * values, values)


def steps_of(stream_key, extent, pieces, least, top_value):
    loudness = 1.0
    for dim, blocks in pieces:
        draws = jax.random.uniform(jax.random.fold_in(jax.random.fold_in(stream_key, 6), dim), (blocks,), jnp.float32, least / len(pieces), top_value / len(pieces))
        loudness = loudness * jnp.repeat(jnp.exp(draws), extent[dim] // blocks).reshape((-1,) + (1,) * (len(extent) - 1 - dim))
    return loudness


def profile(amount, total, bound, lean):
    portions = [(1 << 20) // math.isqrt(grade ** lean) + 1 for grade in range(2, amount + 1)]
    rest, counts = total - bound - (amount - 1), [1] * (amount - 1)
    while rest > 0:
        free = [i for i in range(amount - 1) if counts[i] < bound]
        mass, remaining = sum([portions[i] for i in free]), rest
        for i in free:
            more = min(bound - counts[i], max(1, remaining * portions[i] // mass), rest)
            counts[i] = counts[i] + more
            rest = rest - more
    return np.array([bound] + counts)


def ragged_sizes(key, amount, total, bound, skew):
    if amount == 2:
        one = jax.random.randint(key, (), max(1, total - bound), min(bound, total - 1) + 1)
        return jnp.stack([one, total - one])
    tallies = jnp.asarray(profile(amount, total, bound, skew), jnp.int32)
    pairs = (amount - 1) // 2
    source_of, taker = tallies[1:1 + 2 * pairs:2], tallies[2:2 + 2 * pairs:2]
    margin = jnp.minimum(source_of - 1, bound - taker)
    moved = jax.random.randint(jax.random.fold_in(key, 1), (pairs,), 0, 1 << 20) % (margin + 1)
    tallies = tallies.at[1:1 + 2 * pairs:2].set(source_of - moved).at[2:2 + 2 * pairs:2].set(taker + moved)
    return tallies[jax.random.permutation(jax.random.fold_in(key, 2), amount)]


def noise(stream_key, shape, spread, bound, pieces=(), held_as=jnp.bfloat16):
    gain = steps_of(stream_key, shape, pieces, -0.22, 0.18) if pieces else 1.0
    array = jax.random.normal(stream_key, shape, jnp.float32) * spread * gain
    return jnp.minimum(jnp.maximum(array, -bound), bound).astype(held_as)


def heavy_noise(rng, extent, spread, limit, pieces, heavy, kind=jnp.bfloat16):
    result = spread * jax.random.normal(rng, extent, jnp.float32)
    if pieces:
        result = result * steps_of(rng, extent, pieces, -0.22, 0.18)
    return jnp.clip(strengthened(result, jax.random.fold_in(rng, 3), *heavy), -limit, limit).astype(kind)


def setup_inputs(seed: int = 0) -> dict:
    seeds = jax.random.split(jax.random.key(seed), 18)
    block_input = noise(seeds[0], (TOKENS, D), 1.0, 6.0, ((0, 8),))
    segment_ids = jax.vmap(lambda own: jnp.searchsorted(jnp.cumsum(ragged_sizes(own, 8, LEN, LEN // 4, 1)), jnp.arange(LEN), side="right"))(jax.random.split(seeds[1], SEQS)).reshape((SEQS, LEN)).astype(jnp.int32)
    group_ids = touch_ends(jax.random.randint(seeds[2], (SEQS, LEN), 0, 4), jax.random.fold_in(seeds[2], 1), 0, 3).astype(jnp.int32)
    padding = touch_ends((jax.random.randint(seeds[3], (SEQS, LEN), 0, 8) < 1).astype(jnp.int32), jax.random.fold_in(seeds[3], 1), 0, 1)
    ln1_gain = jnp.clip(1.0 + 0.15 * jax.random.normal(seeds[4], (D,), jnp.float32), 0.25, 1.75)
    ln1_bias = noise(seeds[5], (D,), 0.3, 4.0, (), jnp.float32)
    w_qkv = noise(seeds[6], (D, 3, D), D ** -0.5, 0.21875, ((2, 4),))
    b_qv = noise(seeds[7], (2, D), 0.1, 1.5, ((1, 4),), jnp.float32)
    w_out = noise(seeds[8], (D, D), (D // 64) ** -0.5, 1.75, ((0, 4),))
    b_out = noise(seeds[9], (D,), 0.3, 4.0, (), jnp.float32)
    ln2_gain = jnp.clip(1.0 + 0.15 * jax.random.normal(seeds[10], (D,), jnp.float32), 0.25, 1.75)
    ln2_bias = noise(seeds[11], (D,), 0.3, 4.0, (), jnp.float32)
    w_up = noise(seeds[12], (D, FF), D ** -0.5, 0.21875, ((1, 4),))
    b_up = noise(seeds[13], (FF,), 0.5, 6.0, ((0, 4),), jnp.float32)
    w_down = noise(seeds[14], (FF, D), (FF // 2) ** -0.5, 0.15625, ((0, 4),))
    b_down = noise(seeds[15], (D,), 0.3, 4.0, (), jnp.float32)
    cotangent = heavy_noise(seeds[16], (TOKENS, D), 1.0, 6.0, ((0, 8),), (0, 1, 8, 2.0))
    return dict(block_input=block_input, segment_ids=segment_ids, group_ids=group_ids, padding=padding, ln1_gain=ln1_gain, ln1_bias=ln1_bias, w_qkv=w_qkv, b_qv=b_qv, w_out=w_out, b_out=b_out, ln2_gain=ln2_gain, ln2_bias=ln2_bias, w_up=w_up, b_up=b_up, w_down=w_down, b_down=b_down, cotangent=cotangent)


@jax.custom_vjp
def low(v):
    return lax.optimization_barrier(v.astype(jnp.bfloat16)).astype(jnp.float32)

@jax.custom_vjp
def low_back(v):
    return v

def low_keep(v):
    return (low(v), None)

def low_pass(kept, grad):
    return (grad,)

def back_keep(v):
    return (v, None)

def back_low(kept, grad):
    return (low(grad),)
low.defvjp(low_keep, low_pass)
low_back.defvjp(back_keep, back_low)

def layer_norm(values):
    average = lax.optimization_barrier(jnp.mean(values, -1, keepdims=True))
    centered = values - average
    variance = lax.optimization_barrier(jnp.mean(centered * centered, -1, keepdims=True))
    return centered * lax.rsqrt(variance + 1e-05)

def make_allowed(segment_row, group_row, padding_row):
    position = jnp.arange(segment_row.shape[0])
    same_segment = segment_row[:, None] == segment_row[None, :]
    earlier = group_row[None, :] <= group_row[:, None]
    visible = padding_row[None, :] == 0
    return same_segment & earlier & visible | (position[:, None] == position[None, :])

def attend_sequence(operands):
    queries, key_rows, value_rows, segment_row, group_row, padding_row = operands
    allowed = make_allowed(segment_row, group_row, padding_row)
    scores = jnp.einsum('qhd,khd->hqk', queries, key_rows, precision=lax.Precision.HIGHEST) * 0.125
    scores = low_back(scores)
    scores = jnp.where(allowed[None], scores, -1e+30)
    softmax_out = low(jax.nn.softmax(scores, axis=-1))
    return jnp.einsum('hqk,khd->qhd', softmax_out, value_rows, precision=lax.Precision.HIGHEST)

def reference(block_input, segment_ids, group_ids, padding, ln1_gain, ln1_bias, w_qkv, b_qv, w_out, b_out, ln2_gain, ln2_bias, w_up, b_up, w_down, b_down, cotangent):
    floats = tuple((argument.astype(jnp.float32) for argument in (block_input, ln1_gain, ln1_bias, w_qkv, b_qv, w_out, b_out, ln2_gain, ln2_bias, w_up, b_up, w_down, b_down)))

    def forward(stream, gain_one, bias_one, weight_qkv, bias_qv, weight_out, bias_out, gain_two, bias_two, weight_up, bias_up, weight_down, bias_down):
        row_count = stream.shape[0]
        normed_one = low(layer_norm(stream) * gain_one + bias_one)
        projected = jnp.einsum('td,dje->tje', normed_one, weight_qkv, precision=lax.Precision.HIGHEST)
        queries = low_back(low(projected[:, 0] + bias_qv[0]))
        key_rows = low_back(low(projected[:, 1]))
        value_rows = low_back(low(projected[:, 2] + bias_qv[1]))
        block_shape = (SEQS, LEN, HEADS, HD)
        context = lax.map(jax.checkpoint(attend_sequence), (queries.reshape(block_shape), key_rows.reshape(block_shape), value_rows.reshape(block_shape), segment_ids, group_ids, padding))
        context = low_back(low(context.reshape(row_count, D)))
        partials = jnp.einsum('tgc,gce->gte', context.reshape(row_count, N_MP, D // N_MP), weight_out.reshape(N_MP, D // N_MP, D), precision=lax.Precision.HIGHEST)
        attn_out = low_back(lax.optimization_barrier(jnp.sum(low(partials), 0))) + bias_out
        residual = stream + attn_out
        normed_two = low(layer_norm(residual) * gain_two + bias_two)
        up_proj = low_back(jnp.dot(normed_two, weight_up, precision=lax.Precision.HIGHEST) + bias_up)
        hidden = low(jax.nn.gelu(up_proj, approximate=False))
        partials_two = jnp.einsum('tgc,gce->gte', hidden.reshape(row_count, N_MP, FF // N_MP), weight_down.reshape(N_MP, FF // N_MP, D), precision=lax.Precision.HIGHEST)
        mlp_out = low_back(lax.optimization_barrier(jnp.sum(low(partials_two), 0))) + bias_down
        return residual + mlp_out
    output, backward = jax.vjp(forward, *floats)
    grads = backward(cotangent.astype(jnp.float32))
    return (output.astype(jnp.bfloat16), grads[0], grads[1], grads[2], grads[3], grads[4], grads[5], grads[6], grads[7], grads[8], grads[9], grads[10], grads[11], grads[12])
```

```python
import functools

import jax
import jax.numpy as jnp
from jax import lax
from jax.experimental import pallas as pl
from jax.experimental.pallas import tpu as pltpu
from jax.sharding import PartitionSpec as P

HD = 64
QB = 128
MASKED = -1e30
EPS = 1e-05
LOG2E = 1.4426950408889634
F32 = jnp.float32
BF16 = jnp.bfloat16
NT = (((1,), (1,)), ((), ()))
NN = (((1,), (0,)), ((), ()))
TN = (((0,), (0,)), ((), ()))


def mm(a, b, dims):
    return lax.dot_general(a, b, dims, preferred_element_type=F32)


def params(mib):
    return pltpu.CompilerParams(vmem_limit_bytes=mib * 1024 * 1024)


def cost(flops, traffic, trans=0):
    return pl.CostEstimate(flops=int(flops), bytes_accessed=int(traffic), transcendentals=int(trans))


def whole(shape):
    return pl.BlockSpec(shape, lambda *ids: (0,) * len(shape))


def rows(tile, width):
    return pl.BlockSpec((tile, width), lambda i, *rest: (i, 0))


def sds(shape, dtype):
    return jax.ShapeDtypeStruct(shape, dtype)


def norm_stats(values):
    average = jnp.mean(values, -1, keepdims=True)
    centered = values - average
    variance = jnp.mean(centered * centered, -1, keepdims=True)
    scale = lax.rsqrt(variance + EPS)
    return centered * scale, scale


def norm_back(unit, scale, upstream):
    first = jnp.mean(upstream, -1, keepdims=True)
    second = jnp.mean(upstream * unit, -1, keepdims=True)
    return scale * (upstream - first - unit * second)


def add_rows(ref, values, first):
    total = jnp.sum(values, 0, keepdims=True)

    @pl.when(first)
    def _():
        ref[...] = total

    @pl.when(jnp.logical_not(first))
    def _():
        ref[...] += total


def add_to(ref, values, first):
    @pl.when(first)
    def _():
        ref[...] = values

    @pl.when(jnp.logical_not(first))
    def _():
        ref[...] += values


def project_kernel(x_ref, gain_ref, bias_ref, wt_ref, qkv_bias_ref, n1_ref, q_ref, k_ref, v_ref):
    unit, _ = norm_stats(x_ref[...].astype(F32))
    normed = (unit * gain_ref[...] + bias_ref[...]).astype(BF16)
    n1_ref[...] = normed
    width = q_ref.shape[1]
    for place, out in enumerate((q_ref, k_ref, v_ref)):
        cols = slice(place * width, (place + 1) * width)
        out[...] = (mm(normed, wt_ref[cols, :], NT) + qkv_bias_ref[:, cols]).astype(BF16)


def project(x, gain, bias, wt, qkv_bias):
    tokens, d = x.shape
    width = wt.shape[0] // 3
    tile = min(512, tokens)
    return pl.pallas_call(
        project_kernel,
        grid=(tokens // tile,),
        in_specs=[rows(tile, d), whole((1, d)), whole((1, d)), whole(wt.shape), whole((1, 3 * width))],
        out_specs=[rows(tile, d)] + [rows(tile, width)] * 3,
        out_shape=[sds((tokens, d), BF16)] + [sds((tokens, width), BF16)] * 3,
        compiler_params=params(40),
        cost_estimate=cost(6 * tokens * d * width, tokens * (4 * d + 6 * width) + 6 * d * width),
        name="norm_project",
    )(x, gain, bias, wt, qkv_bias)


def stack_pair(values):
    lane = lax.broadcasted_iota(jnp.int32, values.shape, 1)
    zero = jnp.zeros_like(values)
    return jnp.concatenate(
        [jnp.where(lane < HD, values, zero), jnp.where(lane >= HD, values, zero)], 0
    )


def mask_bias(code_ref, low, high, start, query_start):
    codes = code_ref[pl.ds(start, QB), :]
    key_at = lax.broadcasted_iota(jnp.int32, (QB, QB), 0) + start
    query_at = lax.broadcasted_iota(jnp.int32, (QB, QB), 1) + query_start
    allowed = ((codes >= low) & (codes <= high)) | (key_at == query_at)
    bias = jnp.where(allowed, jnp.float32(0), jnp.float32(MASKED))
    return jnp.concatenate([bias, bias], 1)


def attend_kernel(
    start_ref, count_ref, q_ref, k_ref, v_ref, code_ref, low_ref, high_ref, w_ref,
    ctx_ref, part_ref, lse_ref, acc_ref, stat_ref,
):
    sequence, block = pl.program_id(0), pl.program_id(1)
    place = sequence * pl.num_programs(1) + block
    pairs = q_ref.shape[1] // QB
    stacked = [stack_pair(q_ref[:, p * QB : (p + 1) * QB]) for p in range(pairs)]
    low, high = low_ref[0], high_ref[0]
    acc_ref[...] = jnp.zeros_like(acc_ref)
    stat_ref[0] = jnp.full(stat_ref.shape[1:], MASKED, F32)
    stat_ref[1] = jnp.zeros(stat_ref.shape[1:], F32)

    def step(turn, carry):
        start = pl.multiple_of(start_ref[place] + turn * QB, 16)
        bias = mask_bias(code_ref, low, high, start, block * QB)
        for p in range(pairs):
            cols = slice(p * QB, (p + 1) * QB)
            scores = mm(k_ref[pl.ds(start, QB), cols], stacked[p], NT) * (0.125 * LOG2E) + bias
            old = stat_ref[0, p : p + 1, :]
            top = jnp.maximum(old, jnp.max(scores, 0, keepdims=True))
            shrink = jnp.exp2(old - top)
            weights = jnp.exp2(scores - top)
            stat_ref[0, p : p + 1, :] = top
            stat_ref[1, p : p + 1, :] = stat_ref[1, p : p + 1, :] * shrink + jnp.sum(
                weights, 0, keepdims=True
            )
            acc_ref[p] = acc_ref[p] * shrink + mm(
                v_ref[pl.ds(start, QB), cols], weights.astype(BF16), TN
            )
        return carry

    lax.fori_loop(0, count_ref[place], step, 0)
    row = lax.broadcasted_iota(jnp.int32, (QB, QB), 0)
    for p in range(pairs):
        total = stat_ref[1, p : p + 1, :]
        lse_ref[0, p : p + 1, :] = stat_ref[0, p : p + 1, :] + jnp.log2(total)
        scaled = acc_ref[p] * (1.0 / total)
        both = jnp.where(row < HD, scaled[:, :QB], scaled[:, QB:])
        ctx_ref[:, p * QB : (p + 1) * QB] = both.T.astype(BF16)
    part_ref[...] = mm(ctx_ref[...], w_ref[...], NN).astype(BF16)


def attend(starts, counts, q, k, v, codes, low, high, w_out):
    tokens, width = q.shape
    sequences = codes.shape[0]
    length = tokens // sequences
    blocks = length // QB
    d = w_out.shape[1]
    pairs = width // QB
    block = lambda s, i, *rest: (s * blocks + i, 0)
    rank3 = lambda s, i, *rest: (s * blocks + i, 0, 0)
    whole_sequence = pl.BlockSpec((length, width), lambda s, i, *rest: (s, 0))
    return pl.pallas_call(
        attend_kernel,
        grid_spec=pltpu.PrefetchScalarGridSpec(
            num_scalar_prefetch=2,
            grid=(sequences, blocks),
            in_specs=[
                pl.BlockSpec((QB, width), block),
                whole_sequence,
                whole_sequence,
                pl.BlockSpec((None, length, QB), lambda s, i, *rest: (s, 0, 0)),
                pl.BlockSpec((1, 1, QB), rank3),
                pl.BlockSpec((1, 1, QB), rank3),
                whole(w_out.shape),
            ],
            out_specs=[
                pl.BlockSpec((QB, width), block),
                pl.BlockSpec((QB, d), block),
                pl.BlockSpec((1, 8, 2 * QB), rank3),
            ],
            scratch_shapes=[
                pltpu.VMEM((pairs, QB, 2 * QB), F32),
                pltpu.VMEM((2, 8, 2 * QB), F32),
            ],
        ),
        out_shape=[
            sds((tokens, width), BF16),
            sds((tokens, d), BF16),
            sds((sequences * blocks, 8, 2 * QB), F32),
        ],
        compiler_params=params(40),
        cost_estimate=cost(12e9, 10e6),
        name="attend_forward",
    )(starts, counts, q, k, v, codes, low, high, w_out)


def attend_back_kernel(
    start_ref, count_ref, q_ref, k_ref, v_ref, ctx_ref, grad_ref, lse_ref, code_ref, low_ref, high_ref,
    dq_ref, dk_ref, dv_ref, dq_acc, dk_acc, dv_acc,
):
    sequence, block = pl.program_id(0), pl.program_id(1)
    place = sequence * pl.num_programs(1) + block
    pairs = q_ref.shape[1] // QB

    @pl.when(block == 0)
    def _():
        dk_acc[...] = jnp.zeros_like(dk_acc)
        dv_acc[...] = jnp.zeros_like(dv_acc)

    low, high = low_ref[0], high_ref[0]
    stacked, upstream, delta = [], [], []
    for p in range(pairs):
        cols = slice(p * QB, (p + 1) * QB)
        stacked.append(stack_pair(q_ref[:, cols]))
        upstream.append(stack_pair(grad_ref[:, cols]))
        turned = (ctx_ref[:, cols].astype(F32) * grad_ref[:, cols].astype(F32)).T
        delta.append(
            jnp.concatenate(
                [jnp.sum(turned[:HD], 0, keepdims=True), jnp.sum(turned[HD:], 0, keepdims=True)], 1
            )
        )
    dq_acc[...] = jnp.zeros_like(dq_acc)

    def step(turn, carry):
        start = pl.multiple_of(start_ref[place] + turn * QB, 16)
        here = pl.ds(start, QB)
        bias = mask_bias(code_ref, low, high, start, block * QB)
        for p in range(pairs):
            cols = slice(p * QB, (p + 1) * QB)
            keys = k_ref[here, cols]
            scores = mm(keys, stacked[p], NT) * (0.125 * LOG2E) + bias
            weights = jnp.exp2(scores - lse_ref[0, p : p + 1, :])
            prob_grad = mm(v_ref[here, cols], upstream[p], NT)
            score_grad = (weights * (prob_grad - delta[p])).astype(BF16)
            dv_acc[here, cols] += mm(weights.astype(BF16), upstream[p], NN)
            dk_acc[here, cols] += mm(score_grad, stacked[p], NN)
            dq_acc[p] += mm(keys, score_grad, TN)
        return carry

    lax.fori_loop(0, count_ref[place], step, 0)
    row = lax.broadcasted_iota(jnp.int32, (QB, QB), 0)
    for p in range(pairs):
        both = jnp.where(row < HD, dq_acc[p, :, :QB], dq_acc[p, :, QB:])
        dq_ref[:, p * QB : (p + 1) * QB] = (both.T * 0.125).astype(BF16)

    @pl.when(block == pl.num_programs(1) - 1)
    def _():
        dk_ref[...] = (dk_acc[...] * 0.125).astype(BF16)
        dv_ref[...] = dv_acc[...].astype(BF16)


def attend_back(starts, counts, q, k, v, ctx, grad, lse, codes, low, high):
    tokens, width = q.shape
    sequences = codes.shape[0]
    length = tokens // sequences
    blocks = length // QB
    pairs = width // QB
    block = pl.BlockSpec((QB, width), lambda s, i, *rest: (s * blocks + i, 0))
    rank3 = lambda s, i, *rest: (s * blocks + i, 0, 0)
    whole_sequence = pl.BlockSpec((length, width), lambda s, i, *rest: (s, 0))
    return pl.pallas_call(
        attend_back_kernel,
        grid_spec=pltpu.PrefetchScalarGridSpec(
            num_scalar_prefetch=2,
            grid=(sequences, blocks),
            in_specs=[
                block,
                whole_sequence,
                whole_sequence,
                block,
                block,
                pl.BlockSpec((1, 8, 2 * QB), rank3),
                pl.BlockSpec((None, length, QB), lambda s, i, *rest: (s, 0, 0)),
                pl.BlockSpec((1, 1, QB), rank3),
                pl.BlockSpec((1, 1, QB), rank3),
            ],
            out_specs=[block, whole_sequence, whole_sequence],
            scratch_shapes=[
                pltpu.VMEM((pairs, QB, 2 * QB), F32),
                pltpu.VMEM((length, width), F32),
                pltpu.VMEM((length, width), F32),
            ],
        ),
        out_shape=[sds((tokens, width), BF16)] * 3,
        compiler_params=params(40),
        cost_estimate=cost(24e9, 14e6),
        name="attend_backward",
    )(starts, counts, q, k, v, ctx, grad, lse, codes, low, high)


def gelu_parts(z):
    spread = jnp.exp2(z * z * (-0.5 * LOG2E))
    t = 1.0 / (1.0 + (0.3275911 * 0.7071067811865476) * jnp.abs(z))
    poly = t * (0.254829592 + t * (-0.284496736 + t * (1.421413741 + t * (-1.453152027 + t * 1.061405429))))
    tail = 0.5 * poly * spread
    return jnp.where(z >= 0, 1.0 - tail, tail), spread


def mlp_kernel(
    x_ref, part_a_ref, part_b_ref, b_out_ref, gain_ref, bias_ref, cot_ref,
    up_a_ref, up_b_ref, down_a_ref, down_b_ref, bup_a_ref, bup_b_ref,
    residual_ref, mlp_ref, n2g_ref, dup_ref, ddown_ref, dbup_ref, dgain_ref, dbias_ref, dbdown_ref,
):
    first = pl.program_id(0) == 0
    residual = (
        x_ref[...].astype(F32)
        + (part_a_ref[...].astype(F32) + part_b_ref[...].astype(F32))
        + b_out_ref[...]
    )
    residual_ref[...] = residual
    unit, _ = norm_stats(residual)
    normed = (unit * gain_ref[...] + bias_ref[...]).astype(BF16)
    cot = cot_ref[...]
    mlp_out, n2_grad = None, None
    for own, up_ref, down_ref, bup_ref in (
        (True, up_a_ref, down_a_ref, bup_a_ref),
        (False, up_b_ref, down_b_ref, bup_b_ref),
    ):
        z = mm(normed, up_ref[...], NN) + bup_ref[...]
        hidden_grad = mm(cot, down_ref[...], NT)
        phi, spread = gelu_parts(z)
        hidden = (z * phi).astype(BF16)
        slope = phi + z * spread * 0.3989422804014327
        grad = hidden_grad * slope
        up_grad = grad.astype(BF16)
        here = mm(hidden, down_ref[...], NN)
        mlp_out = here if mlp_out is None else mlp_out + here
        here = mm(up_grad, up_ref[...], NT)
        n2_grad = here if n2_grad is None else n2_grad + here
        if own:
            add_rows(dbup_ref, grad, first)
            add_to(dup_ref, mm(normed, up_grad, TN), first)
            add_to(ddown_ref, mm(cot, hidden, TN), first)
    mlp_ref[...] = mlp_out.astype(BF16)
    n2g_ref[...] = n2_grad.astype(BF16)
    add_rows(dgain_ref, n2_grad * unit, first)
    add_rows(dbias_ref, n2_grad, first)
    add_rows(dbdown_ref, cot.astype(F32), first)


def mlp(x, part_a, part_b, b_out, gain, bias, cot, up_a, up_b, down_a, down_b, bup_a, bup_b):
    tokens, d = x.shape
    f = up_a.shape[1]
    tile = min(256, tokens)
    tall = rows(tile, d)
    flat = whole((1, d))
    flat_f = whole((1, f))
    return pl.pallas_call(
        mlp_kernel,
        grid=(tokens // tile,),
        in_specs=[tall, tall, tall, flat, flat, flat, tall]
        + [whole((d, f))] * 2
        + [whole((f, d))] * 2
        + [flat_f] * 2,
        out_specs=[tall, tall, tall, whole((d, f)), whole((d, f)), flat_f, flat, flat, flat],
        out_shape=[
            sds((tokens, d), F32),
            sds((tokens, d), BF16),
            sds((tokens, d), BF16),
            sds((d, f), F32),
            sds((d, f), F32),
            sds((1, f), F32),
            sds((1, d), F32),
            sds((1, d), F32),
            sds((1, d), F32),
        ],
        compiler_params=params(56),
        cost_estimate=cost(20 * tokens * d * f, tokens * d * 16 + 16 * d * f, 4 * tokens * f),
        name="feed_forward",
    )(x, part_a, part_b, b_out, gain, bias, cot, up_a, up_b, down_a, down_b, bup_a, bup_b)


def middle_kernel(
    residual_ref, grad_a_ref, grad_b_ref, mlp_a_ref, mlp_b_ref, cot_ref, gain_ref, b_down_ref, ctx_ref, w_ref,
    out_ref, rgrad_ref, cgrad_ref, dw_ref, dbout_ref,
):
    first = pl.program_id(0) == 0
    residual = residual_ref[...]
    unit, scale = norm_stats(residual)
    upstream = (grad_a_ref[...].astype(F32) + grad_b_ref[...].astype(F32)) * gain_ref[...]
    rgrad = cot_ref[...].astype(F32) + norm_back(unit, scale, upstream)
    rgrad_ref[...] = rgrad
    agrad = rgrad.astype(BF16)
    cgrad_ref[...] = mm(agrad, w_ref[...], NT).astype(BF16)
    own = dw_ref.shape[1]
    add_to(dw_ref, mm(agrad, ctx_ref[:, :own], TN), first)
    add_rows(dbout_ref, rgrad, first)
    out_ref[...] = (
        residual + ((mlp_a_ref[...].astype(F32) + mlp_b_ref[...].astype(F32)) + b_down_ref[...])
    ).astype(BF16)


def middle(residual, grad_a, grad_b, mlp_a, mlp_b, cot, gain, b_down, ctx, w_out):
    tokens, d = residual.shape
    width = w_out.shape[0]
    own = width // 2
    tile = min(512, tokens)
    tall, flat = rows(tile, d), whole((1, d))
    return pl.pallas_call(
        middle_kernel,
        grid=(tokens // tile,),
        in_specs=[tall] * 6 + [flat] * 2 + [rows(tile, width), whole(w_out.shape)],
        out_specs=[tall, tall, rows(tile, width), whole((d, own)), flat],
        out_shape=[
            sds((tokens, d), BF16),
            sds((tokens, d), F32),
            sds((tokens, width), BF16),
            sds((d, own), F32),
            sds((1, d), F32),
        ],
        compiler_params=params(48),
        cost_estimate=cost(3 * tokens * d * width, tokens * d * 20),
        name="second_norm_back",
    )(residual, grad_a, grad_b, mlp_a, mlp_b, cot, gain, b_down, ctx, w_out)


def project_back_kernel(
    x_ref, n1_ref, dq_ref, dk_ref, dv_ref, wt_ref,
    n1g_ref, dwq_ref, dwk_ref, dwv_ref, dbq_ref, dbv_ref, dgain_ref, dbias_ref,
):
    first = pl.program_id(0) == 0
    width = dq_ref.shape[1]
    own = dwq_ref.shape[1]
    total = None
    for place, grad_ref in enumerate((dq_ref, dk_ref, dv_ref)):
        here = mm(grad_ref[...], wt_ref[place * width : (place + 1) * width, :], NN)
        total = here if total is None else total + here
    n1g_ref[...] = total.astype(BF16)
    unit, _ = norm_stats(x_ref[...].astype(F32))
    add_rows(dgain_ref, total * unit, first)
    add_rows(dbias_ref, total, first)
    normed = n1_ref[...]
    for grad_ref, out in ((dq_ref, dwq_ref), (dk_ref, dwk_ref), (dv_ref, dwv_ref)):
        add_to(out, mm(normed, grad_ref[:, :own], TN), first)
    add_rows(dbq_ref, dq_ref[:, :own].astype(F32), first)
    add_rows(dbv_ref, dv_ref[:, :own].astype(F32), first)


def project_back(x, n1, dq, dk, dv, wt):
    tokens, d = x.shape
    width = dq.shape[1]
    own = width // 2
    tile = min(512, tokens)
    tall, flat = rows(tile, d), whole((1, d))
    return pl.pallas_call(
        project_back_kernel,
        grid=(tokens // tile,),
        in_specs=[tall] * 2 + [rows(tile, width)] * 3 + [whole(wt.shape)],
        out_specs=[tall] + [whole((d, own))] * 3 + [whole((1, own))] * 2 + [flat] * 2,
        out_shape=[sds((tokens, d), BF16)]
        + [sds((d, own), F32)] * 3
        + [sds((1, own), F32)] * 2
        + [sds((1, d), F32)] * 2,
        compiler_params=params(48),
        cost_estimate=cost(9 * tokens * d * width, tokens * d * 12),
        name="project_back",
    )(x, n1, dq, dk, dv, wt)


def first_back_kernel(x_ref, grad_a_ref, grad_b_ref, rgrad_ref, gain_ref, out_ref):
    unit, scale = norm_stats(x_ref[...].astype(F32))
    upstream = (grad_a_ref[...].astype(F32) + grad_b_ref[...].astype(F32)) * gain_ref[...]
    out_ref[...] = rgrad_ref[...] + norm_back(unit, scale, upstream)


def first_back(x, grad_a, grad_b, rgrad, gain):
    tokens, d = x.shape
    tile = min(512, tokens)
    tall = rows(tile, d)
    return pl.pallas_call(
        first_back_kernel,
        grid=(tokens // tile,),
        in_specs=[tall] * 4 + [whole((1, d))],
        out_specs=tall,
        out_shape=sds((tokens, d), F32),
        compiler_params=params(32),
        cost_estimate=cost(0, tokens * d * 14),
        name="first_norm_back",
    )(x, grad_a, grad_b, rgrad, gain)


def swap(value, axis, size, bit):
    return lax.ppermute(value, axis, [(i, i ^ bit) for i in range(size)])


def scatter_sum(chunks, size, bits, dtype):
    me = lax.axis_index("dp")
    levels = size.bit_length() - 1
    value = chunks.reshape((2,) * levels + chunks.shape[1:])
    left = list(range(levels))
    for bit in bits:
        axis = left.index(levels - 1 - bit)
        mine = (me >> bit) & 1
        keep = lax.dynamic_index_in_dim(value, mine, axis, keepdims=False)
        give = lax.dynamic_index_in_dim(value, 1 - mine, axis, keepdims=False)
        got = swap(give.astype(dtype), "dp", size, 1 << bit)
        value = keep.astype(F32) + got.astype(F32)
        left.pop(axis)
    return value


def body(
    n_dp,
    n_mp,
    block_input,
    segment_ids,
    group_ids,
    padding,
    ln1_gain,
    ln1_bias,
    w_qkv,
    b_qv,
    w_out,
    b_out,
    ln2_gain,
    ln2_bias,
    w_up,
    b_up,
    w_down,
    b_down,
    cotangent,
):
    sequences, length = segment_ids.shape
    tokens, d = block_input.shape
    own = w_qkv.shape[2]
    f = w_up.shape[1]
    blocks = length // QB
    far = lambda value: swap(value, "mp", n_mp, 2)
    near = lambda value: swap(value, "mp", n_mp, 1)
    row = lambda value: value.reshape(1, -1)

    wt_own = jnp.transpose(w_qkv, (1, 2, 0))
    wt_other = far(wt_own.reshape(3 * own, d)).reshape(3, own, d)
    wt = jnp.concatenate([wt_own, wt_other], 1).reshape(6 * own, d)
    w_out_all = jnp.concatenate([w_out, far(w_out)], 0)
    small = far(jnp.concatenate([b_qv.reshape(-1), b_up]))
    b_q = jnp.concatenate([b_qv[0], small[:own]])
    b_v = jnp.concatenate([b_qv[1], small[own : 2 * own]])
    b_up_other = small[2 * own :]
    qkv_bias = jnp.concatenate([b_q, jnp.zeros_like(b_q), b_v])
    w_up_other = far(w_up)
    w_down_other = far(w_down)

    codes = jnp.where(padding == 0, segment_ids * 4 + group_ids, -1)
    low = segment_ids * 4
    high = low + group_ids
    earliest = segment_ids[:, ::QB, None]
    latest = segment_ids[:, QB - 1 :: QB, None]
    key_from = jnp.sum(segment_ids[:, None, :] < earliest, -1, dtype=jnp.int32) // 16 * 16
    key_to = jnp.sum(segment_ids[:, None, :] <= latest, -1, dtype=jnp.int32)
    counts = (key_to - key_from + QB - 1) // QB
    starts = jnp.minimum(key_from, length - counts * QB)
    starts, counts = starts.reshape(-1), counts.reshape(-1)
    code_cols = jnp.broadcast_to(codes[:, :, None], (sequences, length, QB))
    low = low.reshape(sequences * blocks, 1, QB)
    high = high.reshape(sequences * blocks, 1, QB)

    n1, q, k, v = project(block_input, row(ln1_gain), row(ln1_bias), wt, row(qkv_bias))
    ctx, part, lse = attend(starts, counts, q, k, v, code_cols, low, high, w_out_all)
    part_near = near(part)
    residual, mlp_a, n2g, dw_up, dw_down, db_up, dgain2, dbias2, db_down = mlp(
        block_input, part, part_near, row(b_out), row(ln2_gain), row(ln2_bias), cotangent,
        w_up, w_up_other, w_down, w_down_other, row(b_up), row(b_up_other),
    )
    n2g_near = near(n2g)
    mlp_near = near(mlp_a)
    block_output, rgrad, cgrad, dw_out, db_out = middle(
        residual, n2g, n2g_near, mlp_a, mlp_near, cotangent, row(ln2_gain), row(b_down), ctx, w_out_all
    )
    bits = list(range(n_dp.bit_length() - 1))
    piece = d // n_dp
    up_sum = scatter_sum(dw_up.reshape(n_dp, piece, f), n_dp, bits, BF16)
    down_sum = scatter_sum(dw_down.reshape(n_dp, piece, f), n_dp, bits[1:] + bits[:1], BF16)
    dq, dk, dv = attend_back(starts, counts, q, k, v, ctx, cgrad, lse, code_cols, low, high)
    n1g, dwq, dwk, dwv, db_q, db_v, dgain1, dbias1 = project_back(block_input, n1, dq, dk, dv, wt)
    n1g_near = near(n1g)
    input_grad = first_back(block_input, n1g, n1g_near, rgrad, row(ln1_gain))

    dw_attn = jnp.concatenate([dwq, dwk, dwv, dw_out], 1).reshape(n_dp, piece, 4 * own)
    attn_sum = scatter_sum(dw_attn, n_dp, bits, BF16)
    by_device = lambda value: value.reshape(n_dp, -1)
    vectors = jnp.concatenate(
        [by_device(value) for value in (dgain1, dbias1, dgain2, dbias2, db_out, db_down, db_up, db_q, db_v)], 1
    )
    vector_sum = scatter_sum(vectors, n_dp, bits, F32)
    norm_sum = vector_sum[: 4 * piece]
    norm_sum = norm_sum + near(norm_sum)
    rest = vector_sum[4 * piece :]
    tiny = own // n_dp
    fp = f // n_dp
    cut = 2 * piece + fp
    return (
        block_output,
        input_grad,
        norm_sum[:piece],
        norm_sum[piece : 2 * piece],
        attn_sum[:, : 3 * own].reshape(piece, 3, own),
        jnp.stack([rest[cut : cut + tiny], rest[cut + tiny : cut + 2 * tiny]]),
        attn_sum[:, 3 * own :].T,
        rest[:piece],
        norm_sum[2 * piece : 3 * piece],
        norm_sum[3 * piece :],
        up_sum,
        rest[2 * piece : cut],
        down_sum.T,
        rest[piece : 2 * piece],
    )


def solution(mesh):
    return jax.shard_map(
        functools.partial(body, mesh.shape["dp"], mesh.shape["mp"]),
        mesh=mesh,
        in_specs=(
            P("dp", None),
            P("dp", None),
            P("dp", None),
            P("dp", None),
            P(),
            P(),
            P(None, None, "mp"),
            P(None, "mp"),
            P("mp", None),
            P(),
            P(),
            P(),
            P(None, "mp"),
            P("mp"),
            P("mp", None),
            P(),
            P("dp", None),
        ),
        out_specs=(
            P("dp", None),
            P("dp", None),
            P("dp"),
            P("dp"),
            P("dp", None, "mp"),
            P(None, ("mp", "dp")),
            P("mp", "dp"),
            P("dp"),
            P("dp"),
            P("dp"),
            P("dp", "mp"),
            P(("mp", "dp")),
            P("mp", "dp"),
            P("dp"),
        ),
        check_vma=False,
    )
```

```python
import functools

import jax
import jax.numpy as jnp
from jax import lax
from jax.experimental import pallas as pl
from jax.experimental.pallas import tpu as pltpu
from jax.sharding import PartitionSpec as P

HD = 64
QB = 128
GRAIN = 64
LONGEST = 256
MASKED = -1e30
EPS = 1e-05
LOG2E = 1.4426950408889634
F32 = jnp.float32
BF16 = jnp.bfloat16
NT = (((1,), (1,)), ((), ()))
NN = (((1,), (0,)), ((), ()))
TN = (((0,), (0,)), ((), ()))


def mm(a, b, dims):
    return lax.dot_general(a, b, dims, preferred_element_type=F32)


def params(mib):
    return pltpu.CompilerParams(vmem_limit_bytes=mib * 1024 * 1024)


def cost(flops, traffic, trans=0):
    return pl.CostEstimate(flops=int(flops), bytes_accessed=int(traffic), transcendentals=int(trans))


def whole(shape):
    return pl.BlockSpec(shape, lambda *ids: (0,) * len(shape))


def rows(tile, width):
    return pl.BlockSpec((tile, width), lambda i, *rest: (i, 0))


def sds(shape, dtype):
    return jax.ShapeDtypeStruct(shape, dtype)


def norm_stats(values):
    average = jnp.mean(values, -1, keepdims=True)
    centered = values - average
    variance = jnp.mean(centered * centered, -1, keepdims=True)
    scale = lax.rsqrt(variance + EPS)
    return centered * scale, scale


def norm_back(unit, scale, upstream):
    first = jnp.mean(upstream, -1, keepdims=True)
    second = jnp.mean(upstream * unit, -1, keepdims=True)
    return scale * (upstream - first - unit * second)


def zero_first(first, *refs):
    @pl.when(first)
    def _():
        for ref in refs:
            ref[...] = jnp.zeros_like(ref)


def add_rows(ref, values):
    ref[...] += jnp.sum(values, 0, keepdims=True)


def project_kernel(x_ref, gain_ref, bias_ref, wt_ref, q_bias_ref, v_bias_ref, n1_ref, q_ref, k_ref, v_ref):
    unit, _ = norm_stats(x_ref[...].astype(F32))
    normed = (unit * gain_ref[...] + bias_ref[...]).astype(BF16)
    n1_ref[...] = normed
    own = q_ref.shape[1]
    q_ref[...] = (mm(normed, wt_ref[:own, :], NT) + q_bias_ref[...]).astype(BF16)
    k_ref[...] = mm(normed, wt_ref[own : 2 * own, :], NT).astype(BF16)
    v_ref[...] = (mm(normed, wt_ref[2 * own :, :], NT) + v_bias_ref[...]).astype(BF16)


def project(x, gain, bias, wt, q_bias, v_bias):
    tokens, d = x.shape
    own = wt.shape[0] // 3
    tile = min(1024, tokens)
    return pl.pallas_call(
        project_kernel,
        grid=(tokens // tile,),
        in_specs=[rows(tile, d), whole((1, d)), whole((1, d)), whole(wt.shape)] + [whole((1, own))] * 2,
        out_specs=[rows(tile, d)] + [rows(tile, own)] * 3,
        out_shape=[sds((tokens, d), BF16)] + [sds((tokens, own), BF16)] * 3,
        compiler_params=params(40),
        cost_estimate=cost(6 * tokens * d * own, tokens * (4 * d + 6 * own) + 6 * d * own),
        name="norm_project",
    )(x, gain, bias, wt, q_bias, v_bias)


def place_halves(half_ref, part_a_ref, part_b_ref, full_ref):
    size = part_a_ref.shape[0]
    at = pl.multiple_of(half_ref[0] * size, 16)
    full_ref[pl.ds(at, size), :] = part_a_ref[...]
    full_ref[pl.ds(pl.multiple_of(size - at, 16), size), :] = part_b_ref[...]


def project_far_kernel(
    half_ref, n1_ref, wa_ref, wb_ref, q_bias_ref, v_bias_ref, q_ref, k_ref, v_ref, wt_ref
):
    @pl.when(pl.program_id(0) == 0)
    def _():
        place_halves(half_ref, wa_ref, wb_ref, wt_ref)

    normed = n1_ref[...]
    own = q_ref.shape[1]
    q_ref[...] = (mm(normed, wt_ref[:own, :], NT) + q_bias_ref[...]).astype(BF16)
    k_ref[...] = mm(normed, wt_ref[own : 2 * own, :], NT).astype(BF16)
    v_ref[...] = (mm(normed, wt_ref[2 * own :, :], NT) + v_bias_ref[...]).astype(BF16)


def project_far(half, n1, wa, wb, q_bias, v_bias):
    tokens, d = n1.shape
    own = 2 * wa.shape[0] // 3
    tile = min(1024, tokens)
    return pl.pallas_call(
        project_far_kernel,
        grid_spec=pltpu.PrefetchScalarGridSpec(
            num_scalar_prefetch=1,
            grid=(tokens // tile,),
            in_specs=[rows(tile, d), whole(wa.shape), whole(wa.shape)] + [whole((1, own))] * 2,
            out_specs=[rows(tile, own)] * 3 + [whole((3 * own, d))],
        ),
        out_shape=[sds((tokens, own), BF16)] * 3 + [sds((3 * own, d), BF16)],
        compiler_params=params(40),
        cost_estimate=cost(6 * tokens * d * own, tokens * (2 * d + 6 * own) + 6 * d * own),
        name="project_far",
    )(half, n1, wa, wb, q_bias, v_bias)


def tables(segment_ids, group_ids, padding):
    sequences, length = segment_ids.shape
    earliest = segment_ids[:, ::QB, None]
    latest = segment_ids[:, QB - 1 :: QB, None]
    key_from = jnp.sum(segment_ids[:, None, :] < earliest, -1, dtype=jnp.int32) // 16 * 16
    key_to = jnp.sum(segment_ids[:, None, :] <= latest, -1, dtype=jnp.int32)
    grains = jnp.maximum((key_to - key_from + GRAIN - 1) // GRAIN, QB // GRAIN)
    starts = jnp.minimum(key_from, length - grains * GRAIN)
    low = segment_ids * 4
    high = low + group_ids
    codes = jnp.stack([jnp.where(padding == 0, high, -1), low, high], 1)
    return starts.reshape(-1), grains.reshape(-1), codes


def extents(length):
    return range(QB // GRAIN, min(QB + 2 * LONGEST, length) // GRAIN + 1)


def head_groups(width):
    return [slice(at, min(at + 2 * HD, width)) for at in range(0, width, 2 * HD)]


def stack_heads(values):
    if values.shape[1] == HD:
        return values
    lane = lax.broadcasted_iota(jnp.int32, values.shape, 1)
    zero = jnp.zeros_like(values)
    return jnp.concatenate(
        [jnp.where(lane < HD, values, zero), jnp.where(lane >= HD, values, zero)], 0
    )


def join_heads(values):
    if values.shape[1] == HD:
        return values
    lane = lax.broadcasted_iota(jnp.int32, (QB, 2 * HD), 1)
    return jnp.where(lane < HD, values[:QB], values[QB:])


def spread_codes(code_ref, column_ref):
    for at in range(0, column_ref.shape[0], QB):
        column_ref[at : at + QB, :] = jnp.broadcast_to(code_ref[0:1, at : at + QB], (QB, QB)).T


def mask_bias(column_ref, code_ref, start, extent, block):
    mine = pl.ds(pl.multiple_of(block * QB, QB), QB)
    codes = column_ref[pl.ds(start, extent), :]
    shape = (extent, QB)
    apart = lax.broadcasted_iota(jnp.int32, shape, 0) - lax.broadcasted_iota(jnp.int32, shape, 1)
    allowed = ((codes >= code_ref[1:2, mine]) & (codes <= code_ref[2:3, mine])) | (
        apart == block * QB - start
    )
    return jnp.where(allowed, jnp.float32(0), jnp.float32(MASKED))


def widen(bias, cols):
    return jnp.concatenate([bias, bias], 1) if cols.stop - cols.start > HD else bias


def each_block(start_ref, grain_ref, length, group, run):
    turns = length // QB // group
    sequence = pl.program_id(0)

    def step(turn, carry):
        place = (sequence * turns + turn) * group
        grains = functools.reduce(jnp.maximum, [grain_ref[place + i] for i in range(group)])
        starts = [
            pl.multiple_of(jnp.minimum(start_ref[place + i], length - grains * GRAIN), 16) for i in range(group)
        ]
        blocks = [turn * group + i for i in range(group)]
        for extent in extents(length):
            pl.when(grains == extent)(functools.partial(run, extent * GRAIN, blocks, starts))
        return carry

    lax.fori_loop(0, turns, step, 0)


def attend_kernel(
    far, start_ref, grain_ref, q_ref, k_ref, v_ref, code_ref, *rest
):
    if far:
        own_ctx_ref, own_w_ref, far_w_ref, ctx_ref, part_ref, lse_ref, column_ref = rest
    else:
        ctx_ref, lse_ref, column_ref = rest
    length, width = q_ref.shape
    heads = head_groups(width)
    spread_codes(code_ref, column_ref)

    def run(extent, blocks, starts):
        units, scores, probs, totals, biases = [], [], [], [], []
        for i, (block, start) in enumerate(zip(blocks, starts)):
            here = pl.ds(start, extent)
            mine = pl.ds(pl.multiple_of(block * QB, QB), QB)
            for p, cols in enumerate(heads):
                units.append((i, block, here, mine, p, cols))
                scores.append(mm(k_ref[here, cols], stack_heads(q_ref[mine, cols]), NT))
            biases.append(mask_bias(column_ref, code_ref, start, extent, block))
        for (i, block, here, mine, p, cols), score in zip(units, scores):
            score = score * (0.125 * LOG2E) + widen(biases[i], cols)
            top = jnp.max(score, 0, keepdims=True)
            weights = jnp.exp2(score - top)
            total = jnp.sum(weights, 0, keepdims=True)
            lse_ref[block, p : p + 1, : score.shape[1]] = top + jnp.log2(total)
            totals.append(1.0 / total)
            probs.append(weights.astype(BF16))
        for (i, block, here, mine, p, cols), prob, total in zip(units, probs, totals):
            turned = v_ref[here, cols].T
            both = [
                mm(turned[at * HD : (at + 1) * HD], prob[:, at * QB : (at + 1) * QB], NN)
                * total[:, at * QB : (at + 1) * QB]
                for at in range(prob.shape[1] // QB)
            ]
            ctx_ref[mine, cols] = jnp.concatenate(both, 0).T.astype(BF16)

    each_block(start_ref, grain_ref, length, 2, run)
    if far:
        part_ref[...] = (
            mm(own_ctx_ref[...], own_w_ref[...], NN) + mm(ctx_ref[...], far_w_ref[...], NN)
        ).astype(BF16)


def attend(q, k, v, table, rest=()):
    starts, grains, codes = table
    tokens, width = q.shape
    sequences, _, length = codes.shape
    blocks = length // QB
    tall = lambda columns: pl.BlockSpec((length, columns), lambda s, *rest: (s, 0))
    groups = len(head_groups(width))
    lse_shape = (blocks, 8, 2 * QB)
    share_specs, share_shapes = [], []
    if rest:
        d = rest[1].shape[1]
        share_specs, share_shapes = [tall(d)], [sds((tokens, d), BF16)]
    return pl.pallas_call(
        functools.partial(attend_kernel, bool(rest)),
        grid_spec=pltpu.PrefetchScalarGridSpec(
            num_scalar_prefetch=2,
            grid=(sequences,),
            in_specs=[tall(width)] * 3
            + [pl.BlockSpec((None, 3, length), lambda s, *rest: (s, 0, 0))]
            + ([tall(width), whole(rest[1].shape), whole(rest[2].shape)] if rest else []),
            out_specs=[tall(width)]
            + share_specs
            + [pl.BlockSpec(lse_shape, lambda s, *rest: (s, 0, 0))],
            scratch_shapes=[pltpu.VMEM((length, QB), jnp.int32)],
        ),
        out_shape=[sds((tokens, width), BF16)]
        + share_shapes
        + [sds((sequences * blocks,) + lse_shape[1:], F32)],
        compiler_params=params(32),
        cost_estimate=cost(6e9 if rest else 4e9, 10e6),
        name="attend_far" if rest else "attend_own",
    )(starts, grains, q, k, v, codes, *rest)


def attend_back_kernel(
    start_ref, grain_ref, q_ref, k_ref, v_ref, ctx_ref, grad_ref, lse_ref, code_ref,
    dq_ref, dk_ref, dv_ref, dk_acc, dv_acc, column_ref,
):
    length, width = q_ref.shape
    heads = head_groups(width)
    spread_codes(code_ref, column_ref)
    dk_acc[...] = jnp.zeros_like(dk_acc)
    dv_acc[...] = jnp.zeros_like(dv_acc)

    def run(extent, blocks, starts):
        units, stacked, upstream, scores, grads, biases = [], [], [], [], [], []
        for i, (block, start) in enumerate(zip(blocks, starts)):
            here = pl.ds(start, extent)
            mine = pl.ds(pl.multiple_of(block * QB, QB), QB)
            for p, cols in enumerate(heads):
                units.append((i, block, here, mine, p, cols))
                stacked.append(stack_heads(q_ref[mine, cols]))
                upstream.append(stack_heads(grad_ref[mine, cols]))
                scores.append(mm(k_ref[here, cols], stacked[-1], NT))
                grads.append(mm(v_ref[here, cols], upstream[-1], NT))
            biases.append(mask_bias(column_ref, code_ref, start, extent, block))
        probs, score_grads = [], []
        for (i, block, here, mine, p, cols), score, grad in zip(units, scores, grads):
            turned = (ctx_ref[mine, cols].astype(F32) * grad_ref[mine, cols].astype(F32)).T
            delta = jnp.concatenate(
                [
                    jnp.sum(turned[at : at + HD], 0, keepdims=True)
                    for at in range(0, turned.shape[0], HD)
                ],
                1,
            )
            weights = jnp.exp2(
                score * (0.125 * LOG2E) + widen(biases[i], cols) - lse_ref[block, p : p + 1, : score.shape[1]]
            )
            probs.append(weights.astype(BF16))
            score_grads.append((weights * (grad - delta)).astype(BF16))
        for n, (i, block, here, mine, p, cols) in enumerate(units):
            dv_acc[here, cols] += mm(probs[n], upstream[n], NN)
            dk_acc[here, cols] += mm(score_grads[n], stacked[n], NN)
            dq = join_heads(mm(score_grads[n], k_ref[here, cols], TN))
            dq_ref[mine, cols] = (dq * 0.125).astype(BF16)

    each_block(start_ref, grain_ref, length, 1, run)
    dk_ref[...] = (dk_acc[...] * 0.125).astype(BF16)
    dv_ref[...] = dv_acc[...].astype(BF16)


def attend_back(q, k, v, ctx, grad, lse, table):
    starts, grains, codes = table
    tokens, width = q.shape
    sequences, _, length = codes.shape
    blocks = length // QB
    tall = pl.BlockSpec((length, width), lambda s, *rest: (s, 0))
    return pl.pallas_call(
        attend_back_kernel,
        grid_spec=pltpu.PrefetchScalarGridSpec(
            num_scalar_prefetch=2,
            grid=(sequences,),
            in_specs=[tall] * 5
            + [
                pl.BlockSpec((blocks, 8, 2 * QB), lambda s, *rest: (s, 0, 0)),
                pl.BlockSpec((None, 3, length), lambda s, *rest: (s, 0, 0)),
            ],
            out_specs=[tall] * 3,
            scratch_shapes=[
                pltpu.VMEM((length, width), F32),
                pltpu.VMEM((length, width), F32),
                pltpu.VMEM((length, QB), jnp.int32),
            ],
        ),
        out_shape=[sds((tokens, width), BF16)] * 3,
        compiler_params=params(32),
        cost_estimate=cost(8e9, 14e6),
        name="attend_backward",
    )(starts, grains, q, k, v, ctx, grad, lse, codes)


def gelu_parts(z):
    spread = jnp.exp2(z * z * (-0.5 * LOG2E))
    t = 1.0 / (1.0 + (0.3275911 * 0.7071067811865476) * jnp.abs(z))
    poly = t * (0.254829592 + t * (-0.284496736 + t * (1.421413741 + t * (-1.453152027 + t * 1.061405429))))
    tail = 0.5 * poly * spread
    return jnp.where(z >= 0, 1.0 - tail, tail), spread


def down_back_kernel(cot_ref, down_ref, out_ref):
    out_ref[...] = mm(cot_ref[...], down_ref[...], NT).astype(BF16)


def down_back(cot, down):
    tokens, d = cot.shape
    f = down.shape[0]
    tile = min(1024, tokens)
    return pl.pallas_call(
        down_back_kernel,
        grid=(tokens // tile,),
        in_specs=[rows(tile, d), whole(down.shape)],
        out_specs=rows(tile, f),
        out_shape=sds((tokens, f), BF16),
        compiler_params=params(32),
        cost_estimate=cost(2 * tokens * d * f, tokens * d * 2 + tokens * f * 2 + 2 * d * f),
        name="feed_forward_upstream",
    )(cot, down)


def hidden_pair(normed, hidden_grad, up, bias):
    z = mm(normed, up, NN) + bias
    phi, spread = gelu_parts(z)
    hidden = (z * phi).astype(BF16)
    grad = hidden_grad * (phi + z * spread * 0.3989422804014327)
    return hidden, grad


def mlp_own_kernel(
    x_ref, part_a_ref, part_b_ref, b_out_ref, gain_ref, bias_ref, cot_ref, cot_down_ref, up_ref, down_ref, bup_ref,
    residual_ref, n2_ref, hidden_ref, upg_ref, mlp_ref, n2g_ref, dbup_ref, dbdown_ref,
):
    zero_first(pl.program_id(0) == 0, dbup_ref, dbdown_ref)
    residual = (
        x_ref[...].astype(F32)
        + (part_a_ref[...].astype(F32) + part_b_ref[...].astype(F32))
        + b_out_ref[...]
    )
    residual_ref[...] = residual
    unit, _ = norm_stats(residual)
    normed = (unit * gain_ref[...] + bias_ref[...]).astype(BF16)
    n2_ref[...] = normed
    hidden, grad = hidden_pair(normed, cot_down_ref[...].astype(F32), up_ref[...], bup_ref[...])
    hidden_ref[...] = hidden
    up_grad = grad.astype(BF16)
    upg_ref[...] = up_grad
    mlp_ref[...] = mm(hidden, down_ref[...], NN).astype(BF16)
    n2g_ref[...] = mm(up_grad, up_ref[...], NT).astype(BF16)
    add_rows(dbup_ref, grad)
    add_rows(dbdown_ref, cot_ref[...].astype(F32))


def mlp_own(x, part_a, part_b, b_out, gain, bias, cot, cot_down, up, down, bup):
    tokens, d = x.shape
    f = up.shape[1]
    tile = min(512, tokens)
    tall, wide = rows(tile, d), rows(tile, f)
    flat, flat_f = whole((1, d)), whole((1, f))
    return pl.pallas_call(
        mlp_own_kernel,
        grid=(tokens // tile,),
        in_specs=[tall, tall, tall, flat, flat, flat, tall, wide, whole((d, f)), whole((f, d)), flat_f],
        out_specs=[tall, tall, wide, wide, tall, tall, flat_f, flat],
        out_shape=[
            sds((tokens, d), F32),
            sds((tokens, d), BF16),
            sds((tokens, f), BF16),
            sds((tokens, f), BF16),
            sds((tokens, d), BF16),
            sds((tokens, d), BF16),
            sds((1, f), F32),
            sds((1, d), F32),
        ],
        compiler_params=params(48),
        cost_estimate=cost(8 * tokens * d * f, tokens * d * 22 + 4 * d * f, 4 * tokens * f),
        name="feed_forward_own",
    )(x, part_a, part_b, b_out, gain, bias, cot, cot_down, up, down, bup)


def mlp_far_kernel(
    half_ref, n2_ref, cot_ref, mlp_own_ref, n2g_own_ref, up_a_ref, up_b_ref, down_a_ref, down_b_ref, bup_ref,
    mlp_ref, n2g_ref, up_ref, down_ref,
):
    @pl.when(pl.program_id(0) == 0)
    def _():
        place_halves(half_ref, up_a_ref, up_b_ref, up_ref)
        place_halves(half_ref, down_a_ref, down_b_ref, down_ref)

    hidden_grad = mm(cot_ref[...], down_ref[...], NT)
    hidden, grad = hidden_pair(n2_ref[...], hidden_grad, up_ref[...], bup_ref[...])
    mlp_ref[...] = (mlp_own_ref[...].astype(F32) + mm(hidden, down_ref[...], NN)).astype(BF16)
    n2g_ref[...] = (n2g_own_ref[...].astype(F32) + mm(grad.astype(BF16), up_ref[...], NT)).astype(BF16)


def mlp_far(half, n2, cot, mlp_share, n2g_share, up_a, up_b, down_a, down_b, bup):
    tokens, d = n2.shape
    f = bup.shape[1]
    tile = min(512, tokens)
    tall = rows(tile, d)
    return pl.pallas_call(
        mlp_far_kernel,
        grid_spec=pltpu.PrefetchScalarGridSpec(
            num_scalar_prefetch=1,
            grid=(tokens // tile,),
            in_specs=[tall] * 4
            + [whole(up_a.shape)] * 2
            + [whole(down_a.shape)] * 2
            + [whole((1, f))],
            out_specs=[tall, tall],
            scratch_shapes=[pltpu.VMEM((d, f), BF16), pltpu.VMEM((f, d), BF16)],
        ),
        out_shape=[sds((tokens, d), BF16)] * 2,
        compiler_params=params(48),
        cost_estimate=cost(8 * tokens * d * f, tokens * d * 12 + 4 * d * f, 4 * tokens * f),
        name="feed_forward_far",
    )(half, n2, cot, mlp_share, n2g_share, up_a, up_b, down_a, down_b, bup)


def two_products_kernel(a_ref, b_ref, c_ref, e_ref, one_ref, two_ref):
    one_ref[...] = mm(a_ref[...], b_ref[...], TN).astype(one_ref.dtype)
    two_ref[...] = mm(c_ref[...], e_ref[...], TN).astype(two_ref.dtype)


def two_products(a, b, c, e):
    tokens, d = a.shape
    f = b.shape[1]
    tile = d // 2 if d % 256 == 0 else d
    side = lambda columns: pl.BlockSpec((tokens, columns), lambda i: (0, i))
    return pl.pallas_call(
        two_products_kernel,
        grid=(d // tile,),
        in_specs=[side(tile), whole(b.shape), side(tile), whole(e.shape)],
        out_specs=[rows(tile, f)] * 2,
        out_shape=[sds((d, f), BF16)] * 2,
        compiler_params=params(48),
        cost_estimate=cost(4 * tokens * d * f, 8 * tokens * d + 4 * d * f),
        name="feed_forward_weights",
    )(a, b, c, e)


def middle_kernel(
    residual_ref, grad_a_ref, grad_b_ref, cot_ref, gain_ref, own_w_ref, far_w_ref,
    agrad_ref, own_cg_ref, far_cg_ref, dbout_ref, dgain_ref, dbias_ref,
):
    zero_first(pl.program_id(0) == 0, dbout_ref, dgain_ref, dbias_ref)
    unit, scale = norm_stats(residual_ref[...])
    summed = grad_a_ref[...].astype(F32) + grad_b_ref[...].astype(F32)
    add_rows(dgain_ref, summed * unit)
    add_rows(dbias_ref, summed)
    rgrad = cot_ref[...].astype(F32) + norm_back(unit, scale, summed * gain_ref[...])
    add_rows(dbout_ref, rgrad)
    agrad = rgrad.astype(BF16)
    agrad_ref[...] = agrad
    own_cg_ref[...] = mm(agrad, own_w_ref[...], NT).astype(BF16)
    far_cg_ref[...] = mm(agrad, far_w_ref[...], NT).astype(BF16)


def middle(residual, grad_a, grad_b, cot, gain, own_w, far_w):
    tokens, d = residual.shape
    own = own_w.shape[0]
    tile = min(512, tokens)
    tall, flat = rows(tile, d), whole((1, d))
    return pl.pallas_call(
        middle_kernel,
        grid=(tokens // tile,),
        in_specs=[tall] * 4 + [flat] + [whole(own_w.shape)] * 2,
        out_specs=[tall] + [rows(tile, own)] * 2 + [flat] * 3,
        out_shape=[sds((tokens, d), BF16)] + [sds((tokens, own), BF16)] * 2 + [sds((1, d), F32)] * 3,
        compiler_params=params(40),
        cost_estimate=cost(4 * tokens * d * own, tokens * d * 14),
        name="second_norm_back",
    )(residual, grad_a, grad_b, cot, gain, own_w, far_w)


def output_kernel(residual_ref, mlp_a_ref, mlp_b_ref, b_down_ref, out_ref):
    out_ref[...] = (
        residual_ref[...]
        + ((mlp_a_ref[...].astype(F32) + mlp_b_ref[...].astype(F32)) + b_down_ref[...])
    ).astype(BF16)


def output(residual, mlp_a, mlp_b, b_down):
    tokens, d = residual.shape
    tile = min(512, tokens)
    tall = rows(tile, d)
    return pl.pallas_call(
        output_kernel,
        grid=(tokens // tile,),
        in_specs=[tall] * 3 + [whole((1, d))],
        out_specs=tall,
        out_shape=sds((tokens, d), BF16),
        compiler_params=params(24),
        cost_estimate=cost(4 * tokens * d, tokens * d * 10),
        name="block_output",
    )(residual, mlp_a, mlp_b, b_down)


def attention_weights_kernel(n1_ref, dq_ref, dk_ref, dv_ref, agrad_ref, ctx_ref, one_ref, two_ref, dbq_ref, dbv_ref):
    own = dq_ref.shape[1]
    normed = n1_ref[...]
    one_ref[:, :own] = mm(normed, dq_ref[...], TN).astype(BF16)
    one_ref[:, own:] = mm(normed, dk_ref[...], TN).astype(BF16)
    two_ref[:, :own] = mm(normed, dv_ref[...], TN).astype(BF16)
    two_ref[:, own:] = mm(agrad_ref[...], ctx_ref[...], TN).astype(BF16)
    dbq_ref[...] = jnp.sum(dq_ref[...].astype(F32), 0, keepdims=True)
    dbv_ref[...] = jnp.sum(dv_ref[...].astype(F32), 0, keepdims=True)


def attention_weights(n1, dq, dk, dv, agrad, ctx):
    tokens, d = n1.shape
    own = dq.shape[1]
    tile = d // 2 if d % 256 == 0 else d
    side = pl.BlockSpec((tokens, tile), lambda i: (0, i))
    return pl.pallas_call(
        attention_weights_kernel,
        grid=(d // tile,),
        in_specs=[side] + [whole(dq.shape)] * 3 + [side, whole(ctx.shape)],
        out_specs=[rows(tile, 2 * own)] * 2 + [whole((1, own))] * 2,
        out_shape=[sds((d, 2 * own), BF16)] * 2 + [sds((1, own), F32)] * 2,
        compiler_params=params(40),
        cost_estimate=cost(8 * tokens * d * own, tokens * d * 8),
        name="attention_weights",
    )(n1, dq, dk, dv, agrad, ctx)


def project_back_kernel(x_ref, aq_ref, ak_ref, av_ref, bq_ref, bk_ref, bv_ref, wa_ref, wb_ref, n1g_ref, dgain_ref, dbias_ref):
    zero_first(pl.program_id(0) == 0, dgain_ref, dbias_ref)
    own = aq_ref.shape[1]
    total = None
    for w_ref, grads in ((wa_ref, (aq_ref, ak_ref, av_ref)), (wb_ref, (bq_ref, bk_ref, bv_ref))):
        for place, grad_ref in enumerate(grads):
            here = mm(grad_ref[...], w_ref[place * own : (place + 1) * own, :], NN)
            total = here if total is None else total + here
    n1g_ref[...] = total.astype(BF16)
    unit, _ = norm_stats(x_ref[...].astype(F32))
    add_rows(dgain_ref, total * unit)
    add_rows(dbias_ref, total)


def project_back(x, own_grads, far_grads, own_wt, far_wt):
    tokens, d = x.shape
    own = own_grads[0].shape[1]
    tile = min(1024, tokens)
    tall, flat = rows(tile, d), whole((1, d))
    return pl.pallas_call(
        project_back_kernel,
        grid=(tokens // tile,),
        in_specs=[tall] + [rows(tile, own)] * 6 + [whole(own_wt.shape)] * 2,
        out_specs=[tall, flat, flat],
        out_shape=[sds((tokens, d), BF16)] + [sds((1, d), F32)] * 2,
        compiler_params=params(40),
        cost_estimate=cost(12 * tokens * d * own, tokens * d * 8),
        name="project_back",
    )(x, *own_grads, *far_grads, own_wt, far_wt)


def first_back_kernel(x_ref, grad_a_ref, grad_b_ref, rgrad_ref, gain_ref, out_ref):
    unit, scale = norm_stats(x_ref[...].astype(F32))
    upstream = (grad_a_ref[...].astype(F32) + grad_b_ref[...].astype(F32)) * gain_ref[...]
    out_ref[...] = rgrad_ref[...].astype(F32) + norm_back(unit, scale, upstream)


def first_back(x, grad_a, grad_b, rgrad, gain):
    tokens, d = x.shape
    tile = min(512, tokens)
    tall = rows(tile, d)
    return pl.pallas_call(
        first_back_kernel,
        grid=(tokens // tile,),
        in_specs=[tall] * 4 + [whole((1, d))],
        out_specs=tall,
        out_shape=sds((tokens, d), F32),
        compiler_params=params(24),
        cost_estimate=cost(20 * tokens * d, tokens * d * 12),
        name="first_norm_back",
    )(x, grad_a, grad_b, rgrad, gain)


def swap(value, axis, size, bit):
    return lax.ppermute(value, axis, [(i, i ^ bit) for i in range(size)])


def tie(value, *others):
    return lax.optimization_barrier((value,) + others)[0]


class ScatterSum:
    def __init__(self, chunks, size, dtype=BF16):
        levels = size.bit_length() - 1
        self.size, self.dtype, self.levels = size, dtype, levels
        self.me = lax.axis_index("dp")
        bits = list(range(levels))
        self.plan = [[0]] + [[bit] for bit in reversed(bits[3:])] + [bits[1:3]]
        self.plan = [stage for stage in self.plan if stage and stage[0] < levels]
        self.left = list(range(levels))
        self.value = chunks.reshape((2,) * levels + chunks.shape[1:])

    def pick(self, bits, flips):
        value = self.value
        left = list(self.left)
        for bit in bits:
            axis = left.index(self.levels - 1 - bit)
            index = ((self.me >> bit) & 1) ^ ((flips >> bit) & 1)
            value = lax.dynamic_index_in_dim(value, index, axis, keepdims=False)
            left.pop(axis)
        return value

    def begin(self, *others):
        bits = self.plan.pop(0)
        self.bits = bits
        moves = [sum(1 << bit for k, bit in enumerate(bits) if (m >> k) & 1) for m in range(1, 1 << len(bits))]
        gives = [self.pick(bits, move).astype(self.dtype) for move in moves]
        if others:
            gives = [tie(give, *others) for give in gives]
        self.got = [swap(give, "dp", self.size, move) for give, move in zip(gives, moves)]
        self.keep = self.pick(bits, 0)

    def end(self):
        total = self.keep.astype(F32)
        for got in self.got:
            total = total + got.astype(F32)
        for bit in self.bits:
            self.left.remove(self.levels - 1 - bit)
        self.value = total
        return self.got

    def finish(self):
        while self.plan:
            self.begin()
            self.end()
        return self.value


def body(
    n_dp,
    n_mp,
    block_input,
    segment_ids,
    group_ids,
    padding,
    ln1_gain,
    ln1_bias,
    w_qkv,
    b_qv,
    w_out,
    b_out,
    ln2_gain,
    ln2_bias,
    w_up,
    b_up,
    w_down,
    b_down,
    cotangent,
):
    tokens, d = block_input.shape
    own = w_qkv.shape[2]
    f = w_up.shape[1]
    far = lambda value: swap(value, "mp", n_mp, 2)
    near = lambda value: swap(value, "mp", n_mp, 1)
    beside = lambda value: swap(value, "dp", n_dp, 1)
    row = lambda value: value.reshape(1, -1)

    half = lax.axis_index("dp") & 1
    cut = lambda value: lax.dynamic_slice_in_dim(value, half * (value.shape[0] // 2), value.shape[0] // 2, 0)
    half_at = half.astype(jnp.int32).reshape(1)
    wt_own = jnp.transpose(w_qkv, (1, 2, 0)).reshape(3 * own, d)
    wt_a = far(cut(wt_own))
    small = far(jnp.concatenate([b_qv.reshape(-1), b_up]))
    table = tables(segment_ids, group_ids, padding)
    n1, *qkv_own = project(block_input, row(ln1_gain), row(ln1_bias), wt_own, b_qv[:1], b_qv[1:])
    w_out_far = far(tie(w_out, n1))
    cot_down = down_back(tie(cotangent, n1), w_down)
    wt_a, cot_down = lax.optimization_barrier((wt_a, cot_down))
    wt_b = beside(wt_a)
    up_a = far(tie(cut(w_up), cot_down))
    down_a = far(tie(cut(w_down), cot_down))
    ctx_own, lse_own = attend(tie(qkv_own[0], wt_a, cot_down), *qkv_own[1:], table)
    *qkv_far, wt_far = project_far(half_at, n1, wt_a, tie(wt_b, ctx_own), row(small[:own]), row(small[own : 2 * own]))
    up_a, q_far = lax.optimization_barrier((up_a, qkv_far[0]))
    up_b = beside(up_a)
    ctx_far, part, lse_far = attend(tie(q_far, up_a), *qkv_far[1:], table, (ctx_own, w_out, w_out_far))
    part_near = near(part)
    down_a, part_near = lax.optimization_barrier((down_a, part_near))
    down_b = beside(down_a)
    residual, n2, hidden, up_grad, mlp_share, n2g_share, db_up, db_down = mlp_own(
        block_input, part, part_near, row(b_out), row(ln2_gain), row(ln2_bias), cotangent, cot_down, w_up, w_down,
        row(b_up),
    )
    mlp_a, n2g_a = mlp_far(
        half_at, n2, cotangent, mlp_share, n2g_share, up_a, tie(up_b, n2), down_a, tie(down_b, n2), row(small[2 * own :])
    )
    n2g_b = near(n2g_a)
    piece = d // n_dp
    scatter = lambda value: ScatterSum(value.reshape(n_dp, piece, value.shape[1]), n_dp)
    dw_up, dw_down = two_products(tie(n2, n2g_a), up_grad, cotangent, hidden)
    sum_up, sum_down = scatter(dw_up), scatter(dw_down)
    sum_up.begin()
    sum_down.begin()
    mlp_b = near(tie(mlp_a, dw_up))
    agrad, cgrad_own, cgrad_far, db_out, dgain2, dbias2 = middle(
        residual, n2g_a, tie(n2g_b, dw_up), cotangent, row(ln2_gain), w_out, w_out_far
    )
    got = sum_up.end()
    sum_up.begin(agrad)
    own_grads = attend_back(*qkv_own, ctx_own, tie(cgrad_own, *got), lse_own, table)
    got = sum_down.end()
    sum_down.begin(own_grads[0])
    dw_qk, dw_vo, db_q, db_v = attention_weights(n1, tie(own_grads[0], *got), *own_grads[1:], agrad, ctx_own)
    sum_qk, sum_vo = scatter(dw_qk), scatter(dw_vo)
    sum_qk.begin()
    sum_vo.begin()
    far_grads = attend_back(*qkv_far, ctx_far, tie(cgrad_far, dw_qk), lse_far, table)
    got = sum_up.end() + sum_qk.end()
    sum_qk.begin(far_grads[0])
    n1g_a, dgain1, dbias1 = project_back(block_input, own_grads, [tie(far_grads[0], *got), *far_grads[1:]], wt_own, wt_far)
    n1g_b = near(n1g_a)
    got = sum_down.end() + sum_vo.end()
    sum_vo.begin(n1g_a)
    block_output = output(tie(residual, n1g_a, *got), mlp_a, mlp_b, row(b_down))
    input_grad = first_back(block_input, n1g_a, tie(n1g_b, block_output), agrad, row(ln1_gain))
    sum_qk.end()
    sum_vo.end()
    up_sum, down_sum, qk_sum, vo_sum = [each.finish() for each in (sum_up, sum_down, sum_qk, sum_vo)]

    by_device = lambda value: value.reshape(n_dp, -1)
    vectors = jnp.concatenate(
        [by_device(value) for value in (dgain1, dbias1, dgain2, dbias2, db_out, db_down, db_up, db_q, db_v)], 1
    )
    vector_sum = ScatterSum(vectors, n_dp, F32).finish()
    first_sum = vector_sum[: 2 * piece]
    first_sum = first_sum + near(first_sum)
    ends = [2 * piece]
    for size in (piece, piece, piece, piece, f // n_dp, own // n_dp, own // n_dp):
        ends.append(ends[-1] + size)
    rest = [vector_sum[a:b] for a, b in zip(ends, ends[1:])]
    return (
        block_output,
        input_grad,
        first_sum[:piece],
        first_sum[piece:],
        jnp.concatenate([qk_sum, vo_sum[:, :own]], 1).reshape(piece, 3, own),
        jnp.stack([rest[5], rest[6]]),
        vo_sum[:, own:].T,
        rest[2],
        rest[0],
        rest[1],
        up_sum,
        rest[4],
        down_sum.T,
        rest[3],
    )


def solution(mesh):
    return jax.shard_map(
        functools.partial(body, mesh.shape["dp"], mesh.shape["mp"]),
        mesh=mesh,
        in_specs=(
            P("dp", None),
            P("dp", None),
            P("dp", None),
            P("dp", None),
            P(),
            P(),
            P(None, None, "mp"),
            P(None, "mp"),
            P("mp", None),
            P(),
            P(),
            P(),
            P(None, "mp"),
            P("mp"),
            P("mp", None),
            P(),
            P("dp", None),
        ),
        out_specs=(
            P("dp", None),
            P("dp", None),
            P("dp"),
            P("dp"),
            P("dp", None, "mp"),
            P(None, ("mp", "dp")),
            P("mp", "dp"),
            P("dp"),
            P("dp"),
            P("dp"),
            P("dp", "mp"),
            P(("mp", "dp")),
            P("mp", "dp"),
            P("dp"),
        ),
        check_vma=False,
    )
```

```python
import functools

import jax
import jax.numpy as jnp
from jax import lax
from jax.experimental import pallas as pl
from jax.experimental.pallas import tpu as pltpu
from jax.sharding import PartitionSpec as P

HD = 64
QB = 128
GRAIN = 64
LONGEST = 256
GRANT = 58 * 1024 * 1024
TILE = 512
COVER = 10**12
LN1_GAIN, LN1_BIAS, B_OUT, LN2_GAIN, LN2_BIAS, B_DOWN, B_UP = range(7)
MASKED = -1e30
EPS = 1e-05
LOG2E = 1.4426950408889634
F32 = jnp.float32
BF16 = jnp.bfloat16
NT = (((1,), (1,)), ((), ()))
NN = (((1,), (0,)), ((), ()))
TN = (((0,), (0,)), ((), ()))


def mm(a, b, dims):
    return lax.dot_general(a, b, dims, preferred_element_type=F32)


def call(kernel, name, grid, in_specs, out, flops, traffic, args, scratch=(), prefetch=0, carried=(), cover=False):
    return pl.pallas_call(
        kernel,
        grid_spec=pltpu.PrefetchScalarGridSpec(
            num_scalar_prefetch=prefetch,
            grid=grid,
            in_specs=list(in_specs) + [pl.BlockSpec(memory_space=pl.ANY)] * len(carried),
            out_specs=[spec for spec, _, _ in out],
            scratch_shapes=list(scratch),
        ),
        out_shape=[jax.ShapeDtypeStruct(shape, dtype) for _, shape, dtype in out],
        input_output_aliases={len(args) + i: i for i in range(len(carried))},
        compiler_params=pltpu.CompilerParams(vmem_limit_bytes=GRANT),
        cost_estimate=pl.CostEstimate(flops=COVER if cover else 0, bytes_accessed=1024, transcendentals=0),
        name=name,
    )(*args, *carried)


def whole(shape):
    return pl.BlockSpec(shape, lambda *ids: (0,) * len(shape))


def rows(tile, width, skip=0):
    return pl.BlockSpec((tile, width), lambda i, *rest: (i + skip, 0))


def norm_stats(values):
    average = jnp.mean(values, -1, keepdims=True)
    centered = values - average
    variance = jnp.mean(centered * centered, -1, keepdims=True)
    scale = lax.rsqrt(variance + EPS)
    return centered * scale, scale


def norm_back(unit, scale, upstream):
    first = jnp.mean(upstream, -1, keepdims=True)
    second = jnp.mean(upstream * unit, -1, keepdims=True)
    return scale * (upstream - first - unit * second)


def constant(ref, which):
    return ref[which : which + 1, :]


def total(values):
    return jnp.sum(values.astype(F32), 0, keepdims=True)


def gather_rows(ref, first, *values):
    @pl.when(first)
    def _():
        ref[...] = jnp.zeros_like(ref)

    for at, value in enumerate(values):
        ref[at : at + 1, :] += total(value)


def project_kernel(far, x_ref, const_ref, wt_ref, bias_ref, *out):
    if far:
        normed = x_ref[...]
    else:
        unit, _ = norm_stats(x_ref[...].astype(F32))
        normed = (unit * constant(const_ref, LN1_GAIN) + constant(const_ref, LN1_BIAS)).astype(BF16)
        out[3][...] = normed
    q_ref, k_ref, v_ref = out[:3]
    own = q_ref.shape[1]
    q_ref[...] = (mm(normed, wt_ref[:own, :], NT) + bias_ref[0:1, :]).astype(BF16)
    k_ref[...] = mm(normed, wt_ref[own : 2 * own, :], NT).astype(BF16)
    v_ref[...] = (mm(normed, wt_ref[2 * own :, :], NT) + bias_ref[1:2, :]).astype(BF16)


def project(far, x, consts, wt, bias):
    tokens, d = x.shape
    own = wt.shape[0] // 3
    tile = tokens // 4
    out = [(rows(tile, own), (tokens, own), BF16)] * 3
    if not far:
        out.append((rows(tile, d), (tokens, d), BF16))
    return call(
        functools.partial(project_kernel, far), "project_far" if far else "project_own", (tokens // tile,),
        [rows(tile, d), whole(consts.shape), whole(wt.shape), whole(bias.shape)], out,
        6 * tokens * d * own, 6 * tokens * d, (x, consts, wt, bias),
    )


def tables(segment_ids, group_ids, padding):
    sequences, length = segment_ids.shape
    earliest = segment_ids[:, ::QB, None]
    latest = segment_ids[:, QB - 1 :: QB, None]
    key_from = jnp.sum(segment_ids[:, None, :] < earliest, -1, dtype=jnp.int32) // 16 * 16
    key_to = jnp.sum(segment_ids[:, None, :] <= latest, -1, dtype=jnp.int32)
    grains = jnp.maximum((key_to - key_from + GRAIN - 1) // GRAIN, QB // GRAIN)
    starts = jnp.minimum(key_from, length - grains * GRAIN)
    low = segment_ids * 4
    high = low + group_ids
    codes = jnp.stack([jnp.where(padding == 0, high, -1), low, high], 1)
    return starts.reshape(-1), grains.reshape(-1), codes


def extents(length):
    return range(QB // GRAIN, min(QB + 2 * LONGEST, length) // GRAIN + 1)


def head_groups(width):
    return [slice(at, min(at + 2 * HD, width)) for at in range(0, width, 2 * HD)]


def stack_heads(values):
    if values.shape[1] == HD:
        return values
    lane = lax.broadcasted_iota(jnp.int32, values.shape, 1)
    zero = jnp.zeros_like(values)
    return jnp.concatenate(
        [jnp.where(lane < HD, values, zero), jnp.where(lane >= HD, values, zero)], 0
    )


def join_heads(values):
    if values.shape[1] == HD:
        return values
    lane = lax.broadcasted_iota(jnp.int32, (QB, 2 * HD), 1)
    return jnp.where(lane < HD, values[:QB], values[QB:])


def spread_codes(code_ref, column_ref):
    for at in range(0, column_ref.shape[0], QB):
        column_ref[at : at + QB, :] = jnp.broadcast_to(code_ref[0:1, at : at + QB], (QB, QB)).T


def mask_bias(column_ref, code_ref, start, extent, block):
    mine = pl.ds(pl.multiple_of(block * QB, QB), QB)
    codes = column_ref[pl.ds(start, extent), :]
    shape = (extent, QB)
    apart = lax.broadcasted_iota(jnp.int32, shape, 0) - lax.broadcasted_iota(jnp.int32, shape, 1)
    allowed = ((codes >= code_ref[1:2, mine]) & (codes <= code_ref[2:3, mine])) | (
        apart == block * QB - start
    )
    return jnp.where(allowed, jnp.float32(0), jnp.float32(MASKED))


def widen(bias, cols):
    return jnp.concatenate([bias, bias], 1) if cols.stop - cols.start > HD else bias


def each_block(start_ref, grain_ref, length, group, sequence, run):
    turns = length // QB // group

    def step(turn, carry):
        place = (sequence * turns + turn) * group
        grains = functools.reduce(jnp.maximum, [grain_ref[place + i] for i in range(group)])
        starts = [
            pl.multiple_of(jnp.minimum(start_ref[place + i], length - grains * GRAIN), 16) for i in range(group)
        ]
        blocks = [turn * group + i for i in range(group)]
        for extent in extents(length):
            pl.when(grains == extent)(functools.partial(run, extent * GRAIN, blocks, starts))
        return carry

    lax.fori_loop(0, turns, step, 0)


def attend_kernel(far, sequence, start_ref, grain_ref, q_ref, k_ref, v_ref, code_ref, *rest):
    if far:
        own_ctx_ref, own_w_ref, far_w_ref = rest[:3]
        ctx_ref, lse_ref, part_ref, column_ref = rest[-4:]
    else:
        ctx_ref, lse_ref, column_ref = rest[-3:]
    length, width = q_ref.shape
    heads = head_groups(width)
    spread_codes(code_ref, column_ref)

    def run(extent, blocks, starts):
        units, scores, probs, totals, biases = [], [], [], [], []
        for i, (block, start) in enumerate(zip(blocks, starts)):
            here = pl.ds(start, extent)
            mine = pl.ds(pl.multiple_of(block * QB, QB), QB)
            for p, cols in enumerate(heads):
                units.append((i, block, here, mine, p, cols))
                scores.append(mm(k_ref[here, cols], stack_heads(q_ref[mine, cols]), NT))
            biases.append(mask_bias(column_ref, code_ref, start, extent, block))
        for (i, block, here, mine, p, cols), score in zip(units, scores):
            score = score * (0.125 * LOG2E) + widen(biases[i], cols)
            top = jnp.max(score, 0, keepdims=True)
            weights = jnp.exp2(score - top)
            total = jnp.sum(weights, 0, keepdims=True)
            lse_ref[block, p : p + 1, : score.shape[1]] = top + jnp.log2(total)
            totals.append(1.0 / total)
            probs.append(weights.astype(BF16))
        for (i, block, here, mine, p, cols), prob, total in zip(units, probs, totals):
            turned = v_ref[here, cols].T
            both = [
                mm(turned[at * HD : (at + 1) * HD], prob[:, at * QB : (at + 1) * QB], NN)
                * total[:, at * QB : (at + 1) * QB]
                for at in range(prob.shape[1] // QB)
            ]
            ctx_ref[mine, cols] = jnp.concatenate(both, 0).T.astype(BF16)

    each_block(start_ref, grain_ref, length, 2, sequence + pl.program_id(0), run)
    if far:
        part_ref[...] = (
            mm(own_ctx_ref[...], own_w_ref[...], NN) + mm(ctx_ref[...], far_w_ref[...], NN)
        ).astype(BF16)


def attend(q, k, v, table, rest=(), sequence=None, carried=()):
    starts, grains, codes = table
    tokens, width = q.shape
    sequences, _, length = codes.shape
    blocks = length // QB
    skip = sequence or 0
    count = sequences if sequence is None else 1
    tall = rows(length, width, skip)
    lse_block = (blocks, 8, 2 * QB)
    out = [
        (tall, (tokens, width), BF16),
        (pl.BlockSpec(lse_block, lambda s, *ids: (s + skip, 0, 0)), (sequences * blocks, 8, 2 * QB), F32),
    ]
    specs = [tall] * 3 + [pl.BlockSpec((None, 3, length), lambda s, *ids: (s + skip, 0, 0))]
    if rest:
        d = rest[1].shape[1]
        specs += [tall, whole(rest[1].shape), whole(rest[2].shape)]
        out.append((rows(length, d), (count * length, d), BF16))
    return call(
        functools.partial(attend_kernel, bool(rest), skip), "attend_far" if rest else "attend_own", (count,),
        specs, out, 4e9 / sequences * count, 10e6, (starts, grains, q, k, v, codes, *rest),
        scratch=[pltpu.VMEM((length, QB), jnp.int32)], prefetch=2, carried=carried,
    )


def attend_back_kernel(
    start_ref, grain_ref, q_ref, k_ref, v_ref, ctx_ref, grad_ref, lse_ref, code_ref,
    dq_ref, dk_ref, dv_ref, dk_acc, dv_acc, column_ref,
):
    length, width = q_ref.shape
    heads = head_groups(width)
    spread_codes(code_ref, column_ref)
    dk_acc[...] = jnp.zeros_like(dk_acc)
    dv_acc[...] = jnp.zeros_like(dv_acc)

    def run(extent, blocks, starts):
        units, stacked, upstream, scores, grads, biases = [], [], [], [], [], []
        for i, (block, start) in enumerate(zip(blocks, starts)):
            here = pl.ds(start, extent)
            mine = pl.ds(pl.multiple_of(block * QB, QB), QB)
            for p, cols in enumerate(heads):
                units.append((i, block, here, mine, p, cols))
                stacked.append(stack_heads(q_ref[mine, cols]))
                upstream.append(stack_heads(grad_ref[mine, cols]))
                scores.append(mm(k_ref[here, cols], stacked[-1], NT))
                grads.append(mm(v_ref[here, cols], upstream[-1], NT))
            biases.append(mask_bias(column_ref, code_ref, start, extent, block))
        probs, score_grads = [], []
        for (i, block, here, mine, p, cols), score, grad in zip(units, scores, grads):
            turned = (ctx_ref[mine, cols].astype(F32) * grad_ref[mine, cols].astype(F32)).T
            delta = jnp.concatenate(
                [
                    jnp.sum(turned[at : at + HD], 0, keepdims=True)
                    for at in range(0, turned.shape[0], HD)
                ],
                1,
            )
            weights = jnp.exp2(
                score * (0.125 * LOG2E) + widen(biases[i], cols) - lse_ref[block, p : p + 1, : score.shape[1]]
            )
            probs.append(weights.astype(BF16))
            score_grads.append((weights * (grad - delta)).astype(BF16))
        for n, (i, block, here, mine, p, cols) in enumerate(units):
            dv_acc[here, cols] += mm(probs[n], upstream[n], NN)
            dk_acc[here, cols] += mm(score_grads[n], stacked[n], NN)
            dq = join_heads(mm(score_grads[n], k_ref[here, cols], TN))
            dq_ref[mine, cols] = (dq * 0.125).astype(BF16)

    each_block(start_ref, grain_ref, length, 1, pl.program_id(0), run)
    dk_ref[...] = (dk_acc[...] * 0.125).astype(BF16)
    dv_ref[...] = dv_acc[...].astype(BF16)


def attend_back(q, k, v, ctx, grad, lse, table):
    starts, grains, codes = table
    tokens, width = q.shape
    sequences, _, length = codes.shape
    blocks = length // QB
    tall = rows(length, width)
    return call(
        attend_back_kernel, "attend_back", (sequences,),
        [tall] * 5
        + [
            pl.BlockSpec((blocks, 8, 2 * QB), lambda s, *ids: (s, 0, 0)),
            pl.BlockSpec((None, 3, length), lambda s, *ids: (s, 0, 0)),
        ],
        [(tall, (tokens, width), BF16)] * 3, 8e9, 14e6, (starts, grains, q, k, v, ctx, grad, lse, codes),
        scratch=[pltpu.VMEM((length, width), F32)] * 2 + [pltpu.VMEM((length, QB), jnp.int32)], prefetch=2,
    )


def gelu_parts(z):
    spread = jnp.exp2(z * z * (-0.5 * LOG2E))
    t = 1.0 / (1.0 + (0.3275911 * 0.7071067811865476) * jnp.abs(z))
    poly = t * (0.254829592 + t * (-0.284496736 + t * (1.421413741 + t * (-1.453152027 + t * 1.061405429))))
    tail = 0.5 * poly * spread
    return jnp.where(z >= 0, 1.0 - tail, tail), spread


def hidden_pair(z, hidden_grad):
    phi, spread = gelu_parts(z)
    return (z * phi).astype(BF16), hidden_grad * (phi + z * spread * 0.3989422804014327)


def upstream_kernel(cot_ref, down_ref, out_ref, sum_ref):
    cot = cot_ref[...]
    out_ref[...] = mm(cot, down_ref[...], NT).astype(BF16)
    gather_rows(sum_ref, pl.program_id(0) == 0, cot)


def upstream(cot, down):
    tokens, d = cot.shape
    f = down.shape[0]
    tile = tokens // 4
    return call(
        upstream_kernel, "feed_forward_upstream", (4,), [rows(tile, d), whole(down.shape)],
        [(rows(tile, f), (tokens, f), BF16), (whole((1, d)), (1, d), F32)],
        2 * tokens * d * f, 4 * tokens * d, (cot, down),
    )


def hidden_kernel(x_ref, part_a_ref, part_b_ref, const_ref, up_ref, cot_down_ref, *rest):
    residual_ref, n2_ref, hidden_ref, upg_ref, sum_ref = rest[-5:]
    residual = (
        x_ref[...].astype(F32)
        + (part_a_ref[...].astype(F32) + part_b_ref[...].astype(F32))
        + constant(const_ref, B_OUT)
    )
    residual_ref[...] = residual.astype(BF16)
    unit, _ = norm_stats(residual)
    normed = (unit * constant(const_ref, LN2_GAIN) + constant(const_ref, LN2_BIAS)).astype(BF16)
    n2_ref[...] = normed
    z = mm(normed, up_ref[...], NN) + constant(const_ref, B_UP)
    hidden, grad = hidden_pair(z, cot_down_ref[...].astype(F32))
    hidden_ref[...] = hidden
    upg_ref[...] = grad.astype(BF16)
    gather_rows(sum_ref, pl.program_id(0) == 0, grad)


def hidden_own(sequence, length, x, part_a, part_b, consts, up, cot_down, carried=()):
    tokens, d = x.shape
    f = up.shape[1]
    tile = length // 4
    tall, wide = rows(tile, d, 4 * sequence), rows(tile, f, 4 * sequence)
    near = rows(tile, d)
    return call(
        hidden_kernel, "hidden_own", (4,),
        [tall, near, near, whole(consts.shape), whole(up.shape), wide],
        [(tall, (tokens, d), BF16)] * 2 + [(wide, (tokens, f), BF16)] * 2 + [(whole((1, f)), (1, f), F32)],
        4 * length * d * f, 16 * length * d, (x, part_a, part_b, consts, up, cot_down), carried=carried,
    )


def products_kernel(
    n2_ref, cot_ref, hidden_ref, upg_ref, up_a_ref, down_a_ref, far_ref, bias_ref, mlp_ref, n2g_ref
):
    d = n2_ref.shape[1]
    up_b, down_b = far_ref[:d, :], far_ref[d:, :]
    bias = jnp.concatenate([bias_ref[at : at + 1, :] for at in range(2, bias_ref.shape[0])], 1)
    z = mm(n2_ref[...], up_b, NN) + bias
    hidden_grad = mm(cot_ref[...], down_b, NT)
    mlp_own = mm(hidden_ref[...], down_a_ref[...], NN)
    n2g_own = mm(upg_ref[...], up_a_ref[...], NT)
    hidden, grad = hidden_pair(z, hidden_grad)
    mlp_ref[...] = (mlp_own + mm(hidden, down_b, NN)).astype(BF16)
    n2g_ref[...] = (n2g_own + mm(grad.astype(BF16), up_b, NT)).astype(BF16)


def products(span, n2, cot, hidden, upg, up, down, far, bias, cover):
    d, f = up.shape
    first, count = span
    size = count * TILE
    tall, wide = rows(TILE, d, first), rows(TILE, f, first)
    return call(
        products_kernel, "feed_forward", (count,),
        [tall, tall, wide, wide, whole(up.shape), whole(down.shape), whole(far.shape), whole(bias.shape)],
        [(rows(TILE, d), (size, d), BF16)] * 2,
        12 * size * d * f, 16 * size * d, (n2, cot, hidden, upg, up, down, far, bias), cover=cover,
    )


def weights_kernel(a_ref, b_ref, c_ref, e_ref, one_ref, two_ref):
    one_ref[...] = mm(a_ref[...], b_ref[...], TN).astype(BF16)
    two_ref[...] = mm(c_ref[...], e_ref[...], TN).astype(BF16)


def weight_products(a, b, c, e):
    tokens, d = a.shape
    f = b.shape[1]
    tile = d // 2
    side = pl.BlockSpec((tokens, tile), lambda i: (0, i))
    return call(
        weights_kernel, "feed_forward_weights", (2,), [side, whole(b.shape), side, whole(e.shape)],
        [(rows(tile, f), (d, f), BF16)] * 2, 4 * tokens * d * f, 8 * tokens * d, (a, b, c, e),
    )


def middle_kernel(residual_ref, grad_a_ref, grad_b_ref, cot_ref, const_ref, own_w_ref, far_w_ref, *rest):
    agrad_ref, own_cg_ref, far_cg_ref, sum_ref = rest[-4:]
    unit, scale = norm_stats(residual_ref[...].astype(F32))
    summed = grad_a_ref[...].astype(F32) + grad_b_ref[...].astype(F32)
    rgrad = cot_ref[...].astype(F32) + norm_back(unit, scale, summed * constant(const_ref, LN2_GAIN))
    agrad = rgrad.astype(BF16)
    agrad_ref[...] = agrad
    own_cg_ref[...] = mm(agrad, own_w_ref[...], NT).astype(BF16)
    far_cg_ref[...] = mm(agrad, far_w_ref[...], NT).astype(BF16)
    gather_rows(sum_ref, pl.program_id(0) == 0, rgrad, summed * unit, summed)


def middle(span, residual, grad_a, grad_b, cot, consts, own_w, far_w, carried=()):
    tokens, d = residual.shape
    own = own_w.shape[0]
    first, count = span
    tile = TILE // 2
    tall, slim, near = rows(tile, d, 2 * first), rows(tile, own, 2 * first), rows(tile, d)
    return call(
        middle_kernel, "second_norm_back", (2 * count,),
        [tall, near, near, tall, whole(consts.shape), whole(own_w.shape), whole(far_w.shape)],
        [(tall, (tokens, d), BF16)] + [(slim, (tokens, own), BF16)] * 2 + [(whole((3, d)), (3, d), F32)],
        4 * tokens * d * own, 12 * tokens * d, (residual, grad_a, grad_b, cot, consts, own_w, far_w), carried=carried,
    )


def output_kernel(residual_ref, mlp_a_ref, mlp_b_ref, const_ref, *rest):
    rest[-1][...] = (
        residual_ref[...].astype(F32)
        + ((mlp_a_ref[...].astype(F32) + mlp_b_ref[...].astype(F32)) + constant(const_ref, B_DOWN))
    ).astype(BF16)


def output(span, residual, mlp_a, mlp_b, consts, carried=()):
    tokens, d = residual.shape
    first, count = span
    tall, near = rows(TILE, d, first), rows(TILE, d)
    return call(
        output_kernel, "block_output", (count,), [tall, near, near, whole(consts.shape)],
        [(tall, (tokens, d), BF16)], 4 * tokens * d, 8 * tokens * d, (residual, mlp_a, mlp_b, consts), carried=carried,
    )


def attention_weights_kernel(n1_ref, dq_ref, dk_ref, dv_ref, agrad_ref, ctx_ref, out_ref, sum_ref):
    own = dq_ref.shape[1]
    normed = n1_ref[...]
    for at, grad_ref in enumerate((dq_ref, dk_ref, dv_ref)):
        out_ref[:, at * own : (at + 1) * own] = mm(normed, grad_ref[...], TN).astype(BF16)
    out_ref[:, 3 * own :] = mm(agrad_ref[...], ctx_ref[...], TN).astype(BF16)
    sum_ref[0:1, :] = total(dq_ref[...])
    sum_ref[1:2, :] = total(dv_ref[...])


def attention_weights(n1, dq, dk, dv, agrad, ctx):
    tokens, d = n1.shape
    own = dq.shape[1]
    tile = d // 2
    side = pl.BlockSpec((tokens, tile), lambda i: (0, i))
    return call(
        attention_weights_kernel, "attention_weights", (2,),
        [side] + [whole(dq.shape)] * 3 + [side, whole(ctx.shape)],
        [(rows(tile, 4 * own), (d, 4 * own), BF16), (whole((2, own)), (2, own), F32)],
        8 * tokens * d * own, 8 * tokens * d, (n1, dq, dk, dv, agrad, ctx),
    )


def project_back_kernel(
    x_ref, aq_ref, ak_ref, av_ref, bq_ref, bk_ref, bv_ref, wa_ref, wb_ref, n1g_ref, sum_ref
):
    own = aq_ref.shape[1]
    grad = None
    for w_ref, grads in ((wa_ref, (aq_ref, ak_ref, av_ref)), (wb_ref, (bq_ref, bk_ref, bv_ref))):
        for place, grad_ref in enumerate(grads):
            here = mm(grad_ref[...], w_ref[place * own : (place + 1) * own, :], NN)
            grad = here if grad is None else grad + here
    n1g_ref[...] = grad.astype(BF16)
    unit, _ = norm_stats(x_ref[...].astype(F32))
    gather_rows(sum_ref, pl.program_id(0) == 0, grad * unit, grad)


def project_back(x, own_grads, far_grads, own_wt, far_wt):
    tokens, d = x.shape
    own = own_grads[0].shape[1]
    tile = tokens // 4
    return call(
        project_back_kernel, "project_back", (4,),
        [rows(tile, d)] + [rows(tile, own)] * 6 + [whole(own_wt.shape)] * 2,
        [(rows(tile, d), (tokens, d), BF16), (whole((2, d)), (2, d), F32)],
        12 * tokens * d * own, 8 * tokens * d, (x, *own_grads, *far_grads, own_wt, far_wt),
    )


def first_back_kernel(x_ref, grad_a_ref, grad_b_ref, rgrad_ref, const_ref, out_ref):
    unit, scale = norm_stats(x_ref[...].astype(F32))
    upstream = (grad_a_ref[...].astype(F32) + grad_b_ref[...].astype(F32)) * constant(const_ref, LN1_GAIN)
    out_ref[...] = rgrad_ref[...].astype(F32) + norm_back(unit, scale, upstream)


def first_back(x, grad_a, grad_b, rgrad, consts):
    tokens, d = x.shape
    tile = tokens // 8
    tall = rows(tile, d)
    return call(
        first_back_kernel, "first_norm_back", (8,), [tall] * 4 + [whole(consts.shape)],
        [(tall, (tokens, d), F32)], 20 * tokens * d, 12 * tokens * d, (x, grad_a, grad_b, rgrad, consts),
    )[0]


def swap(value, axis, size, bit):
    return lax.ppermute(value, axis, [(i, i ^ bit) for i in range(size)])


def tie(value, *others):
    return lax.optimization_barrier((value,) + others)[0]


class ScatterSum:
    def __init__(self, terms, size, first=()):
        self.size, self.levels = size, size.bit_length() - 1
        self.bits = list(first) + [bit for bit in range(self.levels) if bit not in first]
        self.left = list(reversed(range(self.levels)))
        self.me = lax.axis_index("dp")
        self.value = terms.reshape((2,) * self.levels + (terms.shape[0] // size, terms.shape[1]))

    def begin(self):
        bit = self.bits.pop(0)
        axis = self.left.index(bit)
        self.left.pop(axis)
        mine = (self.me >> bit) & 1
        give = lax.dynamic_index_in_dim(self.value, 1 - mine, axis, keepdims=False).astype(BF16)
        self.got = swap(give, "dp", self.size, 1 << bit)
        self.keep = lax.dynamic_index_in_dim(self.value, mine, axis, keepdims=False)

    def end(self, *others):
        got = tie(self.got, *others) if others else self.got
        self.value = self.keep.astype(F32) + got.astype(F32)
        return got

    def finish(self):
        while self.bits:
            self.begin()
            self.end()
        return self.value


def body(
    n_dp,
    n_mp,
    block_input,
    segment_ids,
    group_ids,
    padding,
    ln1_gain,
    ln1_bias,
    w_qkv,
    b_qv,
    w_out,
    b_out,
    ln2_gain,
    ln2_bias,
    w_up,
    b_up,
    w_down,
    b_down,
    cotangent,
):
    tokens, d = block_input.shape
    sequences, length = segment_ids.shape
    own = w_qkv.shape[2]
    far = lambda value: swap(value, "mp", n_mp, 2)
    near = lambda value: swap(value, "mp", n_mp, 1)
    beside = lambda value: swap(value, "dp", n_dp, 1)

    half = lax.axis_index("dp") & 1
    wt_own = jnp.transpose(w_qkv, (1, 2, 0)).reshape(3 * own, d)
    size = wt_own.shape[0] // 2
    wt_a = far(lax.dynamic_slice_in_dim(wt_own, half * size, size, 0))
    small_own = jnp.concatenate([b_qv, b_up.reshape(-1, own)], 0)
    small_far = far(small_own)
    consts = jnp.concatenate([ln1_gain, ln1_bias, b_out, ln2_gain, ln2_bias, b_down, b_up]).reshape(-1, d)
    table = tables(segment_ids, group_ids, padding)

    *qkv_own, n1 = project(False, block_input, consts, wt_own, b_qv)
    w_out_far = far(tie(w_out, n1))
    cot_down, sum_cot = upstream(tie(cotangent, n1), w_down)
    wt_a, cot_down = lax.optimization_barrier((wt_a, cot_down))
    wt_b = beside(wt_a)
    mlp_far = far(jnp.concatenate([tie(w_up, cot_down), w_down], 0))
    ctx_own, lse_own = attend(tie(qkv_own[0], wt_a, cot_down), *qkv_own[1:], table)
    wt_b = tie(wt_b, ctx_own)
    wt_far = jnp.where(half == 0, jnp.concatenate([wt_a, wt_b], 0), jnp.concatenate([wt_b, wt_a], 0))
    qkv_far = project(True, n1, consts, wt_far, small_far)
    parts, carried = [], ()
    for s in range(sequences):
        ctx_far, lse_far, part = attend(*qkv_far, table, (ctx_own, w_out, w_out_far), s, carried)
        carried = (ctx_far, lse_far)
        parts.append((part, near(part)))
    carried, sums_up = (), []
    for s, (part, other) in enumerate(parts):
        if s == 0:
            other = tie(other, parts[-1][0])
        elif carried:
            other = tie(other, carried[0])
        *carried, sum_up = hidden_own(s, length, block_input, part, other, consts, w_up, cot_down, carried)
        sums_up.append(sum_up)
    residual, n2, hidden, upg = carried
    dw_up, dw_down = weight_products(n2, upg, cotangent, hidden)
    sum_w_up, sum_w_down = ScatterSum(dw_up, n_dp), ScatterSum(dw_down, n_dp, (1, 0))
    sum_w_up.begin()
    sum_w_down.begin()
    mlp_far = tie(mlp_far, dw_up)
    tiles = tokens // TILE
    spans = ((0, tiles - 1), (tiles - 1, 1))
    shares, gate = [], (dw_up,)
    for span in spans:
        mlp, n2g = products(span, tie(n2, *gate), cotangent, hidden, upg, w_up, w_down, mlp_far, small_far, bool(shares))
        shares.append((span, mlp, n2g, near(n2g)))
        if len(shares) == 1:
            gate = (n2g, sum_w_up.end(n2g), sum_w_down.end(n2g))
            sum_w_up.begin()
            sum_w_down.begin()
    gate, carried, sums_mid = (n2g,), (), []
    for span, mlp, n2g, other in shares:
        other = tie(other, *gate)
        *carried, sum_mid = middle(span, residual, n2g, other, cotangent, consts, w_out, w_out_far, carried)
        sums_mid.append(sum_mid)
        if len(sums_mid) == 1:
            gate = (carried[0], sum_w_up.end(sum_mid), sum_w_down.end(sum_mid))
            sum_w_up.begin()
            sum_w_down.begin()
    agrad, cgrad_own, cgrad_far = carried
    own_grads = attend_back(*qkv_own, ctx_own, cgrad_own, lse_own, table)
    others = [near(tie(mlp, own_grads[0])) for _, mlp, _, _ in shares]
    got = [each.end(own_grads[0]) for each in (sum_w_up, sum_w_down)]
    dw_attn, sum_qv = attention_weights(n1, tie(own_grads[0], *got), *own_grads[1:], agrad, ctx_own)
    sum_attn = ScatterSum(dw_attn, n_dp)
    sum_attn.begin()
    far_grads = attend_back(*qkv_far, ctx_far, tie(cgrad_far, dw_attn), lse_far, table)
    got = sum_attn.end(far_grads[0])
    sum_attn.begin()
    n1g, sum_first = project_back(block_input, own_grads, [tie(far_grads[0], got), *far_grads[1:]], wt_own, wt_far)
    sum_first = sum_first + near(sum_first)
    n1g_near = near(tie(n1g, sum_first))
    add = lambda values: functools.reduce(jnp.add, values)
    wide_qv = jnp.concatenate([sum_qv.reshape(1, -1), jnp.zeros((1, d - 2 * own), F32)], 1)
    sums = jnp.concatenate([sum_first, add(sums_mid), sum_cot, add(sums_up), wide_qv], 0)
    outputs = ()
    for bit in range(n_dp.bit_length() - 1):
        other = swap(sums, "dp", n_dp, 1 << bit)
        if bit < len(shares):
            span, mlp = shares[bit][:2]
            outputs = output(span, tie(residual, n1g, sums), mlp, others[bit], consts, outputs)
            other = tie(other, outputs[0])
        sums = sums + other
    block_output = outputs[0]
    got = sum_attn.end(block_output)
    sum_attn.begin()
    input_grad = first_back(block_input, n1g, tie(n1g_near, block_output, got), agrad, consts)
    sum_attn.end(input_grad)
    attn_sum = sum_attn.finish()

    piece, tiny = d // n_dp, own // n_dp
    me = lax.axis_index("dp")
    mine = lax.dynamic_slice(sums, (0, me * piece), (sums.shape[0] - 1, piece))
    fp = b_up.shape[0] // n_dp
    vectors = [mine[i] for i in range(7)]
    return (
        block_output,
        input_grad,
        vectors[0],
        vectors[1],
        attn_sum[:, : 3 * own].reshape(piece, 3, own),
        lax.dynamic_slice(sums[7, : 2 * own].reshape(2, own), (0, me * tiny), (2, tiny)),
        attn_sum[:, 3 * own :].T,
        vectors[2],
        vectors[3],
        vectors[4],
        sum_w_up.finish(),
        vectors[6],
        sum_w_down.finish().T,
        vectors[5],
    )


def solution(mesh):
    return jax.shard_map(
        functools.partial(body, mesh.shape["dp"], mesh.shape["mp"]),
        mesh=mesh,
        in_specs=(
            P("dp", None),
            P("dp", None),
            P("dp", None),
            P("dp", None),
            P(),
            P(),
            P(None, None, "mp"),
            P(None, "mp"),
            P("mp", None),
            P(),
            P(),
            P(),
            P(None, "mp"),
            P("mp"),
            P("mp", None),
            P(),
            P("dp", None),
        ),
        out_specs=(
            P("dp", None),
            P("dp", None),
            P("dp"),
            P("dp"),
            P("dp", None, "mp"),
            P(None, ("mp", "dp")),
            P("mp", "dp"),
            P("dp"),
            P("dp"),
            P("dp"),
            P("dp", "mp"),
            P(("mp", "dp")),
            P("mp", "dp"),
            P("dp"),
        ),
        check_vma=False,
    )
```

```python
import functools

import jax
import jax.numpy as jnp
from jax import lax
from jax.experimental import pallas as pl
from jax.experimental.pallas import tpu as pltpu
from jax.sharding import PartitionSpec as P

HD = 64
QB = 128
GRAIN = 64
LONGEST = 256
GRANTS = dict(
    attend_own=58, attend_far=58, attend_own_back=58, attend_far_back=58, upstream=58, hidden_own=58, feed_forward=58,
    second_norm_back=58, block_output=58, first_norm_back=58, merge=58, last_sum=58,
)
TILE = 512
COVER = 10**12
MASKED = -1e30
EPS = 1e-05
LOG2E = 1.4426950408889634
F32 = jnp.float32
BF16 = jnp.bfloat16
NT = (((1,), (1,)), ((), ()))
NN = (((1,), (0,)), ((), ()))
TN = (((0,), (0,)), ((), ()))


def mm(a, b, dims):
    return lax.dot_general(a, b, dims, preferred_element_type=F32)


def flat(ref):
    return ref[...].reshape(1, -1)


def call(kernel, name, grid, in_specs, out, args, scratch=(), prefetch=0, carried=(), cover=False, carried_specs=()):
    return pl.pallas_call(
        kernel,
        grid_spec=pltpu.PrefetchScalarGridSpec(
            num_scalar_prefetch=prefetch,
            grid=grid,
            in_specs=list(in_specs) + list(carried_specs or [pl.BlockSpec(memory_space=pl.ANY)] * len(carried)),
            out_specs=[spec for spec, _, _ in out],
            scratch_shapes=list(scratch),
        ),
        out_shape=[jax.ShapeDtypeStruct(shape, dtype) for _, shape, dtype in out],
        input_output_aliases={len(args) + i: i for i in range(len(carried))},
        compiler_params=pltpu.CompilerParams(vmem_limit_bytes=GRANTS[name] * 1024 * 1024),
        cost_estimate=pl.CostEstimate(flops=COVER if cover else 0, bytes_accessed=1024, transcendentals=0),
        name=name,
    )(*args, *carried)


def whole(shape):
    return pl.BlockSpec(shape, lambda *ids: (0,) * len(shape))


def rows(tile, width, skip=0):
    return pl.BlockSpec((tile, width), lambda i, *rest: (i + skip, 0))


def norm_stats(values):
    average = jnp.mean(values, -1, keepdims=True)
    centered = values - average
    variance = jnp.mean(centered * centered, -1, keepdims=True)
    scale = lax.rsqrt(variance + EPS)
    return centered * scale, scale


def norm_back(unit, scale, upstream):
    first = jnp.mean(upstream, -1, keepdims=True)
    second = jnp.mean(upstream * unit, -1, keepdims=True)
    return scale * (upstream - first - unit * second)


def total(values):
    return jnp.sum(values.astype(F32), 0, keepdims=True)


def gather_rows(ref, first, *values):
    @pl.when(first)
    def _():
        ref[...] = jnp.zeros_like(ref)

    for at, value in enumerate(values):
        ref[at : at + 1, :] += total(value)


def tables(segment_ids, group_ids, padding):
    sequences, length = segment_ids.shape
    earliest = segment_ids[:, ::QB, None]
    latest = segment_ids[:, QB - 1 :: QB, None]
    key_from = jnp.sum(segment_ids[:, None, :] < earliest, -1, dtype=jnp.int32) // 16 * 16
    key_to = jnp.sum(segment_ids[:, None, :] <= latest, -1, dtype=jnp.int32)
    grains = jnp.maximum((key_to - key_from + GRAIN - 1) // GRAIN, QB // GRAIN)
    starts = jnp.minimum(key_from, length - grains * GRAIN)
    low = segment_ids * 4
    high = low + group_ids
    codes = jnp.stack([jnp.where(padding == 0, high, -1), low, high], 1)
    return starts.reshape(-1), grains.reshape(-1), codes


def extents(length):
    return range(QB // GRAIN, min(QB + 2 * LONGEST, length) // GRAIN + 1)


def head_groups(width):
    return [slice(at, min(at + 2 * HD, width)) for at in range(0, width, 2 * HD)]


def stack_heads(values):
    if values.shape[1] == HD:
        return values
    lane = lax.broadcasted_iota(jnp.int32, values.shape, 1)
    zero = jnp.zeros_like(values)
    return jnp.concatenate(
        [jnp.where(lane < HD, values, zero), jnp.where(lane >= HD, values, zero)], 0
    )


def join_heads(values):
    if values.shape[1] == HD:
        return values
    lane = lax.broadcasted_iota(jnp.int32, (QB, 2 * HD), 1)
    return jnp.where(lane < HD, values[:QB], values[QB:])


def spread_codes(code_ref, column_ref):
    for at in range(0, column_ref.shape[0], QB):
        column_ref[at : at + QB, :] = jnp.broadcast_to(code_ref[0:1, at : at + QB], (QB, QB)).T


def mask_bias(column_ref, code_ref, start, extent, block):
    mine = pl.ds(pl.multiple_of(block * QB, QB), QB)
    codes = column_ref[pl.ds(start, extent), :]
    shape = (extent, QB)
    apart = lax.broadcasted_iota(jnp.int32, shape, 0) - lax.broadcasted_iota(jnp.int32, shape, 1)
    allowed = ((codes >= code_ref[1:2, mine]) & (codes <= code_ref[2:3, mine])) | (
        apart == block * QB - start
    )
    return jnp.where(allowed, jnp.float32(0), jnp.float32(MASKED))


def widen(bias, cols):
    return jnp.concatenate([bias, bias], 1) if cols.stop - cols.start > HD else bias


def each_block(start_ref, grain_ref, length, group, sequence, run):
    turns = length // QB // group

    def step(turn, carry):
        place = (sequence * turns + turn) * group
        grains = functools.reduce(jnp.maximum, [grain_ref[place + i] for i in range(group)])
        starts = [
            pl.multiple_of(jnp.minimum(start_ref[place + i], length - grains * GRAIN), 16) for i in range(group)
        ]
        blocks = [turn * group + i for i in range(group)]
        for extent in extents(length):
            pl.when(grains == extent)(functools.partial(run, extent * GRAIN, blocks, starts))
        return carry

    lax.fori_loop(0, turns, step, 0)


def project(normed, wt_ref, q_bias, v_bias, q_ref, k_ref, v_ref):
    own = q_ref.shape[1]
    q_ref[...] = (mm(normed, wt_ref[:own, :], NT) + q_bias).astype(BF16)
    k_ref[...] = mm(normed, wt_ref[own : 2 * own, :], NT).astype(BF16)
    v_ref[...] = (mm(normed, wt_ref[2 * own :, :], NT) + v_bias).astype(BF16)


def attend(sequence, start_ref, grain_ref, code_ref, column_ref, q_ref, k_ref, v_ref, ctx_ref, lse_ref):
    length, width = q_ref.shape
    heads = head_groups(width)
    spread_codes(code_ref, column_ref)

    def run(extent, blocks, starts):
        units, scores, probs, totals, biases = [], [], [], [], []
        for i, (block, start) in enumerate(zip(blocks, starts)):
            here = pl.ds(start, extent)
            mine = pl.ds(pl.multiple_of(block * QB, QB), QB)
            for p, cols in enumerate(heads):
                units.append((i, block, here, mine, p, cols))
                scores.append(mm(k_ref[here, cols], stack_heads(q_ref[mine, cols]), NT))
            biases.append(mask_bias(column_ref, code_ref, start, extent, block))
        for (i, block, here, mine, p, cols), score in zip(units, scores):
            score = score * (0.125 * LOG2E) + widen(biases[i], cols)
            top = jnp.max(score, 0, keepdims=True)
            weights = jnp.exp2(score - top)
            summed = jnp.sum(weights, 0, keepdims=True)
            lse_ref[block, p : p + 1, : score.shape[1]] = top + jnp.log2(summed)
            totals.append(1.0 / summed)
            probs.append(weights.astype(BF16))
        for (i, block, here, mine, p, cols), prob, scale in zip(units, probs, totals):
            turned = v_ref[here, cols].T
            both = [
                mm(turned[at * HD : (at + 1) * HD], prob[:, at * QB : (at + 1) * QB], NN)
                * scale[:, at * QB : (at + 1) * QB]
                for at in range(prob.shape[1] // QB)
            ]
            ctx_ref[mine, cols] = jnp.concatenate(both, 0).T.astype(BF16)

    each_block(start_ref, grain_ref, length, 2, sequence, run)


def own_kernel(
    start_ref, grain_ref, code_ref, x_ref, gain_ref, bias_ref, wt_ref, qv_ref,
    q_ref, k_ref, v_ref, ctx_ref, lse_ref, n1_ref, column_ref,
):
    unit, _ = norm_stats(x_ref[...].astype(F32))
    normed = (unit * flat(gain_ref) + flat(bias_ref)).astype(BF16)
    n1_ref[...] = normed
    project(normed, wt_ref, qv_ref[0:1, :], qv_ref[1:2, :], q_ref, k_ref, v_ref)
    attend(pl.program_id(0), start_ref, grain_ref, code_ref, column_ref, q_ref, k_ref, v_ref, ctx_ref, lse_ref)


def attention_outs(tokens, width, length, sequences, skip=0):
    tall = rows(length, width, skip)
    lse = (length // QB, 8, 2 * QB)
    return [(tall, (tokens, width), BF16)] * 4 + [
        (pl.BlockSpec(lse, lambda s, *ids: (s + skip, 0, 0)), (sequences * lse[0],) + lse[1:], F32)
    ]


def projections(pack):
    return pl.BlockSpec((pack.shape[0] // 4 * 3, pack.shape[1]), lambda *ids: (0, 0))


def out_weights(pack):
    return pl.BlockSpec((pack.shape[0] // 4, pack.shape[1]), lambda *ids: (3, 0))


def codes_spec(codes, skip=0):
    return pl.BlockSpec((None,) + codes.shape[1:], lambda s, *ids: (s + skip, 0, 0))


def attend_own(table, x, gain, bias, wt, b_qv):
    starts, grains, codes = table
    tokens, d = x.shape
    sequences, _, length = codes.shape
    return call(
        own_kernel, "attend_own", (sequences,),
        [codes_spec(codes), rows(length, d), whole(gain.shape), whole(bias.shape), projections(wt), whole(b_qv.shape)],
        attention_outs(tokens, b_qv.shape[1], length, sequences) + [(rows(length, d), (tokens, d), BF16)],
        (starts, grains, codes, x, gain, bias, wt, b_qv),
        scratch=[pltpu.VMEM((length, QB), jnp.int32)], prefetch=2,
    )


def far_kernel(
    sequence, start_ref, grain_ref, code_ref, n1_ref, wt_ref, small_ref, own_ctx_ref, own_w_ref, far_w_ref, *rest
):
    q_ref, k_ref, v_ref, ctx_ref, lse_ref, part_ref, column_ref = rest[-7:]
    project(n1_ref[...], wt_ref, small_ref[0:1, :], small_ref[1:2, :], q_ref, k_ref, v_ref)
    attend(sequence, start_ref, grain_ref, code_ref, column_ref, q_ref, k_ref, v_ref, ctx_ref, lse_ref)
    part_ref[...] = (
        mm(own_ctx_ref[...], own_w_ref[...], NN) + mm(ctx_ref[...], far_w_ref[...], NN)
    ).astype(BF16)


def attend_far(sequence, table, n1, far, small, own_ctx, pack, carried=()):
    starts, grains, codes = table
    tokens, d = n1.shape
    sequences, _, length = codes.shape
    own = own_ctx.shape[1]
    return call(
        functools.partial(far_kernel, sequence), "attend_far", (1,),
        [codes_spec(codes, sequence), rows(length, d, sequence), projections(far), whole(small.shape)]
        + [rows(length, own, sequence), out_weights(pack), out_weights(far)],
        attention_outs(tokens, own, length, sequences, sequence) + [(rows(length, d), (length, d), BF16)],
        (starts, grains, codes, n1, far, small, own_ctx, pack, far),
        scratch=[pltpu.VMEM((length, QB), jnp.int32)], prefetch=2, carried=carried,
    )


def attend_back(
    start_ref, grain_ref, code_ref, column_ref, q_ref, k_ref, v_ref, ctx_ref, grad_ref, lse_ref,
    dq_ref, dk_ref, dv_ref, dk_acc, dv_acc,
):
    length, width = q_ref.shape
    heads = head_groups(width)
    spread_codes(code_ref, column_ref)
    dk_acc[...] = jnp.zeros_like(dk_acc)
    dv_acc[...] = jnp.zeros_like(dv_acc)

    def run(extent, blocks, starts):
        units, stacked, upstream, scores, grads, biases = [], [], [], [], [], []
        for i, (block, start) in enumerate(zip(blocks, starts)):
            here = pl.ds(start, extent)
            mine = pl.ds(pl.multiple_of(block * QB, QB), QB)
            for p, cols in enumerate(heads):
                units.append((i, block, here, mine, p, cols))
                stacked.append(stack_heads(q_ref[mine, cols]))
                upstream.append(stack_heads(grad_ref[mine, cols]))
                scores.append(mm(k_ref[here, cols], stacked[-1], NT))
                grads.append(mm(v_ref[here, cols], upstream[-1], NT))
            biases.append(mask_bias(column_ref, code_ref, start, extent, block))
        probs, score_grads = [], []
        for (i, block, here, mine, p, cols), score, grad in zip(units, scores, grads):
            turned = (ctx_ref[mine, cols].astype(F32) * grad_ref[mine, cols].astype(F32)).T
            delta = jnp.concatenate(
                [
                    jnp.sum(turned[at : at + HD], 0, keepdims=True)
                    for at in range(0, turned.shape[0], HD)
                ],
                1,
            )
            weights = jnp.exp2(
                score * (0.125 * LOG2E) + widen(biases[i], cols) - lse_ref[block, p : p + 1, : score.shape[1]]
            )
            probs.append(weights.astype(BF16))
            score_grads.append((weights * (grad - delta)).astype(BF16))
        for n, (i, block, here, mine, p, cols) in enumerate(units):
            dv_acc[here, cols] += mm(probs[n], upstream[n], NN)
            dk_acc[here, cols] += mm(score_grads[n], stacked[n], NN)
            dq = join_heads(mm(score_grads[n], k_ref[here, cols], TN))
            dq_ref[mine, cols] = (dq * 0.125).astype(BF16)

    each_block(start_ref, grain_ref, length, 1, pl.program_id(0), run)
    dk_ref[...] = (dk_acc[...] * 0.125).astype(BF16)
    dv_ref[...] = dv_acc[...].astype(BF16)


def own_back_kernel(
    order, start_ref, grain_ref, half_ref, code_ref, q_ref, k_ref, v_ref, ctx_ref, grad_ref, lse_ref, n1_ref, agrad_ref,
    dq_ref, dk_ref, dv_ref, keep_ref, give_ref, sum_ref, dk_acc, dv_acc, column_ref, weight_acc,
):
    attend_back(
        start_ref, grain_ref, code_ref, column_ref, q_ref, k_ref, v_ref, ctx_ref, grad_ref, lse_ref,
        dq_ref, dk_ref, dv_ref, dk_acc, dv_acc,
    )
    first = pl.program_id(0) == 0

    @pl.when(first)
    def _():
        weight_acc[...] = jnp.zeros_like(weight_acc)
        sum_ref[...] = jnp.zeros_like(sum_ref)

    own = dq_ref.shape[1]
    normed = n1_ref[...]
    for at, grad in enumerate((dq_ref, dk_ref, dv_ref)):
        weight_acc[:, at * own : (at + 1) * own] += mm(normed, grad[...], TN)
    weight_acc[:, 3 * own :] += mm(agrad_ref[...], ctx_ref[...], TN)
    sum_ref[0:1, :] += total(dq_ref[...])
    sum_ref[1:2, :] += total(dv_ref[...])

    @pl.when(pl.program_id(0) == pl.num_programs(0) - 1)
    def _():
        split_chunks(half_ref[0], order, weight_acc, keep_ref, give_ref)


def attend_own_back(table, half, order, q, k, v, ctx, grad, lse, n1, agrad):
    starts, grains, codes = table
    tokens, d = n1.shape
    own = q.shape[1]
    sequences, _, length = codes.shape
    tall, high = rows(length, own), rows(length, d)
    lse_spec = pl.BlockSpec((length // QB, 8, 2 * QB), lambda s, *ids: (s, 0, 0))
    count = len(order[0])
    chunk = (count, d // (2 * count), 4 * own)
    return call(
        functools.partial(own_back_kernel, order), "attend_own_back", (sequences,),
        [codes_spec(codes)] + [tall] * 5 + [lse_spec, high, high],
        [(tall, (tokens, own), BF16)] * 3 + [(whole(chunk), chunk, BF16)] * 2 + [(whole((2, own)), (2, own), F32)],
        (starts, grains, half, codes, q, k, v, ctx, grad, lse, n1, agrad),
        scratch=[pltpu.VMEM((length, own), F32)] * 2
        + [pltpu.VMEM((length, QB), jnp.int32), pltpu.VMEM((d, 4 * own), F32)], prefetch=3, cover=True,
    )


def far_back_kernel(
    start_ref, grain_ref, code_ref, q_ref, k_ref, v_ref, ctx_ref, grad_ref, lse_ref,
    x_ref, aq_ref, ak_ref, av_ref, wa_ref, wb_ref,
    n1g_ref, sum_ref, dk_acc, dv_acc, column_ref, dq_ref, dk_ref, dv_ref,
):
    attend_back(
        start_ref, grain_ref, code_ref, column_ref, q_ref, k_ref, v_ref, ctx_ref, grad_ref, lse_ref,
        dq_ref, dk_ref, dv_ref, dk_acc, dv_acc,
    )
    own = aq_ref.shape[1]
    grad = None
    for w_ref, grads in ((wa_ref, (aq_ref, ak_ref, av_ref)), (wb_ref, (dq_ref, dk_ref, dv_ref))):
        for place, one_ref in enumerate(grads):
            here = mm(one_ref[...], w_ref[place * own : (place + 1) * own, :], NN)
            grad = here if grad is None else grad + here
    n1g_ref[...] = grad.astype(BF16)
    unit, _ = norm_stats(x_ref[...].astype(F32))
    gather_rows(sum_ref, pl.program_id(0) == 0, grad * unit, grad)


def attend_far_back(table, q, k, v, ctx, grad, lse, x, own_grads, own_wt, far_wt):
    starts, grains, codes = table
    tokens, d = x.shape
    own = q.shape[1]
    sequences, _, length = codes.shape
    tall, high = rows(length, own), rows(length, d)
    lse_spec = pl.BlockSpec((length // QB, 8, 2 * QB), lambda s, *ids: (s, 0, 0))
    return call(
        far_back_kernel, "attend_far_back", (sequences,),
        [codes_spec(codes)] + [tall] * 5 + [lse_spec, high] + [tall] * 3 + [projections(own_wt)] * 2,
        [(high, (tokens, d), BF16), (whole((2, d)), (2, d), F32)],
        (starts, grains, codes, q, k, v, ctx, grad, lse, x, *own_grads, own_wt, far_wt),
        scratch=[pltpu.VMEM((length, own), F32)] * 2
        + [pltpu.VMEM((length, QB), jnp.int32)] + [pltpu.VMEM((length, own), BF16)] * 3, prefetch=2, cover=True,
    )


def reversed_bits(value, count):
    return sum(((value >> i) & 1) << (count - 1 - i) for i in range(count))


def chunk_order(size, bits):
    inner = range(size // 2)
    spread = lambda low, at: sum(((low >> (len(bits) - 2 - i)) & 1) << bit for i, bit in enumerate(bits[1:])) | at << bits[0]
    return [[spread(low, at) for low in inner] for at in (0, 1)]


def split_chunks(half, order, terms, keep_ref, give_ref):
    piece = keep_ref.shape[1]

    def store(mine):
        for ref, devices in ((keep_ref, order[mine]), (give_ref, order[1 - mine])):
            for at, device in enumerate(devices):
                ref[at] = terms[device * piece : (device + 1) * piece, :].astype(BF16)

    for mine in (0, 1):
        pl.when(half == mine)(functools.partial(store, mine))


def merge_kernel(half_ref, keep_a_ref, got_a_ref, keep_b_ref, got_b_ref, keep_ref, give_ref):
    keep_ref[...] = (keep_a_ref[...].astype(F32) + got_a_ref[...].astype(F32)).astype(keep_ref.dtype)
    give_ref[...] = (keep_b_ref[...].astype(F32) + got_b_ref[...].astype(F32)).astype(BF16)


def merge(half, keep, got):
    count, piece, width = keep.shape
    block = (count // 2, piece, width)
    mine = pl.BlockSpec(block, lambda i, ref: (ref[0], 0, 0))
    other = pl.BlockSpec(block, lambda i, ref: (1 - ref[0], 0, 0))
    return call(
        merge_kernel, "merge", (1,), [mine, mine, other, other],
        [(whole(block), block, F32), (whole(block), block, BF16)], (half, keep, got, keep, got), prefetch=1,
    )


def last_sum_kernel(keep_ref, got_ref, *out):
    value = keep_ref[0].astype(F32) + got_ref[0].astype(F32)
    at = 0
    for ref in out:
        ref[...] = value[:, at : at + ref.shape[1]]
        at += ref.shape[1]


def last_sum(widths, keep, got):
    piece = keep.shape[1]
    return call(
        last_sum_kernel, "last_sum", (1,), [whole(keep.shape)] * 2,
        [(whole((piece, width)), (piece, width), F32) for width in widths], (keep, got),
    )


def gelu_parts(z):
    spread = jnp.exp2(z * z * (-0.5 * LOG2E))
    t = 1.0 / (1.0 + (0.3275911 * 0.7071067811865476) * jnp.abs(z))
    poly = t * (0.254829592 + t * (-0.284496736 + t * (1.421413741 + t * (-1.453152027 + t * 1.061405429))))
    tail = 0.5 * poly * spread
    return jnp.where(z >= 0, 1.0 - tail, tail), spread


def hidden_pair(z, hidden_grad):
    phi, spread = gelu_parts(z)
    return (z * phi).astype(BF16), hidden_grad * (phi + z * spread * 0.3989422804014327)


def upstream_kernel(cot_ref, up_ref, down_ref, out_ref, sum_ref, pack_ref):
    cot = cot_ref[...]
    out_ref[...] = mm(cot, down_ref[...], NT).astype(BF16)

    @pl.when(pl.program_id(0) == 0)
    def _():
        pack_ref[: up_ref.shape[0], :] = up_ref[...]
        pack_ref[up_ref.shape[0] :, :] = down_ref[...]

    gather_rows(sum_ref, pl.program_id(0) == 0, cot)


def upstream(cot, up, down):
    tokens, d = cot.shape
    f = down.shape[0]
    tile = tokens // 4
    return call(
        upstream_kernel, "upstream", (4,), [rows(tile, d), whole(up.shape), whole(down.shape)],
        [
            (rows(tile, f), (tokens, f), BF16),
            (whole((1, d)), (1, d), F32),
            (whole((d + f, d)), (d + f, d), BF16),
        ],
        (cot, up, down),
    )


def hidden_kernel(
    orders, x_ref, part_a_ref, part_b_ref, b_out_ref, gain_ref, bias_ref, up_ref, b_up_ref, cot_down_ref, *rest
):
    first = pl.program_id(0) == 0
    if orders:
        half_ref, cot_ref, rest_cot, rest = rest[0], rest[1], rest[2:3], rest[2:]
        earlier, rest = rest[1:-11], rest[-11:]
        up_keep_ref, up_give_ref, down_keep_ref, down_give_ref, up_acc, down_acc = rest[-6:]
        rest = rest[:-6]
    residual_ref, n2_ref, hidden_ref, upg_ref, sum_ref = rest[-5:]
    residual = (
        x_ref[...].astype(F32) + (part_a_ref[...].astype(F32) + part_b_ref[...].astype(F32)) + flat(b_out_ref)
    )
    residual_ref[...] = residual.astype(BF16)
    unit, _ = norm_stats(residual)
    normed = (unit * flat(gain_ref) + flat(bias_ref)).astype(BF16)
    n2_ref[...] = normed
    hidden, grad = hidden_pair(mm(normed, up_ref[...], NN) + flat(b_up_ref), cot_down_ref[...].astype(F32))
    up_grad = grad.astype(BF16)
    hidden_ref[...] = hidden
    upg_ref[...] = up_grad
    gather_rows(sum_ref, first, grad)
    if not orders:
        return

    @pl.when(first)
    def _():
        up_acc[...] = jnp.zeros_like(up_acc)
        down_acc[...] = jnp.zeros_like(down_acc)

    up_acc[...] += mm(normed, up_grad, TN)
    down_acc[...] += mm(cot_ref[...], hidden, TN)
    if earlier:
        n2_old, hidden_old, upg_old, cot_old = earlier[-3:] + rest_cot
        up_acc[...] += mm(n2_old[...], upg_old[...], TN)
        down_acc[...] += mm(cot_old[...], hidden_old[...], TN)

    @pl.when(pl.program_id(0) == pl.num_programs(0) - 1)
    def _():
        split_chunks(half_ref[0], orders[0], up_acc, up_keep_ref, up_give_ref)
        split_chunks(half_ref[1], orders[1], down_acc, down_keep_ref, down_give_ref)


def hidden_own(sequence, length, x, part_a, part_b, b_out, gain, bias, up, b_up, cot_down, carried=(), weights=()):
    tokens, d = x.shape
    f = up.shape[1]
    count = 4
    tile = length // count
    tall, wide = rows(tile, d, count * sequence), rows(tile, f, count * sequence)
    near = rows(tile, d)
    specs = [tall, near, near] + [whole((d,))] * 3 + [whole(up.shape), whole((f,)), wide]
    out = [(tall, (tokens, d), BF16)] * 2 + [(wide, (tokens, f), BF16)] * 2 + [(whole((1, f)), (1, f), F32)]
    args = [x, part_a, part_b, b_out, gain, bias, up, b_up, cot_down]
    orders, scratch, earlier = None, [], ()
    if weights:
        orders, halves, cot = weights
        half_count = len(orders[0][0])
        chunk = (half_count, d // (2 * half_count), f)
        specs += [pl.BlockSpec(memory_space=pltpu.SMEM), tall]
        args += [halves, cot]
        specs.append(rows(tile, d))
        args.append(cot)
        earlier = [pl.BlockSpec(memory_space=pl.ANY), rows(tile, d), rows(tile, f), rows(tile, f)]
        out += [(whole(chunk), chunk, BF16)] * 4
        scratch = [pltpu.VMEM((d, f), F32)] * 2
    return call(
        functools.partial(hidden_kernel, orders), "hidden_own", (count,), specs, out, args, scratch=scratch, carried=carried,
        carried_specs=earlier,
    )


def products_kernel(
    n2_ref, cot_ref, hidden_ref, upg_ref, up_a_ref, down_a_ref, far_ref, bias_ref, *rest
):
    mlp_ref, n2g_ref = rest[-2:]
    d = n2_ref.shape[1]
    up_b, down_b = far_ref[:d, :], far_ref[d:, :]
    bias = jnp.concatenate([bias_ref[at : at + 1, :] for at in range(2, bias_ref.shape[0])], 1)
    z = mm(n2_ref[...], up_b, NN) + bias
    hidden_grad = mm(cot_ref[...], down_b, NT)
    mlp_own = mm(hidden_ref[...], down_a_ref[...], NN)
    n2g_own = mm(upg_ref[...], up_a_ref[...], NT)
    hidden, grad = hidden_pair(z, hidden_grad)
    mlp_ref[...] = (mlp_own + mm(hidden, down_b, NN)).astype(BF16)
    n2g_ref[...] = (n2g_own + mm(grad.astype(BF16), up_b, NT)).astype(BF16)


def products(span, n2, cot, hidden, upg, up, down, far, bias, carried=()):
    tokens = n2.shape[0]
    d, f = up.shape
    first, count = span
    tall, wide = rows(TILE, d, first), rows(TILE, f, first)
    return call(
        products_kernel, "feed_forward", (count,),
        [tall, tall, wide, wide, whole(up.shape), whole(down.shape), whole(far.shape), whole(bias.shape)],
        [(tall, (tokens, d), BF16), (rows(TILE, d), (count * TILE, d), BF16)],
        (n2, cot, hidden, upg, up, down, far, bias), carried=carried, cover=True,
    )


def middle_kernel(residual_ref, grad_a_ref, grad_b_ref, cot_ref, gain_ref, own_w_ref, far_w_ref, *rest):
    agrad_ref, own_cg_ref, far_cg_ref, sum_ref = rest[-4:]
    unit, scale = norm_stats(residual_ref[...].astype(F32))
    summed = grad_a_ref[...].astype(F32) + grad_b_ref[...].astype(F32)
    rgrad = cot_ref[...].astype(F32) + norm_back(unit, scale, summed * flat(gain_ref))
    agrad = rgrad.astype(BF16)
    agrad_ref[...] = agrad
    own_cg_ref[...] = mm(agrad, own_w_ref[...], NT).astype(BF16)
    far_cg_ref[...] = mm(agrad, far_w_ref[...], NT).astype(BF16)
    gather_rows(sum_ref, pl.program_id(0) == 0, rgrad, summed * unit, summed)


def middle(span, residual, grad_a, grad_b, cot, gain, own_w, far_w, carried=()):
    tokens, d = residual.shape
    own = own_w.shape[0] // 4
    first, count = span
    tile = TILE // 2
    tall, slim, near = rows(tile, d, 2 * first), rows(tile, own, 2 * first), rows(tile, d)
    return call(
        middle_kernel, "second_norm_back", (2 * count,),
        [tall, near, near, tall, whole((d,)), out_weights(own_w), out_weights(far_w)],
        [(tall, (tokens, d), BF16)] + [(slim, (tokens, own), BF16)] * 2 + [(whole((3, d)), (3, d), F32)],
        (residual, grad_a, grad_b, cot, gain, own_w, far_w), carried=carried,
    )


def output_kernel(residual_ref, mlp_a_ref, mlp_b_ref, b_down_ref, out_ref):
    out_ref[...] = (
        residual_ref[...].astype(F32)
        + ((mlp_a_ref[...].astype(F32) + mlp_b_ref[...].astype(F32)) + flat(b_down_ref))
    ).astype(BF16)


def output(residual, mlp_a, mlp_b, b_down):
    tokens, d = residual.shape
    tall = rows(TILE, d)
    return call(
        output_kernel, "block_output", (tokens // TILE,), [tall] * 3 + [whole((d,))],
        [(tall, (tokens, d), BF16)], (residual, mlp_a, mlp_b, b_down), cover=True,
    )[0]


def first_back_kernel(x_ref, grad_a_ref, grad_b_ref, rgrad_ref, gain_ref, *rest):
    unit, scale = norm_stats(x_ref[...].astype(F32))
    upstream = (grad_a_ref[...].astype(F32) + grad_b_ref[...].astype(F32)) * flat(gain_ref)
    rest[-1][...] = rgrad_ref[...].astype(F32) + norm_back(unit, scale, upstream)


def first_back(span, x, grad_a, grad_b, rgrad, gain, carried=()):
    tokens, d = x.shape
    first, count = span
    tall = rows(TILE, d, first)
    return call(
        first_back_kernel, "first_norm_back", (count,), [tall] * 4 + [whole((d,))],
        [(tall, (tokens, d), F32)], (x, grad_a, grad_b, rgrad, gain), carried=carried,
    )


def swap(value, axis, size, bit):
    got = lax.ppermute(value, axis, [(i, i ^ bit) for i in range(size)])
    return got


def tie(value, *others):
    return lax.optimization_barrier((value,) + others)[0]


class ScatterSum:
    def __init__(self, keep, give, size, bits):
        self.keep, self.give, self.size, self.bits = keep, give, size, list(bits)
        self.me = lax.axis_index("dp")

    def begin(self):
        self.got = swap(self.give, "dp", self.size, 1 << self.bits.pop(0))

    def end(self, *others):
        got = tie(self.got, *others) if others else self.got
        if self.bits:
            mine = ((self.me >> self.bits[0]) & 1).astype(jnp.int32).reshape(1)
            self.keep, self.give = merge(mine, self.keep, got)
        else:
            self.got = got
        return got

    def finish(self, *widths):
        while self.bits:
            self.begin()
            self.end()
        return last_sum(widths, self.keep, self.got)


def body(
    n_dp,
    n_mp,
    block_input,
    segment_ids,
    group_ids,
    padding,
    ln1_gain,
    ln1_bias,
    w_qkv,
    b_qv,
    w_out,
    b_out,
    ln2_gain,
    ln2_bias,
    w_up,
    b_up,
    w_down,
    b_down,
    cotangent,
):
    tokens, d = block_input.shape
    sequences, length = segment_ids.shape
    own = w_qkv.shape[2]
    far = lambda value: swap(value, "mp", n_mp, 2)
    near = lambda value: swap(value, "mp", n_mp, 1)
    levels = n_dp.bit_length() - 1
    bits = list(range(levels))
    other_bits = [1, 0] + bits[2:]
    me = lax.axis_index("dp").astype(jnp.int32)
    halves = jnp.stack([me & 1, (me >> 1) & 1])
    orders = (chunk_order(n_dp, bits), chunk_order(n_dp, other_bits))

    pack = jnp.concatenate([jnp.transpose(w_qkv, (1, 2, 0)).reshape(3 * own, d), w_out], 0)
    pack_far = far(pack)
    small_far = far(jnp.concatenate([b_qv, b_up.reshape(-1, own)], 0))
    table = tables(segment_ids, group_ids, padding)

    *saved_own, n1 = attend_own(table, block_input, ln1_gain, ln1_bias, pack, b_qv)
    ctx_own = saved_own[3]
    cot_down, sum_cot, mlp_own = upstream(tie(cotangent, n1, small_far), w_up, w_down)
    mlp_far = far(mlp_own)
    parts, saved_far = [], ()
    for s in range(sequences):
        *saved_far, part = attend_far(s, table, n1, tie(pack_far, cot_down), small_far, ctx_own, pack, saved_far)
        parts.append((part, near(part)))
    carried, sums_up = (), []
    for s, (part, other) in enumerate(parts):
        other = tie(other, carried[0] if carried else parts[-1][0])
        weights = (orders, halves, cotangent) if s == sequences - 1 else ()
        *carried, = hidden_own(
            s, length, block_input, part, other, b_out, ln2_gain, ln2_bias, w_up, b_up, cot_down, carried[:4], weights
        )
        sums_up.append(carried[4])
    residual, n2, hidden, upg, _, up_keep, up_give, down_keep, down_give = carried
    sum_w_up = ScatterSum(up_keep, up_give, n_dp, bits)
    sum_w_down = ScatterSum(down_keep, down_give, n_dp, other_bits)
    sum_w_up.begin()
    sum_w_down.begin()
    mlp_far = tie(mlp_far, up_keep)
    tiles = tokens // TILE
    shares, mlp, gate = [], (), (up_keep,)
    for span in ((0, tiles - 1), (tiles - 1, 1)):
        *mlp, n2g = products(
            span, tie(n2, *gate), cotangent, hidden, upg, w_up, w_down, mlp_far, small_far, mlp
        )
        shares.append((span, n2g, near(n2g)))
        if len(shares) == 1:
            gate = (sum_w_up.end(n2g), sum_w_down.end(n2g))
            sum_w_up.begin()
            sum_w_down.begin()
    gate, carried, sums_mid = (n2g,), (), []
    for span, n2g, other in shares:
        other = tie(other, *gate)
        *carried, sum_mid = middle(span, residual, n2g, other, cotangent, ln2_gain, pack, pack_far, carried)
        sums_mid.append(sum_mid)
        if len(sums_mid) == 1:
            gate = (carried[0], sum_w_up.end(sum_mid), sum_w_down.end(sum_mid))
            sum_w_up.begin()
            sum_w_down.begin()
    agrad, cgrad_own, cgrad_far = carried
    q, k, v, ctx, lse = saved_own
    *own_grads, keep, give, sum_qv = attend_own_back(
        table, halves[:1], orders[0], q, k, v, ctx, cgrad_own, lse, n1, agrad
    )
    mlp_near = near(mlp[0])
    sum_attn = ScatterSum(keep, give, n_dp, bits)
    sum_attn.begin()
    got = (sum_w_up.end(keep), sum_w_down.end(keep))
    up_sum, = sum_w_up.finish(up_keep.shape[2])
    down_sum, = sum_w_down.finish(up_keep.shape[2])
    q, k, v, ctx, lse = saved_far
    n1g, sum_first = attend_far_back(
        table, q, k, v, ctx, tie(cgrad_far, keep, *got), lse, block_input, own_grads, pack, pack_far
    )
    sum_first = sum_first + near(sum_first)
    n1g_near = near(tie(n1g, sum_first))
    got = sum_attn.end(n1g)
    sum_attn.begin()
    add = lambda values: functools.reduce(jnp.add, values)
    wide_qv = jnp.concatenate([sum_qv.reshape(1, -1), jnp.zeros((1, d - 2 * own), F32)], 1)
    sums = jnp.concatenate([sum_first, add(sums_mid), sum_cot, add(sums_up), wide_qv], 0)
    other = swap(sums, "dp", n_dp, 1)
    block_output = output(tie(residual, n1g, got, sums), mlp[0], mlp_near, b_down)
    sums = sums + tie(other, block_output)
    other = swap(sums, "dp", n_dp, 2)
    got = sum_attn.end(block_output, sums)
    sum_attn.begin()
    outputs = first_back((0, tiles - 1), block_input, n1g, tie(n1g_near, block_output, got, sums), agrad, ln1_gain)
    sums = sums + tie(other, *outputs)
    if levels > 2:
        other = swap(sums, "dp", n_dp, 4)
    got = sum_attn.end(*outputs)
    qkv_sum, out_sum = sum_attn.finish(3 * own, own)
    input_grad, = first_back((tiles - 1, 1), block_input, n1g, tie(n1g_near, sums, qkv_sum), agrad, ln1_gain, outputs)
    if levels > 2:
        sums = sums + tie(other, input_grad)
    for bit in range(3, levels):
        sums = sums + swap(sums, "dp", n_dp, 1 << bit)

    piece, tiny = d // n_dp, own // n_dp
    mine = lax.dynamic_slice(sums, (0, me * piece), (sums.shape[0] - 1, piece))
    vectors = [mine[i] for i in range(7)]
    return (
        block_output,
        input_grad,
        vectors[0],
        vectors[1],
        qkv_sum.reshape(piece, 3, own),
        lax.dynamic_slice(sums[7, : 2 * own].reshape(2, own), (0, me * tiny), (2, tiny)),
        out_sum.T,
        vectors[2],
        vectors[3],
        vectors[4],
        up_sum,
        vectors[6],
        down_sum.T,
        vectors[5],
    )


def solution(mesh):
    return jax.shard_map(
        functools.partial(body, mesh.shape["dp"], mesh.shape["mp"]),
        mesh=mesh,
        in_specs=(
            P("dp", None),
            P("dp", None),
            P("dp", None),
            P("dp", None),
            P(),
            P(),
            P(None, None, "mp"),
            P(None, "mp"),
            P("mp", None),
            P(),
            P(),
            P(),
            P(None, "mp"),
            P("mp"),
            P("mp", None),
            P(),
            P("dp", None),
        ),
        out_specs=(
            P("dp", None),
            P("dp", None),
            P("dp"),
            P("dp"),
            P("dp", None, "mp"),
            P(None, ("mp", "dp")),
            P("mp", "dp"),
            P("dp"),
            P("dp"),
            P("dp"),
            P("dp", "mp"),
            P(("mp", "dp")),
            P("mp", "dp"),
            P("dp"),
        ),
        check_vma=False,
    )
```

```python
import functools

import jax
import jax.numpy as jnp
from jax import lax
from jax.experimental import pallas as pl
from jax.experimental.pallas import tpu as pltpu
from jax.sharding import PartitionSpec as P

HD = 64
QB = 128
GRAIN = 64
GRAIN_BITS = 6
LONGEST = 256
FREE = dict(
    masks=(), attend_own=(), attend_far=(), attend_own_back=(7, 10), attend_far_back=(6, 9, 10, 11), upstream=(),
    hidden_own=(1, 2, 8), feed_forward=(4, 5, 6), second_norm_back=(1, 2), block_output=(), first_norm_back=(1, 2),
    merge=range(99), last_sum=range(99),
)
GRANTS = dict(
    masks=4, attend_own=20, attend_far=14, attend_own_back=28, attend_far_back=34, upstream=12, hidden_own=34,
    feed_forward=20, second_norm_back=10, block_output=8, first_norm_back=14, merge=6, last_sum=4,
)
TILE = 512
COVER = 10**12
MASKED = -1e30
EPS = 1e-05
LOG2E = 1.4426950408889634
F32 = jnp.float32
BF16 = jnp.bfloat16
NT = (((1,), (1,)), ((), ()))
NN = (((1,), (0,)), ((), ()))
TN = (((0,), (0,)), ((), ()))


def mm(a, b, dims):
    return lax.dot_general(a, b, dims, preferred_element_type=F32)


def flat(ref):
    return ref[...].reshape(1, -1)


def call(kernel, name, grid, in_specs, out, args, scratch=(), prefetch=0, carried=(), cover=False, carried_specs=()):
    args = [
        arg if at < prefetch or arg.size < 1 << 17 or at in FREE[name] else pltpu.with_memory_space_constraint(arg, pltpu.HBM)
        for at, arg in enumerate(args)
    ]
    return pl.pallas_call(
        kernel,
        grid_spec=pltpu.PrefetchScalarGridSpec(
            num_scalar_prefetch=prefetch,
            grid=grid,
            in_specs=list(in_specs) + list(carried_specs or [pl.BlockSpec(memory_space=pl.ANY)] * len(carried)),
            out_specs=[entry[0] for entry in out],
            scratch_shapes=list(scratch),
        ),
        out_shape=[pltpu.HBM(*entry[1:3]) if entry[3:] else jax.ShapeDtypeStruct(*entry[1:3]) for entry in out],
        input_output_aliases={len(args) + i: i for i in range(len(carried))},
        compiler_params=pltpu.CompilerParams(vmem_limit_bytes=GRANTS[name] * 1024 * 1024),
        cost_estimate=pl.CostEstimate(flops=COVER if cover else 0, bytes_accessed=1024, transcendentals=0),
        name=name,
    )(*args, *carried)


def whole(shape):
    return pl.BlockSpec(shape, lambda *ids: (0,) * len(shape))


def rows(tile, width, skip=0):
    return pl.BlockSpec((tile, width), lambda i, *rest: (i + skip, 0))


def norm_stats(values):
    average = jnp.mean(values, -1, keepdims=True)
    centered = values - average
    variance = jnp.mean(centered * centered, -1, keepdims=True)
    scale = lax.rsqrt(variance + EPS)
    return centered * scale, scale


def norm_back(unit, scale, upstream):
    first = jnp.mean(upstream, -1, keepdims=True)
    second = jnp.mean(upstream * unit, -1, keepdims=True)
    return scale * (upstream - first - unit * second)


def total(values):
    return jnp.sum(values.astype(F32), 0, keepdims=True)


def gather_rows(ref, first, *values):
    @pl.when(first)
    def _():
        ref[...] = jnp.zeros_like(ref)

    for at, value in enumerate(values):
        ref[at : at + 1, :] += total(value)


def masks_kernel(segment_ref, group_ref, padding_ref, bounds_ref, code_ref):
    sequences, length = segment_ref.shape
    blocks = length // QB
    low = segment_ref[...] * 4
    high = low + group_ref[...]
    codes = jnp.where(padding_ref[...] == 0, high, -1)
    place = lax.broadcasted_iota(jnp.int32, (1, sequences * blocks), 1)
    key_from = jnp.zeros((1, sequences * blocks), jnp.int32)
    key_to = jnp.zeros((1, sequences * blocks), jnp.int32)
    for s in range(sequences):
        for at, rows_of in enumerate((codes, low, high)):
            code_ref[s, at : at + 1, :] = rows_of[s : s + 1, :]
        row = segment_ref[s : s + 1, :]
        for block in range(blocks):
            earliest = row[:, block * QB : block * QB + 1]
            latest = row[:, (block + 1) * QB - 1 : (block + 1) * QB]
            before = jnp.sum((row < earliest).astype(F32), 1, keepdims=True).astype(jnp.int32)
            until = jnp.sum((row <= latest).astype(F32), 1, keepdims=True).astype(jnp.int32)
            here = place == s * blocks + block
            key_from = jnp.where(here, before, key_from)
            key_to = jnp.where(here, until, key_to)
    key_from = key_from & -16
    grains = jnp.maximum((key_to - key_from + (GRAIN - 1)) >> GRAIN_BITS, QB // GRAIN)
    bounds_ref[0:1, :] = jnp.minimum(key_from, length - grains * GRAIN)
    bounds_ref[1:2, :] = grains


def tables(segment_ids, group_ids, padding):
    sequences, length = segment_ids.shape
    bounds = (2, sequences * (length // QB))
    codes = (sequences, 3, length)
    return call(
        masks_kernel, "masks", (1,), [whole(segment_ids.shape)] * 3,
        [(whole(bounds), bounds, jnp.int32), (whole(codes), codes, jnp.int32)], (segment_ids, group_ids, padding),
    )


def extents(length):
    return range(QB // GRAIN, min(QB + 2 * LONGEST, length) // GRAIN + 1)


def head_groups(width):
    return [slice(at, min(at + 2 * HD, width)) for at in range(0, width, 2 * HD)]


def stack_heads(values):
    if values.shape[1] == HD:
        return values
    lane = lax.broadcasted_iota(jnp.int32, values.shape, 1)
    zero = jnp.zeros_like(values)
    return jnp.concatenate(
        [jnp.where(lane < HD, values, zero), jnp.where(lane >= HD, values, zero)], 0
    )


def join_heads(values):
    if values.shape[1] == HD:
        return values
    lane = lax.broadcasted_iota(jnp.int32, (QB, 2 * HD), 1)
    return jnp.where(lane < HD, values[:QB], values[QB:])


def spread_codes(code_ref, column_ref):
    for at in range(0, column_ref.shape[0], QB):
        column_ref[at : at + QB, :] = jnp.broadcast_to(code_ref[0:1, at : at + QB], (QB, QB)).T


def mask_bias(column_ref, code_ref, start, extent, block):
    mine = pl.ds(pl.multiple_of(block * QB, QB), QB)
    codes = column_ref[pl.ds(start, extent), :]
    shape = (extent, QB)
    apart = lax.broadcasted_iota(jnp.int32, shape, 0) - lax.broadcasted_iota(jnp.int32, shape, 1)
    allowed = ((codes >= code_ref[1:2, mine]) & (codes <= code_ref[2:3, mine])) | (
        apart == block * QB - start
    )
    return jnp.where(allowed, jnp.float32(0), jnp.float32(MASKED))


def widen(bias, cols):
    return jnp.concatenate([bias, bias], 1) if cols.stop - cols.start > HD else bias


def each_block(bound_ref, length, group, sequence, run):
    turns = length // QB // group

    def step(turn, carry):
        place = (sequence * turns + turn) * group
        grains = functools.reduce(jnp.maximum, [bound_ref[1, place + i] for i in range(group)])
        starts = [
            pl.multiple_of(jnp.minimum(bound_ref[0, place + i], length - grains * GRAIN), 16) for i in range(group)
        ]
        blocks = [turn * group + i for i in range(group)]
        for extent in extents(length):
            pl.when(grains == extent)(functools.partial(run, extent * GRAIN, blocks, starts))
        return carry

    lax.fori_loop(0, turns, step, 0)


def project(normed, wt_ref, q_bias, v_bias, q_ref, k_ref, v_ref):
    own = q_ref.shape[1]
    q_ref[...] = (mm(normed, wt_ref[:own, :], NT) + q_bias).astype(BF16)
    k_ref[...] = mm(normed, wt_ref[own : 2 * own, :], NT).astype(BF16)
    v_ref[...] = (mm(normed, wt_ref[2 * own :, :], NT) + v_bias).astype(BF16)


def attend(sequence, bound_ref, code_ref, column_ref, q_ref, k_ref, v_ref, ctx_ref, lse_ref):
    length, width = q_ref.shape
    heads = head_groups(width)
    spread_codes(code_ref, column_ref)

    def run(extent, blocks, starts):
        units, scores, probs, totals, biases = [], [], [], [], []
        for i, (block, start) in enumerate(zip(blocks, starts)):
            here = pl.ds(start, extent)
            mine = pl.ds(pl.multiple_of(block * QB, QB), QB)
            for p, cols in enumerate(heads):
                units.append((i, block, here, mine, p, cols))
                scores.append(mm(k_ref[here, cols], stack_heads(q_ref[mine, cols]), NT))
            biases.append(mask_bias(column_ref, code_ref, start, extent, block))
        for (i, block, here, mine, p, cols), score in zip(units, scores):
            score = score * (0.125 * LOG2E) + widen(biases[i], cols)
            top = jnp.max(score, 0, keepdims=True)
            weights = jnp.exp2(score - top)
            summed = jnp.sum(weights, 0, keepdims=True)
            lse_ref[block, p : p + 1, : score.shape[1]] = top + jnp.log2(summed)
            totals.append(1.0 / summed)
            probs.append(weights.astype(BF16))
        for (i, block, here, mine, p, cols), prob, scale in zip(units, probs, totals):
            turned = v_ref[here, cols].T
            both = [
                mm(turned[at * HD : (at + 1) * HD], prob[:, at * QB : (at + 1) * QB], NN)
                * scale[:, at * QB : (at + 1) * QB]
                for at in range(prob.shape[1] // QB)
            ]
            ctx_ref[mine, cols] = jnp.concatenate(both, 0).T.astype(BF16)

    each_block(bound_ref, length, 2, sequence, run)


def own_kernel(
    bound_ref, code_ref, x_ref, gain_ref, bias_ref, wt_ref, qv_ref,
    q_ref, k_ref, v_ref, ctx_ref, lse_ref, n1_ref, column_ref,
):
    unit, _ = norm_stats(x_ref[...].astype(F32))
    normed = (unit * flat(gain_ref) + flat(bias_ref)).astype(BF16)
    n1_ref[...] = normed
    project(normed, wt_ref, qv_ref[0:1, :], qv_ref[1:2, :], q_ref, k_ref, v_ref)
    attend(pl.program_id(0), bound_ref, code_ref, column_ref, q_ref, k_ref, v_ref, ctx_ref, lse_ref)


def attention_outs(tokens, width, length, sequences, skip=0):
    tall = rows(length, width, skip)
    lse = (length // QB, 8, 2 * QB)
    return [(tall, (tokens, width), BF16, True)] * 4 + [
        (pl.BlockSpec(lse, lambda s, *ids: (s + skip, 0, 0)), (sequences * lse[0],) + lse[1:], F32, True)
    ]


def projections(pack):
    return pl.BlockSpec((pack.shape[1] // 4 * 3, pack.shape[1]), lambda *ids: (0, 0))


def out_weights(pack):
    return pl.BlockSpec((pack.shape[1] // 4, pack.shape[1]), lambda *ids: (3, 0))


def biases(pack):
    return pl.BlockSpec((16, pack.shape[1]), lambda *ids: (pack.shape[1] // 16, 0))


def bias_of(ref, which):
    part = [ref[3 * which + at : 3 * which + at + 1, :].astype(F32) for at in range(3)]
    return part[0] + (part[1] + part[2])


def codes_spec(codes, skip=0):
    return pl.BlockSpec((None,) + codes.shape[1:], lambda s, *ids: (s + skip, 0, 0))


def attend_own(table, x, gain, bias, wt, b_qv):
    bounds, codes = table
    tokens, d = x.shape
    sequences, _, length = codes.shape
    return call(
        own_kernel, "attend_own", (sequences,),
        [codes_spec(codes), rows(length, d), whole(gain.shape), whole(bias.shape), projections(wt), whole(b_qv.shape)],
        attention_outs(tokens, b_qv.shape[1], length, sequences) + [(rows(length, d), (tokens, d), BF16, True)],
        (bounds, codes, x, gain, bias, wt, b_qv),
        scratch=[pltpu.VMEM((length, QB), jnp.int32)], prefetch=1,
    )


def far_kernel(
    sequence, bound_ref, code_ref, n1_ref, wt_ref, bias_ref, own_ctx_ref, own_w_ref, far_w_ref, *rest
):
    q_ref, k_ref, v_ref, ctx_ref, lse_ref, part_ref, column_ref = rest[-7:]
    bias = bias_of(bias_ref, 1)
    own = q_ref.shape[1]
    project(n1_ref[...], wt_ref, bias[:, :own], bias[:, own : 2 * own], q_ref, k_ref, v_ref)
    attend(sequence, bound_ref, code_ref, column_ref, q_ref, k_ref, v_ref, ctx_ref, lse_ref)
    part_ref[...] = (
        mm(own_ctx_ref[...], own_w_ref[...], NN) + mm(ctx_ref[...], far_w_ref[...], NN)
    ).astype(BF16)


def attend_far(sequence, table, n1, far, own_ctx, pack, carried=()):
    bounds, codes = table
    tokens, d = n1.shape
    sequences, _, length = codes.shape
    own = own_ctx.shape[1]
    return call(
        functools.partial(far_kernel, sequence), "attend_far", (1,),
        [codes_spec(codes, sequence), rows(length, d, sequence), projections(far), biases(far)]
        + [rows(length, own, sequence), out_weights(pack), out_weights(far)],
        attention_outs(tokens, own, length, sequences, sequence) + [(rows(length, d), (length, d), BF16)],
        (bounds, codes, n1, far, far, own_ctx, pack, far),
        scratch=[pltpu.VMEM((length, QB), jnp.int32)], prefetch=1, carried=carried,
    )


def attend_back(
    bound_ref, code_ref, column_ref, q_ref, k_ref, v_ref, ctx_ref, grad_ref, lse_ref,
    dq_ref, dk_ref, dv_ref, dk_acc, dv_acc,
):
    length, width = q_ref.shape
    heads = head_groups(width)
    spread_codes(code_ref, column_ref)
    dk_acc[...] = jnp.zeros_like(dk_acc)
    dv_acc[...] = jnp.zeros_like(dv_acc)

    def run(extent, blocks, starts):
        units, stacked, upstream, scores, grads, biases = [], [], [], [], [], []
        for i, (block, start) in enumerate(zip(blocks, starts)):
            here = pl.ds(start, extent)
            mine = pl.ds(pl.multiple_of(block * QB, QB), QB)
            for p, cols in enumerate(heads):
                units.append((i, block, here, mine, p, cols))
                stacked.append(stack_heads(q_ref[mine, cols]))
                upstream.append(stack_heads(grad_ref[mine, cols]))
                scores.append(mm(k_ref[here, cols], stacked[-1], NT))
                grads.append(mm(v_ref[here, cols], upstream[-1], NT))
            biases.append(mask_bias(column_ref, code_ref, start, extent, block))
        probs, score_grads = [], []
        for (i, block, here, mine, p, cols), score, grad in zip(units, scores, grads):
            turned = (ctx_ref[mine, cols].astype(F32) * grad_ref[mine, cols].astype(F32)).T
            delta = jnp.concatenate(
                [
                    jnp.sum(turned[at : at + HD], 0, keepdims=True)
                    for at in range(0, turned.shape[0], HD)
                ],
                1,
            )
            weights = jnp.exp2(
                score * (0.125 * LOG2E) + widen(biases[i], cols) - lse_ref[block, p : p + 1, : score.shape[1]]
            )
            probs.append(weights.astype(BF16))
            score_grads.append((weights * (grad - delta)).astype(BF16))
        for n, (i, block, here, mine, p, cols) in enumerate(units):
            dv_acc[here, cols] += mm(probs[n], upstream[n], NN)
            dk_acc[here, cols] += mm(score_grads[n], stacked[n], NN)
            dq = join_heads(mm(score_grads[n], k_ref[here, cols], TN))
            dq_ref[mine, cols] = (dq * 0.125).astype(BF16)

    each_block(bound_ref, length, 1, pl.program_id(0), run)
    dk_ref[...] = (dk_acc[...] * 0.125).astype(BF16)
    dv_ref[...] = dv_acc[...].astype(BF16)


def own_back_kernel(
    order, bound_ref, half_ref, code_ref, q_ref, k_ref, v_ref, ctx_ref, grad_ref, lse_ref, n1_ref, agrad_ref,
    dq_ref, dk_ref, dv_ref, keep_ref, give_ref, sum_ref, dk_acc, dv_acc, column_ref, weight_acc,
):
    attend_back(
        bound_ref, code_ref, column_ref, q_ref, k_ref, v_ref, ctx_ref, grad_ref, lse_ref,
        dq_ref, dk_ref, dv_ref, dk_acc, dv_acc,
    )
    first = pl.program_id(0) == 0

    @pl.when(first)
    def _():
        weight_acc[...] = jnp.zeros_like(weight_acc)
        sum_ref[...] = jnp.zeros_like(sum_ref)

    own = dq_ref.shape[1]
    normed = n1_ref[...]
    for at, grad in enumerate((dq_ref, dk_ref, dv_ref)):
        weight_acc[:, at * own : (at + 1) * own] += mm(normed, grad[...], TN)
    weight_acc[:, 3 * own :] += mm(agrad_ref[...], ctx_ref[...], TN)
    sum_ref[0:1, :] += total(dq_ref[...])
    sum_ref[1:2, :] += total(dv_ref[...])

    @pl.when(pl.program_id(0) == pl.num_programs(0) - 1)
    def _():
        split_chunks(half_ref[0], order, weight_acc, keep_ref, give_ref)


def attend_own_back(table, half, order, q, k, v, ctx, grad, lse, n1, agrad):
    bounds, codes = table
    tokens, d = n1.shape
    own = q.shape[1]
    sequences, _, length = codes.shape
    tall, high = rows(length, own), rows(length, d)
    lse_spec = pl.BlockSpec((length // QB, 8, 2 * QB), lambda s, *ids: (s, 0, 0))
    count = len(order[0])
    chunk = (count, d // (2 * count), 4 * own)
    return call(
        functools.partial(own_back_kernel, order), "attend_own_back", (sequences,),
        [codes_spec(codes)] + [tall] * 5 + [lse_spec, high, high],
        [(tall, (tokens, own), BF16)] * 3 + [(whole(chunk), chunk, BF16)] * 2 + [(whole((2, own)), (2, own), F32)],
        (bounds, half, codes, q, k, v, ctx, grad, lse, n1, agrad),
        scratch=[pltpu.VMEM((length, own), F32)] * 2
        + [pltpu.VMEM((length, QB), jnp.int32), pltpu.VMEM((d, 4 * own), F32)], prefetch=2, cover=True,
    )


def far_back_kernel(
    bound_ref, code_ref, q_ref, k_ref, v_ref, ctx_ref, grad_ref, lse_ref,
    x_ref, aq_ref, ak_ref, av_ref, wa_ref, wb_ref,
    n1g_ref, sum_ref, dk_acc, dv_acc, column_ref, dq_ref, dk_ref, dv_ref,
):
    attend_back(
        bound_ref, code_ref, column_ref, q_ref, k_ref, v_ref, ctx_ref, grad_ref, lse_ref,
        dq_ref, dk_ref, dv_ref, dk_acc, dv_acc,
    )
    own = aq_ref.shape[1]
    grad = None
    for w_ref, grads in ((wa_ref, (aq_ref, ak_ref, av_ref)), (wb_ref, (dq_ref, dk_ref, dv_ref))):
        for place, one_ref in enumerate(grads):
            here = mm(one_ref[...], w_ref[place * own : (place + 1) * own, :], NN)
            grad = here if grad is None else grad + here
    n1g_ref[...] = grad.astype(BF16)
    unit, _ = norm_stats(x_ref[...].astype(F32))
    gather_rows(sum_ref, pl.program_id(0) == 0, grad * unit, grad)


def attend_far_back(table, q, k, v, ctx, grad, lse, x, own_grads, own_wt, far_wt):
    bounds, codes = table
    tokens, d = x.shape
    own = q.shape[1]
    sequences, _, length = codes.shape
    tall, high = rows(length, own), rows(length, d)
    lse_spec = pl.BlockSpec((length // QB, 8, 2 * QB), lambda s, *ids: (s, 0, 0))
    return call(
        far_back_kernel, "attend_far_back", (sequences,),
        [codes_spec(codes)] + [tall] * 5 + [lse_spec, high] + [tall] * 3 + [projections(own_wt)] * 2,
        [(high, (tokens, d), BF16), (whole((2, d)), (2, d), F32)],
        (bounds, codes, q, k, v, ctx, grad, lse, x, *own_grads, own_wt, far_wt),
        scratch=[pltpu.VMEM((length, own), F32)] * 2
        + [pltpu.VMEM((length, QB), jnp.int32)] + [pltpu.VMEM((length, own), BF16)] * 3, prefetch=1, cover=True,
    )


def reversed_bits(value, count):
    return sum(((value >> i) & 1) << (count - 1 - i) for i in range(count))


def chunk_order(size, bits):
    inner = range(size // 2)
    spread = lambda low, at: sum(((low >> (len(bits) - 2 - i)) & 1) << bit for i, bit in enumerate(bits[1:])) | at << bits[0]
    return [[spread(low, at) for low in inner] for at in (0, 1)]


def split_chunks(half, order, terms, keep_ref, give_ref):
    piece = keep_ref.shape[1]

    def store(mine):
        for ref, devices in ((keep_ref, order[mine]), (give_ref, order[1 - mine])):
            for at, device in enumerate(devices):
                ref[at] = terms[device * piece : (device + 1) * piece, :].astype(BF16)

    for mine in (0, 1):
        pl.when(half == mine)(functools.partial(store, mine))


def merge_kernel(half_ref, *refs):
    count = len(refs) // 6
    for chain in range(count):
        keep_a, got_a, keep_b, got_b = refs[4 * chain : 4 * chain + 4]
        keep_ref, give_ref = refs[4 * count + 2 * chain :][:2]
        keep_ref[...] = keep_a[...].astype(F32) + got_a[...].astype(F32)
        give_ref[...] = (keep_b[...].astype(F32) + got_b[...].astype(F32)).astype(BF16)


def merge(halves, pairs):
    specs, out, args = [], [], []
    for chain, (keep, got) in enumerate(pairs):
        count, piece, width = keep.shape
        block = (count // 2, piece, width)
        specs += [pl.BlockSpec(block, lambda i, ref, chain=chain: (ref[chain], 0, 0))] * 2
        specs += [pl.BlockSpec(block, lambda i, ref, chain=chain: (1 - ref[chain], 0, 0))] * 2
        out += [(whole(block), block, F32), (whole(block), block, BF16)]
        args += [keep, got, keep, got]
    got = call(merge_kernel, "merge", (1,), specs, out, (halves, *args), prefetch=1)
    return [got[2 * chain : 2 * chain + 2] for chain in range(len(pairs))]


def last_sum_kernel(count, *refs):
    out = refs[2 * count :]
    for chain in range(count):
        value = refs[2 * chain][0].astype(F32) + refs[2 * chain + 1][0].astype(F32)
        at = 0
        while at < value.shape[1]:
            out[0][...] = value[:, at : at + out[0].shape[1]]
            at += out[0].shape[1]
            out = out[1:]


def last_sum(pairs, widths):
    piece = pairs[0][0].shape[1]
    return call(
        functools.partial(last_sum_kernel, len(pairs)), "last_sum", (1,),
        [whole(keep.shape) for keep, _ in pairs for _ in range(2)],
        [(whole((piece, width)), (piece, width), F32) for width in widths], [one for pair in pairs for one in pair],
    )


def gelu_parts(z):
    spread = jnp.exp2(z * z * (-0.5 * LOG2E))
    t = 1.0 / (1.0 + (0.3275911 * 0.7071067811865476) * jnp.abs(z))
    poly = t * (0.254829592 + t * (-0.284496736 + t * (1.421413741 + t * (-1.453152027 + t * 1.061405429))))
    tail = 0.5 * poly * spread
    return jnp.where(z >= 0, 1.0 - tail, tail), spread


def hidden_pair(z, hidden_grad):
    phi, spread = gelu_parts(z)
    return (z * phi).astype(BF16), hidden_grad * (phi + z * spread * 0.3989422804014327)


def upstream_kernel(cot_ref, down_ref, up_ref, out_ref, sum_ref, pack_hbm, sems):
    d = up_ref.shape[0]
    copies = [
        pltpu.make_async_copy(up_ref, pack_hbm.at[pl.ds(0, d)], sems.at[0]),
        pltpu.make_async_copy(down_ref, pack_hbm.at[pl.ds(d, down_ref.shape[0])], sems.at[1]),
    ]

    @pl.when(pl.program_id(0) == 0)
    def _():
        for copy in copies:
            copy.start()

    cot = cot_ref[...]
    out_ref[...] = mm(cot, down_ref[...], NT).astype(BF16)
    gather_rows(sum_ref, pl.program_id(0) == 0, cot)

    @pl.when(pl.program_id(0) == pl.num_programs(0) - 1)
    def _():
        for copy in copies:
            copy.wait()


def upstream(cot, up, down):
    tokens, d = cot.shape
    f = down.shape[0]
    tile = tokens // 4
    stay = pl.BlockSpec(memory_space=pl.ANY)
    return call(
        upstream_kernel, "upstream", (4,), [rows(tile, d), whole(down.shape), whole(up.shape)],
        [(rows(tile, f), (tokens, f), BF16), (whole((1, d)), (1, d), F32), (stay, (d + f, d), BF16, True)],
        (cot, down, up), scratch=[pltpu.SemaphoreType.DMA((2,))],
    )


def hidden_kernel(
    orders, x_ref, part_a_ref, part_b_ref, b_out_ref, gain_ref, bias_ref, up_ref, b_up_ref, cot_down_ref, *rest
):
    first = pl.program_id(0) == 0
    if orders:
        half_ref, cot_ref, rest_cot, rest = rest[0], rest[1], rest[2:3], rest[2:]
        earlier, rest = rest[1:-11], rest[-11:]
        up_keep_ref, up_give_ref, down_keep_ref, down_give_ref, up_acc, down_acc = rest[-6:]
        rest = rest[:-6]
    residual_ref, n2_ref, hidden_ref, upg_ref, sum_ref = rest[-5:]
    residual = (
        x_ref[...].astype(F32) + (part_a_ref[...].astype(F32) + part_b_ref[...].astype(F32)) + flat(b_out_ref)
    )
    residual_ref[...] = residual.astype(BF16)
    unit, _ = norm_stats(residual)
    normed = (unit * flat(gain_ref) + flat(bias_ref)).astype(BF16)
    n2_ref[...] = normed
    hidden, grad = hidden_pair(mm(normed, up_ref[...], NN) + flat(b_up_ref), cot_down_ref[...].astype(F32))
    up_grad = grad.astype(BF16)
    hidden_ref[...] = hidden
    upg_ref[...] = up_grad
    gather_rows(sum_ref, first, grad)
    if not orders:
        return

    @pl.when(first)
    def _():
        up_acc[...] = jnp.zeros_like(up_acc)
        down_acc[...] = jnp.zeros_like(down_acc)

    up_acc[...] += mm(normed, up_grad, TN)
    down_acc[...] += mm(cot_ref[...], hidden, TN)
    if earlier:
        n2_old, hidden_old, upg_old, cot_old = earlier[-3:] + rest_cot
        up_acc[...] += mm(n2_old[...], upg_old[...], TN)
        down_acc[...] += mm(cot_old[...], hidden_old[...], TN)

    @pl.when(pl.program_id(0) == pl.num_programs(0) - 1)
    def _():
        split_chunks(half_ref[0], orders[0], up_acc, up_keep_ref, up_give_ref)
        split_chunks(half_ref[1], orders[1], down_acc, down_keep_ref, down_give_ref)


def hidden_own(sequence, length, x, part_a, part_b, b_out, gain, bias, up, b_up, cot_down, carried=(), weights=()):
    tokens, d = x.shape
    f = up.shape[1]
    count = 4
    tile = length // count
    tall, wide = rows(tile, d, count * sequence), rows(tile, f, count * sequence)
    near = rows(tile, d)
    specs = [tall, near, near] + [whole((d,))] * 3 + [whole(up.shape), whole((f,)), wide]
    out = [(tall, (tokens, d), BF16, True)] * 2 + [(wide, (tokens, f), BF16, True)] * 2 + [(whole((1, f)), (1, f), F32)]
    args = [x, part_a, part_b, b_out, gain, bias, up, b_up, cot_down]
    orders, scratch, earlier = None, [], ()
    if weights:
        orders, halves, cot = weights
        half_count = len(orders[0][0])
        chunk = (half_count, d // (2 * half_count), f)
        specs += [pl.BlockSpec(memory_space=pltpu.SMEM), tall]
        args += [halves, cot]
        specs.append(rows(tile, d))
        args.append(cot)
        earlier = [pl.BlockSpec(memory_space=pl.ANY), rows(tile, d), rows(tile, f), rows(tile, f)]
        out += [(whole(chunk), chunk, BF16)] * 4
        scratch = [pltpu.VMEM((d, f), F32)] * 2
    return call(
        functools.partial(hidden_kernel, orders), "hidden_own", (count,), specs, out, args, scratch=scratch, carried=carried,
        carried_specs=earlier,
    )


def products_kernel(
    n2_ref, cot_ref, hidden_ref, upg_ref, up_a_ref, down_a_ref, far_ref, bias_ref, *rest
):
    mlp_ref, n2g_ref = rest[-2:]
    d = n2_ref.shape[1]
    up_b, down_b = far_ref[:d, :], far_ref[d:, :]
    z = mm(n2_ref[...], up_b, NN) + bias_of(bias_ref, 0)
    hidden_grad = mm(cot_ref[...], down_b, NT)
    mlp_own = mm(hidden_ref[...], down_a_ref[...], NN)
    n2g_own = mm(upg_ref[...], up_a_ref[...], NT)
    hidden, grad = hidden_pair(z, hidden_grad)
    mlp_ref[...] = (mlp_own + mm(hidden, down_b, NN)).astype(BF16)
    n2g_ref[...] = (n2g_own + mm(grad.astype(BF16), up_b, NT)).astype(BF16)


def products(span, n2, cot, hidden, upg, up, down, far, bias, carried=()):
    tokens = n2.shape[0]
    d, f = up.shape
    first, count = span
    tall, wide = rows(TILE, d, first), rows(TILE, f, first)
    return call(
        products_kernel, "feed_forward", (count,),
        [tall, tall, wide, wide, whole(up.shape), whole(down.shape), whole(far.shape), biases(bias)],
        [(tall, (tokens, d), BF16, True), (rows(TILE, d), (count * TILE, d), BF16)],
        (n2, cot, hidden, upg, up, down, far, bias), carried=carried, cover=True,
    )


def middle_kernel(residual_ref, grad_a_ref, grad_b_ref, cot_ref, gain_ref, own_w_ref, far_w_ref, *rest):
    agrad_ref, own_cg_ref, far_cg_ref, sum_ref = rest[-4:]
    unit, scale = norm_stats(residual_ref[...].astype(F32))
    summed = grad_a_ref[...].astype(F32) + grad_b_ref[...].astype(F32)
    rgrad = cot_ref[...].astype(F32) + norm_back(unit, scale, summed * flat(gain_ref))
    agrad = rgrad.astype(BF16)
    agrad_ref[...] = agrad
    own_cg_ref[...] = mm(agrad, own_w_ref[...], NT).astype(BF16)
    far_cg_ref[...] = mm(agrad, far_w_ref[...], NT).astype(BF16)
    gather_rows(sum_ref, pl.program_id(0) == 0, rgrad, summed * unit, summed)


def middle(span, residual, grad_a, grad_b, cot, gain, own_w, far_w, carried=()):
    tokens, d = residual.shape
    own = own_w.shape[1] // 4
    first, count = span
    tile = TILE // 2
    tall, slim, near = rows(tile, d, 2 * first), rows(tile, own, 2 * first), rows(tile, d)
    return call(
        middle_kernel, "second_norm_back", (2 * count,),
        [tall, near, near, tall, whole((d,)), out_weights(own_w), out_weights(far_w)],
        [(tall, (tokens, d), BF16)] + [(slim, (tokens, own), BF16)] * 2 + [(whole((3, d)), (3, d), F32)],
        (residual, grad_a, grad_b, cot, gain, own_w, far_w), carried=carried,
    )


def output_kernel(residual_ref, mlp_a_ref, mlp_b_ref, b_down_ref, out_ref):
    out_ref[...] = (
        residual_ref[...].astype(F32)
        + ((mlp_a_ref[...].astype(F32) + mlp_b_ref[...].astype(F32)) + flat(b_down_ref))
    ).astype(BF16)


def output(residual, mlp_a, mlp_b, b_down):
    tokens, d = residual.shape
    tall = rows(TILE, d)
    return call(
        output_kernel, "block_output", (tokens // TILE,), [tall] * 3 + [whole((d,))],
        [(tall, (tokens, d), BF16)], (residual, mlp_a, mlp_b, b_down), cover=True,
    )[0]


def first_back_kernel(x_ref, grad_a_ref, grad_b_ref, rgrad_ref, gain_ref, *rest):
    unit, scale = norm_stats(x_ref[...].astype(F32))
    upstream = (grad_a_ref[...].astype(F32) + grad_b_ref[...].astype(F32)) * flat(gain_ref)
    rest[-1][...] = rgrad_ref[...].astype(F32) + norm_back(unit, scale, upstream)


def first_back(span, x, grad_a, grad_b, rgrad, gain, carried=()):
    tokens, d = x.shape
    first, count = span
    tall = rows(TILE, d, first)
    return call(
        first_back_kernel, "first_norm_back", (count,), [tall] * 4 + [whole((d,))],
        [(tall, (tokens, d), F32)], (x, grad_a, grad_b, rgrad, gain), carried=carried,
    )


def swap(value, axis, size, bit):
    return lax.ppermute(value, axis, [(i, i ^ bit) for i in range(size)])


def tie(value, *others):
    return lax.optimization_barrier((value,) + others)[0]


class ScatterSums:
    def __init__(self, size, *chains):
        self.size = size
        self.keeps, self.gives, bits = [list(part) for part in zip(*chains)]
        self.bits = [list(each) for each in bits]
        self.me = lax.axis_index("dp").astype(jnp.int32)

    def begin(self):
        self.gots = [swap(give, "dp", self.size, 1 << bits.pop(0)) for give, bits in zip(self.gives, self.bits)]

    def end(self, *others):
        self.gots = [tie(got, *others) if others else got for got in self.gots]
        if self.bits[0]:
            mine = jnp.stack([(self.me >> bits[0]) & 1 for bits in self.bits])
            self.keeps, self.gives = zip(*merge(mine, list(zip(self.keeps, self.gots))))
        return self.gots

    def finish(self, *widths):
        while self.bits[0]:
            self.begin()
            self.end()
        return last_sum(list(zip(self.keeps, self.gots)), widths)


def body(
    n_dp,
    n_mp,
    block_input,
    segment_ids,
    group_ids,
    padding,
    ln1_gain,
    ln1_bias,
    w_qkv,
    b_qv,
    w_out,
    b_out,
    ln2_gain,
    ln2_bias,
    w_up,
    b_up,
    w_down,
    b_down,
    cotangent,
):
    tokens, d = block_input.shape
    sequences, length = segment_ids.shape
    own = w_qkv.shape[2]
    far = lambda value: swap(value, "mp", n_mp, 2)
    near = lambda value: swap(value, "mp", n_mp, 1)
    levels = n_dp.bit_length() - 1
    bits = list(range(levels))
    other_bits = [1, 0] + bits[2:]
    me = lax.axis_index("dp").astype(jnp.int32)
    halves = jnp.stack([me & 1, (me >> 1) & 1])
    orders = (chunk_order(n_dp, bits), chunk_order(n_dp, other_bits))

    small = jnp.stack([b_up, jnp.pad(b_qv.reshape(-1), (0, d - 2 * own))])
    parts = []
    for _ in range(3):
        parts.append(lax.reduce_precision(small, 8, 7))
        small = small - parts[-1]
    small = jnp.pad(jnp.stack(parts, 1).reshape(6, d).astype(BF16), ((0, 10), (0, 0)))
    pack = jnp.concatenate([jnp.transpose(w_qkv, (1, 2, 0)).reshape(3 * own, d), w_out, small], 0)
    pack_far = far(pack)
    table = tables(segment_ids, group_ids, padding)

    *saved_own, n1 = attend_own(table, block_input, ln1_gain, ln1_bias, pack, b_qv)
    ctx_own = saved_own[3]
    cot_down, sum_cot, mlp_own = upstream(tie(cotangent, n1), w_up, w_down)
    mlp_far = far(mlp_own)
    parts, saved_far = [], ()
    for s in range(sequences):
        *saved_far, part = attend_far(s, table, n1, tie(pack_far, cot_down), ctx_own, pack, saved_far)
        parts.append((part, near(part)))
    carried, sums_up = (), []
    for s, (part, other) in enumerate(parts):
        other = tie(other, carried[0] if carried else parts[-1][0])
        weights = (orders, halves, cotangent) if s == sequences - 1 else ()
        *carried, = hidden_own(
            s, length, block_input, part, other, b_out, ln2_gain, ln2_bias, w_up, b_up, cot_down, carried[:4], weights
        )
        sums_up.append(carried[4])
    residual, n2, hidden, upg, _, up_keep, up_give, down_keep, down_give = carried
    sum_mlp = ScatterSums(n_dp, (up_keep, up_give, bits), (down_keep, down_give, other_bits))
    sum_mlp.begin()
    mlp_far = tie(mlp_far, up_keep)
    tiles = tokens // TILE
    shares, mlp, gate = [], (), (up_keep,)
    for span in ((0, tiles - 1), (tiles - 1, 1)):
        *mlp, n2g = products(
            span, tie(n2, *gate), cotangent, hidden, upg, w_up, w_down, mlp_far, pack_far, mlp
        )
        shares.append((span, n2g, near(n2g)))
        if len(shares) == 1:
            gate = sum_mlp.end(n2g)
            sum_mlp.begin()
    gate, carried, sums_mid = (n2g,), (), []
    for span, n2g, other in shares:
        other = tie(other, *gate)
        *carried, sum_mid = middle(span, residual, n2g, other, cotangent, ln2_gain, pack, pack_far, carried)
        sums_mid.append(sum_mid)
        if len(sums_mid) == 1:
            gate = (carried[0], *sum_mlp.end(sum_mid))
            sum_mlp.begin()
    agrad, cgrad_own, cgrad_far = carried
    q, k, v, ctx, lse = saved_own
    *own_grads, keep, give, sum_qv = attend_own_back(
        table, halves[:1], orders[0], q, k, v, ctx, cgrad_own, lse, n1, agrad
    )
    mlp_near = near(mlp[0])
    sum_attn = ScatterSums(n_dp, (keep, give, bits))
    sum_attn.begin()
    got = sum_mlp.end(keep)
    up_sum, down_sum = sum_mlp.finish(up_keep.shape[2], up_keep.shape[2])
    q, k, v, ctx, lse = saved_far
    n1g, sum_first = attend_far_back(
        table, q, k, v, ctx, tie(cgrad_far, keep, *got), lse, block_input, own_grads, pack, pack_far
    )
    sum_first = sum_first + near(sum_first)
    n1g_near = near(tie(n1g, sum_first))
    got = sum_attn.end(n1g)
    sum_attn.begin()
    add = lambda values: functools.reduce(jnp.add, values)
    wide_qv = jnp.concatenate([sum_qv.reshape(1, -1), jnp.zeros((1, d - 2 * own), F32)], 1)
    sums = jnp.concatenate([sum_first, add(sums_mid), sum_cot, add(sums_up), wide_qv], 0)
    other = swap(sums, "dp", n_dp, 1)
    block_output = output(tie(residual, n1g, *got, sums), mlp[0], mlp_near, b_down)
    sums = sums + tie(other, block_output)
    other = swap(sums, "dp", n_dp, 2)
    got = sum_attn.end(block_output, sums)
    sum_attn.begin()
    outputs = first_back((0, tiles - 1), block_input, n1g, tie(n1g_near, block_output, *got, sums), agrad, ln1_gain)
    sums = sums + tie(other, *outputs)
    if levels > 2:
        other = swap(sums, "dp", n_dp, 4)
    got = sum_attn.end(*outputs)
    qkv_sum, out_sum = sum_attn.finish(3 * own, own)
    input_grad, = first_back((tiles - 1, 1), block_input, n1g, tie(n1g_near, sums, qkv_sum), agrad, ln1_gain, outputs)
    if levels > 2:
        sums = sums + tie(other, input_grad)
    for bit in range(3, levels):
        sums = sums + swap(sums, "dp", n_dp, 1 << bit)

    piece, tiny = d // n_dp, own // n_dp
    mine = lax.dynamic_slice(sums, (0, me * piece), (sums.shape[0] - 1, piece))
    vectors = [mine[i] for i in range(7)]
    return (
        block_output,
        input_grad,
        vectors[0],
        vectors[1],
        qkv_sum.reshape(piece, 3, own),
        lax.dynamic_slice(sums[7, : 2 * own].reshape(2, own), (0, me * tiny), (2, tiny)),
        out_sum.T,
        vectors[2],
        vectors[3],
        vectors[4],
        up_sum,
        vectors[6],
        down_sum.T,
        vectors[5],
    )


def solution(mesh):
    return jax.shard_map(
        functools.partial(body, mesh.shape["dp"], mesh.shape["mp"]),
        mesh=mesh,
        in_specs=(
            P("dp", None),
            P("dp", None),
            P("dp", None),
            P("dp", None),
            P(),
            P(),
            P(None, None, "mp"),
            P(None, "mp"),
            P("mp", None),
            P(),
            P(),
            P(),
            P(None, "mp"),
            P("mp"),
            P("mp", None),
            P(),
            P("dp", None),
        ),
        out_specs=(
            P("dp", None),
            P("dp", None),
            P("dp"),
            P("dp"),
            P("dp", None, "mp"),
            P(None, ("mp", "dp")),
            P("mp", "dp"),
            P("dp"),
            P("dp"),
            P("dp"),
            P("dp", "mp"),
            P(("mp", "dp")),
            P("mp", "dp"),
            P("dp"),
        ),
        check_vma=False,
    )
```

```python
import functools

import jax
import jax.numpy as jnp
from jax import lax
from jax.experimental import pallas as pl
from jax.experimental.pallas import tpu as pltpu
from jax.sharding import PartitionSpec as P

HD = 64
QB = 128
GRAIN = 64
GRAIN_BITS = 6
GROUP = 2
BACK_GROUP = 2
LONGEST = 256
FREE = dict(
    masks=(), attend_own=(), attend_far=(), attend_own_back=(7, 10), attend_far_back=(6, 9, 10, 11), upstream=(),
    hidden_own=(1, 2, 8), feed_forward=(4, 5, 6), second_norm_back=(1, 2), block_output=(), first_norm_back=(1, 2),
    merge=range(99), last_sum=range(99),
)
GRANTS = dict(
    masks=4, attend_own=20, attend_far=14, attend_own_back=28, attend_far_back=34, upstream=12, hidden_own=34,
    feed_forward=22, second_norm_back=17, block_output=8, first_norm_back=14, merge=6, last_sum=4,
)
TILE = 512
COVER = 10**12
MASKED = -1e30
EPS = 1e-05
LOG2E = 1.4426950408889634
F32 = jnp.float32
BF16 = jnp.bfloat16
NT = (((1,), (1,)), ((), ()))
NN = (((1,), (0,)), ((), ()))
TN = (((0,), (0,)), ((), ()))


def mm(a, b, dims):
    return lax.dot_general(a, b, dims, preferred_element_type=F32)


def flat(ref):
    return ref[...].reshape(1, -1)


def hosted(kernel, taken, carried, given, rider, half_ref, *refs):
    refs = list(refs)
    cut = lambda count: [refs.pop(0) for _ in range(count)]
    main_in, rider_in, kept, main_out, rider_out = map(cut, (taken, len(rider.args), carried, given, len(rider.out)))
    kernel(*main_in, *kept, *main_out, *refs)

    @pl.when(pl.program_id(0) == 0)
    def _():
        rider.body(rider_in, rider_out)


def call(kernel, name, grid, in_specs, out, args, scratch=(), prefetch=0, carried=(), cover=False, carried_specs=(), rider=None):
    in_specs, out, args = list(in_specs), list(out), list(args)
    pinned = lambda at: at >= prefetch and args[at].size >= 1 << 17 and at not in FREE[name]
    args = [pltpu.with_memory_space_constraint(arg, pltpu.HBM) if pinned(at) else arg for at, arg in enumerate(args)]
    if rider:
        kernel = functools.partial(hosted, kernel, len(args), len(carried), len(out), rider)
        in_specs, out, args, prefetch = in_specs + rider.specs, out + rider.out, [rider.halves] + args + rider.args, 1
    return pl.pallas_call(
        kernel,
        grid_spec=pltpu.PrefetchScalarGridSpec(
            num_scalar_prefetch=prefetch,
            grid=grid,
            in_specs=in_specs + list(carried_specs or [pl.BlockSpec(memory_space=pl.ANY)] * len(carried)),
            out_specs=[entry[0] for entry in out],
            scratch_shapes=list(scratch),
        ),
        out_shape=[pltpu.HBM(*entry[1:3]) if entry[3:] else jax.ShapeDtypeStruct(*entry[1:3]) for entry in out],
        input_output_aliases={len(args) + i: i for i in range(len(carried))},
        compiler_params=pltpu.CompilerParams(vmem_limit_bytes=GRANTS[name] * 1024 * 1024),
        cost_estimate=pl.CostEstimate(flops=COVER if cover else 0, bytes_accessed=1024, transcendentals=0),
        name=name,
    )(*args, *carried)


def whole(shape):
    return pl.BlockSpec(shape, lambda *ids: (0,) * len(shape))


def rows(tile, width, skip=0):
    return pl.BlockSpec((tile, width), lambda i, *rest: (i + skip, 0))


def norm_stats(values):
    average = jnp.mean(values, -1, keepdims=True)
    centered = values - average
    variance = jnp.mean(centered * centered, -1, keepdims=True)
    scale = lax.rsqrt(variance + EPS)
    return centered * scale, scale


def norm_back(unit, scale, upstream):
    first = jnp.mean(upstream, -1, keepdims=True)
    second = jnp.mean(upstream * unit, -1, keepdims=True)
    return scale * (upstream - first - unit * second)


def total(values):
    return jnp.sum(values.astype(F32), 0, keepdims=True)


def gather_rows(ref, first, *values):
    @pl.when(first)
    def _():
        ref[...] = jnp.zeros_like(ref)

    for at, value in enumerate(values):
        ref[at : at + 1, :] += total(value)


def masks_kernel(segment_ref, group_ref, padding_ref, bounds_ref, code_ref):
    sequences, length = segment_ref.shape
    blocks = length // QB
    low = segment_ref[...] * 4
    high = low + group_ref[...]
    codes = jnp.where(padding_ref[...] == 0, high, -1)
    place = lax.broadcasted_iota(jnp.int32, (1, sequences * blocks), 1)
    key_from = jnp.zeros((1, sequences * blocks), jnp.int32)
    key_to = jnp.zeros((1, sequences * blocks), jnp.int32)
    for s in range(sequences):
        for at, rows_of in enumerate((codes, low, high)):
            code_ref[s, at : at + 1, :] = rows_of[s : s + 1, :]
        row = segment_ref[s : s + 1, :]
        for block in range(blocks):
            earliest = row[:, block * QB : block * QB + 1]
            latest = row[:, (block + 1) * QB - 1 : (block + 1) * QB]
            before = jnp.sum((row < earliest).astype(F32), 1, keepdims=True).astype(jnp.int32)
            until = jnp.sum((row <= latest).astype(F32), 1, keepdims=True).astype(jnp.int32)
            here = place == s * blocks + block
            key_from = jnp.where(here, before, key_from)
            key_to = jnp.where(here, until, key_to)
    key_from = key_from & -16
    grains = jnp.maximum((key_to - key_from + (GRAIN - 1)) >> GRAIN_BITS, QB // GRAIN)
    bounds_ref[0:1, :] = jnp.minimum(key_from, length - grains * GRAIN)
    bounds_ref[1:2, :] = grains


def tables(segment_ids, group_ids, padding):
    sequences, length = segment_ids.shape
    bounds = (2, sequences * (length // QB))
    codes = (sequences, 3, length)
    return call(
        masks_kernel, "masks", (1,), [whole(segment_ids.shape)] * 3,
        [(whole(bounds), bounds, jnp.int32), (whole(codes), codes, jnp.int32)], (segment_ids, group_ids, padding),
    )


def extents(length):
    most = min(QB + 2 * LONGEST, length) // GRAIN
    return [extent for extent in (3, 4, 5, 6, 8) if extent < most] + [most]


def head_groups(width):
    return [slice(at, min(at + 2 * HD, width)) for at in range(0, width, 2 * HD)]


def stack_heads(values):
    if values.shape[1] == HD:
        return values
    lane = lax.broadcasted_iota(jnp.int32, values.shape, 1)
    zero = jnp.zeros_like(values)
    return jnp.concatenate(
        [jnp.where(lane < HD, values, zero), jnp.where(lane >= HD, values, zero)], 0
    )


def join_heads(values):
    if values.shape[1] == HD:
        return values
    lane = lax.broadcasted_iota(jnp.int32, (QB, 2 * HD), 1)
    return jnp.where(lane < HD, values[:QB], values[QB:])


def spread_codes(code_ref, column_ref):
    for at in range(0, column_ref.shape[0], QB):
        column_ref[at : at + QB, :] = jnp.broadcast_to(code_ref[0:1, at : at + QB], (QB, QB)).T


def mask_bias(column_ref, code_ref, start, extent, block):
    mine = pl.ds(pl.multiple_of(block * QB, QB), QB)
    codes = column_ref[pl.ds(start, extent), :]
    shape = (extent, QB)
    apart = lax.broadcasted_iota(jnp.int32, shape, 0) - lax.broadcasted_iota(jnp.int32, shape, 1)
    allowed = ((codes >= code_ref[1:2, mine]) & (codes <= code_ref[2:3, mine])) | (
        apart == block * QB - start
    )
    return jnp.where(allowed, jnp.float32(0), jnp.float32(MASKED))


def widen(bias, cols):
    return jnp.concatenate([bias, bias], 1) if cols.stop - cols.start > HD else bias


def each_block(bound_ref, length, group, sequence, run):
    turns = length // QB // group

    def step(turn, carry):
        place = (sequence * turns + turn) * group
        grains = functools.reduce(jnp.maximum, [bound_ref[1, place + i] for i in range(group)])
        blocks = [turn * group + i for i in range(group)]
        least = 0
        for extent in extents(length):
            starts = [
                pl.multiple_of(jnp.minimum(bound_ref[0, place + i], length - extent * GRAIN), 16) for i in range(group)
            ]
            pl.when((grains > least) & (grains <= extent))(functools.partial(run, extent * GRAIN, blocks, starts))
            least = extent
        return carry

    lax.fori_loop(0, turns, step, 0)


def project(normed, wt_ref, q_bias, v_bias, q_ref, k_ref, v_ref):
    own = q_ref.shape[1]
    q_ref[...] = (mm(normed, wt_ref[:own, :], NT) + q_bias).astype(BF16)
    k_ref[...] = mm(normed, wt_ref[own : 2 * own, :], NT).astype(BF16)
    v_ref[...] = (mm(normed, wt_ref[2 * own :, :], NT) + v_bias).astype(BF16)


def attend(sequence, bound_ref, code_ref, column_ref, q_ref, k_ref, v_ref, ctx_ref, lse_ref):
    length, width = q_ref.shape
    heads = head_groups(width)
    spread_codes(code_ref, column_ref)

    def run(extent, blocks, starts):
        units, scores, probs, totals, biases = [], [], [], [], []
        for i, (block, start) in enumerate(zip(blocks, starts)):
            here = pl.ds(start, extent)
            mine = pl.ds(pl.multiple_of(block * QB, QB), QB)
            for p, cols in enumerate(heads):
                units.append((i, block, here, mine, p, cols))
                scores.append(mm(k_ref[here, cols], stack_heads(q_ref[mine, cols]), NT))
            biases.append(mask_bias(column_ref, code_ref, start, extent, block))
        for (i, block, here, mine, p, cols), score in zip(units, scores):
            score = score * (0.125 * LOG2E) + widen(biases[i], cols)
            top = jnp.max(score, 0, keepdims=True)
            weights = jnp.exp2(score - top)
            summed = jnp.sum(weights, 0, keepdims=True)
            lse_ref[block, p : p + 1, : score.shape[1]] = top + jnp.log2(summed)
            totals.append(1.0 / summed)
            probs.append(weights.astype(BF16))
        for (i, block, here, mine, p, cols), prob, scale in zip(units, probs, totals):
            turned = v_ref[here, cols].T
            both = [
                mm(turned[at * HD : (at + 1) * HD], prob[:, at * QB : (at + 1) * QB], NN)
                * scale[:, at * QB : (at + 1) * QB]
                for at in range(prob.shape[1] // QB)
            ]
            ctx_ref[mine, cols] = jnp.concatenate(both, 0).T.astype(BF16)

    each_block(bound_ref, length, GROUP, sequence, run)


def begin_copies(pairs, sems):
    copies = [pltpu.make_async_copy(source, target, sems.at[at]) for at, (source, target) in enumerate(pairs)]
    for copy in copies:
        copy.start()

    def finish():
        for copy in copies:
            copy.wait()

    return finish


def own_kernel(
    bound_ref, code_ref, x_ref, gain_ref, bias_ref, wt_ref, qv_ref,
    ctx_ref, lse_ref, q_hbm, k_hbm, v_hbm, n1_hbm, column_ref, q_ref, k_ref, v_ref, n1_ref, sems,
):
    length = x_ref.shape[0]
    here = pl.ds(pl.multiple_of(pl.program_id(0) * length, length), length)
    chunks = [pl.ds(at, length // 4) for at in range(0, length, length // 4)]

    def norm(chunk):
        unit, _ = norm_stats(x_ref[chunk, :].astype(F32))
        n1_ref[chunk, :] = (unit * flat(gain_ref) + flat(bias_ref)).astype(BF16)

    norm(chunks[0])
    for at, chunk in enumerate(chunks):
        for following in chunks[at + 1 : at + 2]:
            norm(following)
        project(
            n1_ref[chunk, :], wt_ref, qv_ref[0:1, :], qv_ref[1:2, :], *(ref.at[chunk] for ref in (q_ref, k_ref, v_ref))
        )
    finish = begin_copies(
        [(q_ref, q_hbm.at[here]), (k_ref, k_hbm.at[here]), (v_ref, v_hbm.at[here]), (n1_ref, n1_hbm.at[here])], sems
    )
    attend(pl.program_id(0), bound_ref, code_ref, column_ref, q_ref, k_ref, v_ref, ctx_ref, lse_ref)
    finish()


STAY = pl.BlockSpec(memory_space=pl.ANY)


def attention_outs(tokens, width, length, sequences, skip=0):
    tall = rows(length, width, skip)
    lse = (length // QB, 8, 2 * QB)
    return [
        (tall, (tokens, width), BF16, True),
        (pl.BlockSpec(lse, lambda s, *ids: (s + skip, 0, 0)), (sequences * lse[0],) + lse[1:], F32, True),
    ] + [(STAY, (tokens, width), BF16, True)] * 3


def attention_scratch(length, width):
    return [pltpu.VMEM((length, QB), jnp.int32)] + [pltpu.VMEM((length, width), BF16)] * 3


def projections(pack):
    return pl.BlockSpec((pack.shape[1] // 4 * 3, pack.shape[1]), lambda *ids: (0, 0))


def out_weights(pack):
    return pl.BlockSpec((pack.shape[1] // 4, pack.shape[1]), lambda *ids: (3, 0))


def biases(pack):
    return pl.BlockSpec((16, pack.shape[1]), lambda *ids: (pack.shape[1] // 16, 0))


def bias_of(ref, which):
    part = [ref[3 * which + at : 3 * which + at + 1, :].astype(F32) for at in range(3)]
    return part[0] + (part[1] + part[2])


def codes_spec(codes, skip=0):
    return pl.BlockSpec((None,) + codes.shape[1:], lambda s, *ids: (s + skip, 0, 0))


def attend_own(table, x, gain, bias, wt, b_qv):
    bounds, codes = table
    tokens, d = x.shape
    sequences, _, length = codes.shape
    return call(
        own_kernel, "attend_own", (sequences,),
        [codes_spec(codes), rows(length, d), whole(gain.shape), whole(bias.shape), projections(wt), whole(b_qv.shape)],
        attention_outs(tokens, b_qv.shape[1], length, sequences) + [(STAY, (tokens, d), BF16, True)],
        (bounds, codes, x, gain, bias, wt, b_qv),
        scratch=attention_scratch(length, b_qv.shape[1])
        + [pltpu.VMEM((length, d), BF16), pltpu.SemaphoreType.DMA((4,))],
        prefetch=1,
    )


def far_kernel(
    sequence, bound_ref, code_ref, n1_ref, wt_ref, bias_ref, own_ctx_hbm, pack_hbm, far_hbm, *rest
):
    ctx_ref, lse_ref, q_hbm, k_hbm, v_hbm, part_ref = rest[-14:-8]
    column_ref, q_ref, k_ref, v_ref, own_ctx_ref, own_w_ref, far_w_ref, sems = rest[-8:]
    length, own = q_ref.shape
    here = pl.ds(sequence * length, length)
    weights = pl.ds(3 * own, own)
    late = begin_copies(
        [
            (own_ctx_hbm.at[here], own_ctx_ref),
            (pack_hbm.at[weights], own_w_ref),
            (far_hbm.at[weights], far_w_ref),
        ],
        sems.at[pl.ds(0, 3)],
    )
    bias = bias_of(bias_ref, 1)
    project(n1_ref[...], wt_ref, bias[:, :own], bias[:, own : 2 * own], q_ref, k_ref, v_ref)
    finish = begin_copies(
        [(q_ref, q_hbm.at[here]), (k_ref, k_hbm.at[here]), (v_ref, v_hbm.at[here])], sems.at[pl.ds(3, 3)]
    )
    attend(sequence, bound_ref, code_ref, column_ref, q_ref, k_ref, v_ref, ctx_ref, lse_ref)
    late()
    part_ref[...] = (
        mm(own_ctx_ref[...], own_w_ref[...], NN) + mm(ctx_ref[...], far_w_ref[...], NN)
    ).astype(BF16)
    finish()


def attend_far(sequence, table, n1, far, own_ctx, pack, carried=()):
    bounds, codes = table
    tokens, d = n1.shape
    sequences, _, length = codes.shape
    own = own_ctx.shape[1]
    return call(
        functools.partial(far_kernel, sequence), "attend_far", (1,),
        [codes_spec(codes, sequence), rows(length, d, sequence), projections(far), biases(far)] + [STAY] * 3,
        attention_outs(tokens, own, length, sequences, sequence) + [(rows(length, d), (length, d), BF16)],
        (bounds, codes, n1, far, far, own_ctx, pack, far),
        scratch=attention_scratch(length, own)
        + [pltpu.VMEM((length, own), BF16)]
        + [pltpu.VMEM((own, d), BF16)] * 2
        + [pltpu.SemaphoreType.DMA((6,))],
        prefetch=1, carried=carried,
    )


def attend_back(
    bound_ref, code_ref, column_ref, q_ref, k_ref, v_ref, ctx_ref, grad_ref, lse_ref,
    dq_ref, dk_ref, dv_ref, dk_acc, dv_acc,
):
    length, width = q_ref.shape
    heads = head_groups(width)
    spread_codes(code_ref, column_ref)
    dk_acc[...] = jnp.zeros_like(dk_acc)
    dv_acc[...] = jnp.zeros_like(dv_acc)

    def run(extent, blocks, starts):
        units, stacked, upstream, scores, grads, biases = [], [], [], [], [], []
        for i, (block, start) in enumerate(zip(blocks, starts)):
            here = pl.ds(start, extent)
            mine = pl.ds(pl.multiple_of(block * QB, QB), QB)
            for p, cols in enumerate(heads):
                units.append((i, block, here, mine, p, cols))
                stacked.append(stack_heads(q_ref[mine, cols]))
                upstream.append(stack_heads(grad_ref[mine, cols]))
                scores.append(mm(k_ref[here, cols], stacked[-1], NT))
                grads.append(mm(v_ref[here, cols], upstream[-1], NT))
            biases.append(mask_bias(column_ref, code_ref, start, extent, block))
        probs, score_grads = [], []
        for (i, block, here, mine, p, cols), score, grad in zip(units, scores, grads):
            turned = (ctx_ref[mine, cols].astype(F32) * grad_ref[mine, cols].astype(F32)).T
            delta = jnp.concatenate(
                [
                    jnp.sum(turned[at : at + HD], 0, keepdims=True)
                    for at in range(0, turned.shape[0], HD)
                ],
                1,
            )
            weights = jnp.exp2(
                score * (0.125 * LOG2E) + widen(biases[i], cols) - lse_ref[block, p : p + 1, : score.shape[1]]
            )
            probs.append(weights.astype(BF16))
            score_grads.append((weights * (grad - delta)).astype(BF16))
        for n, (i, block, here, mine, p, cols) in enumerate(units):
            dv_acc[here, cols] += mm(probs[n], upstream[n], NN)
            dk_acc[here, cols] += mm(score_grads[n], stacked[n], NN)
            dq = join_heads(mm(score_grads[n], k_ref[here, cols], TN))
            dq_ref[mine, cols] = (dq * 0.125).astype(BF16)

    each_block(bound_ref, length, BACK_GROUP, pl.program_id(0), run)
    dk_ref[...] = (dk_acc[...] * 0.125).astype(BF16)
    dv_ref[...] = dv_acc[...].astype(BF16)


def own_back_kernel(
    order, bound_ref, half_ref, code_ref, q_ref, k_ref, v_ref, ctx_ref, grad_ref, lse_ref, n1_hbm, agrad_hbm,
    dq_ref, dk_ref, dv_ref, keep_ref, give_ref, sum_ref, dk_acc, dv_acc, column_ref, weight_acc, n1_ref, agrad_ref, sems,
):
    length = q_ref.shape[0]
    here = pl.ds(pl.multiple_of(pl.program_id(0) * length, length), length)
    late = begin_copies([(n1_hbm.at[here], n1_ref), (agrad_hbm.at[here], agrad_ref)], sems)
    attend_back(
        bound_ref, code_ref, column_ref, q_ref, k_ref, v_ref, ctx_ref, grad_ref, lse_ref,
        dq_ref, dk_ref, dv_ref, dk_acc, dv_acc,
    )
    first = pl.program_id(0) == 0

    @pl.when(first)
    def _():
        weight_acc[...] = jnp.zeros_like(weight_acc)
        sum_ref[...] = jnp.zeros_like(sum_ref)

    own = dq_ref.shape[1]
    late()
    normed = n1_ref[...]
    for at, grad in enumerate((dq_ref, dk_ref, dv_ref)):
        weight_acc[:, at * own : (at + 1) * own] += mm(normed, grad[...], TN)
    weight_acc[:, 3 * own :] += mm(agrad_ref[...], ctx_ref[...], TN)
    sum_ref[0:1, :] += total(dq_ref[...])
    sum_ref[1:2, :] += total(dv_ref[...])

    @pl.when(pl.program_id(0) == pl.num_programs(0) - 1)
    def _():
        split_chunks(half_ref[0], order, weight_acc, keep_ref, give_ref)


def attend_own_back(table, half, order, q, k, v, ctx, grad, lse, n1, agrad):
    bounds, codes = table
    tokens, d = n1.shape
    own = q.shape[1]
    sequences, _, length = codes.shape
    tall = rows(length, own)
    lse_spec = pl.BlockSpec((length // QB, 8, 2 * QB), lambda s, *ids: (s, 0, 0))
    count = len(order[0])
    chunk = (count, d // (2 * count), 4 * own)
    return call(
        functools.partial(own_back_kernel, order), "attend_own_back", (sequences,),
        [codes_spec(codes)] + [tall] * 5 + [lse_spec, STAY, STAY],
        [(tall, (tokens, own), BF16)] * 3 + [(whole(chunk), chunk, BF16)] * 2 + [(whole((2, own)), (2, own), F32)],
        (bounds, half, codes, q, k, v, ctx, grad, lse, n1, agrad),
        scratch=[pltpu.VMEM((length, own), F32)] * 2
        + [pltpu.VMEM((length, QB), jnp.int32), pltpu.VMEM((d, 4 * own), F32)]
        + [pltpu.VMEM((length, d), BF16)] * 2
        + [pltpu.SemaphoreType.DMA((2,))],
        prefetch=2, cover=True,
    )


def far_back_kernel(
    bound_ref, code_ref, q_ref, k_ref, v_ref, ctx_ref, grad_ref, lse_ref,
    x_hbm, aq_hbm, ak_hbm, av_hbm, wa_hbm, wb_hbm,
    n1g_ref, sum_ref, dk_acc, dv_acc, column_ref, dq_ref, dk_ref, dv_ref,
    x_ref, aq_ref, ak_ref, av_ref, wa_ref, wb_ref, sems,
):
    length = q_ref.shape[0]
    here = pl.ds(pl.multiple_of(pl.program_id(0) * length, length), length)
    first = pl.ds(0, wa_ref.shape[0])
    late = begin_copies(
        [
            (aq_hbm.at[here], aq_ref),
            (ak_hbm.at[here], ak_ref),
            (av_hbm.at[here], av_ref),
            (wa_hbm.at[first], wa_ref),
            (wb_hbm.at[first], wb_ref),
            (x_hbm.at[here], x_ref),
        ],
        sems,
    )
    attend_back(
        bound_ref, code_ref, column_ref, q_ref, k_ref, v_ref, ctx_ref, grad_ref, lse_ref,
        dq_ref, dk_ref, dv_ref, dk_acc, dv_acc,
    )
    own = aq_ref.shape[1]
    late()
    grad = None
    for w_ref, grads in ((wa_ref, (aq_ref, ak_ref, av_ref)), (wb_ref, (dq_ref, dk_ref, dv_ref))):
        for place, one_ref in enumerate(grads):
            here = mm(one_ref[...], w_ref[place * own : (place + 1) * own, :], NN)
            grad = here if grad is None else grad + here
    n1g_ref[...] = grad.astype(BF16)
    unit, _ = norm_stats(x_ref[...].astype(F32))
    gather_rows(sum_ref, pl.program_id(0) == 0, grad * unit, grad)


def attend_far_back(table, q, k, v, ctx, grad, lse, x, own_grads, own_wt, far_wt):
    bounds, codes = table
    tokens, d = x.shape
    own = q.shape[1]
    sequences, _, length = codes.shape
    tall, high = rows(length, own), rows(length, d)
    lse_spec = pl.BlockSpec((length // QB, 8, 2 * QB), lambda s, *ids: (s, 0, 0))
    return call(
        far_back_kernel, "attend_far_back", (sequences,),
        [codes_spec(codes)] + [tall] * 5 + [lse_spec] + [STAY] * 6,
        [(high, (tokens, d), BF16), (whole((2, d)), (2, d), F32)],
        (bounds, codes, q, k, v, ctx, grad, lse, x, *own_grads, own_wt, far_wt),
        scratch=[pltpu.VMEM((length, own), F32)] * 2
        + attention_scratch(length, own)
        + [pltpu.VMEM((length, d), BF16)]
        + [pltpu.VMEM((length, own), BF16)] * 3
        + [pltpu.VMEM((3 * own, d), BF16)] * 2
        + [pltpu.SemaphoreType.DMA((6,))],
        prefetch=1, cover=True,
    )


def reversed_bits(value, count):
    return sum(((value >> i) & 1) << (count - 1 - i) for i in range(count))


def chunk_order(size, bits):
    inner = range(size // 2)
    spread = lambda low, at: sum(((low >> (len(bits) - 2 - i)) & 1) << bit for i, bit in enumerate(bits[1:])) | at << bits[0]
    return [[spread(low, at) for low in inner] for at in (0, 1)]


def split_chunks(half, order, terms, keep_ref, give_ref):
    piece = keep_ref.shape[1]

    def store(mine):
        for ref, devices in ((keep_ref, order[mine]), (give_ref, order[1 - mine])):
            for at, device in enumerate(devices):
                ref[at] = terms[device * piece : (device + 1) * piece, :].astype(BF16)

    for mine in (0, 1):
        pl.when(half == mine)(functools.partial(store, mine))


class Rider:
    def __init__(self, halves, keeps, gots, joint):
        self.halves, self.joint = halves, joint
        self.specs, self.out, self.args = [], [], []
        for chain, keep in enumerate(keeps):
            count, piece, width = keep.shape
            block = (count // 2, piece, width)
            base = 2 * chain if len(gots) < len(keeps) else 0
            got = gots[0 if base else min(chain, len(gots) - 1)]
            at = lambda mine, first, chain=chain: pl.BlockSpec(
                block, lambda i, ref, *ids: (first + (ref[chain] if mine else 1 - ref[chain]), 0, 0)
            )
            self.specs += [at(True, 0), at(True, base), at(False, 0), at(False, base)]
            self.out.append((whole(block), block, F32))
            self.args += [keep, got, keep, got]
        shape = (block[0] * len(keeps),) + block[1:]
        self.out += [(whole(shape), shape, BF16)] if joint else [(whole(block), block, BF16)] * len(keeps)

    def body(self, refs, out):
        chains = len(refs) // 4
        for chain in range(chains):
            keep_a, got_a, keep_b, got_b = refs[4 * chain : 4 * chain + 4]
            out[chain][...] = keep_a[...].astype(F32) + got_a[...].astype(F32)
            give = (keep_b[...].astype(F32) + got_b[...].astype(F32)).astype(BF16)
            if self.joint:
                size = give.shape[0]
                out[chains][chain * size : (chain + 1) * size] = give
            else:
                out[chains + chain][...] = give


def alone_kernel():
    pass


def last_sum_kernel(count, joint, *refs):
    arrived = 1 if joint else count
    keeps, gots, out = refs[:count], refs[count : count + arrived], refs[count + arrived :]
    for chain in range(count):
        value = keeps[chain][0].astype(F32) + (gots[0][chain] if joint else gots[chain][0]).astype(F32)
        at = 0
        while at < value.shape[1]:
            out[0][...] = value[:, at : at + out[0].shape[1]]
            at += out[0].shape[1]
            out = out[1:]


def last_sum(keeps, gots, widths):
    piece = keeps[0].shape[1]
    arrays = [*keeps, *gots]
    return call(
        functools.partial(last_sum_kernel, len(keeps), len(gots) < len(keeps)), "last_sum", (1,),
        [whole(array.shape) for array in arrays],
        [(whole((piece, width)), (piece, width), F32) for width in widths], arrays,
    )


def gelu_parts(z):
    spread = jnp.exp2(z * z * (-0.5 * LOG2E))
    t = 1.0 / (1.0 + (0.3275911 * 0.7071067811865476) * jnp.abs(z))
    poly = t * (0.254829592 + t * (-0.284496736 + t * (1.421413741 + t * (-1.453152027 + t * 1.061405429))))
    tail = 0.5 * poly * spread
    return jnp.where(z >= 0, 1.0 - tail, tail), spread


def hidden_pair(z, hidden_grad):
    phi, spread = gelu_parts(z)
    return (z * phi).astype(BF16), hidden_grad * (phi + z * spread * 0.3989422804014327)


def upstream_kernel(cot_ref, down_ref, up_ref, out_ref, sum_ref, pack_hbm, sems):
    d = up_ref.shape[0]
    copies = [
        pltpu.make_async_copy(up_ref, pack_hbm.at[pl.ds(0, d)], sems.at[0]),
        pltpu.make_async_copy(down_ref, pack_hbm.at[pl.ds(d, down_ref.shape[0])], sems.at[1]),
    ]

    @pl.when(pl.program_id(0) == 0)
    def _():
        for copy in copies:
            copy.start()

    cot = cot_ref[...]
    out_ref[...] = mm(cot, down_ref[...], NT).astype(BF16)
    gather_rows(sum_ref, pl.program_id(0) == 0, cot)

    @pl.when(pl.program_id(0) == pl.num_programs(0) - 1)
    def _():
        for copy in copies:
            copy.wait()


def upstream(cot, up, down):
    tokens, d = cot.shape
    f = down.shape[0]
    tile = tokens // 4
    stay = pl.BlockSpec(memory_space=pl.ANY)
    return call(
        upstream_kernel, "upstream", (4,), [rows(tile, d), whole(down.shape), whole(up.shape)],
        [(rows(tile, f), (tokens, f), BF16), (whole((1, d)), (1, d), F32), (stay, (d + f, d), BF16, True)],
        (cot, down, up), scratch=[pltpu.SemaphoreType.DMA((2,))],
    )


def hidden_kernel(
    orders, x_ref, part_a_ref, part_b_ref, b_out_ref, gain_ref, bias_ref, up_ref, b_up_ref, cot_down_ref, *rest
):
    first = pl.program_id(0) == 0
    if orders:
        half_ref, cot_ref, rest_cot, rest = rest[0], rest[1], rest[2:3], rest[2:]
        earlier, rest = rest[1:-11], rest[-11:]
        up_keep_ref, up_give_ref, down_keep_ref, down_give_ref, up_acc, down_acc = rest[-6:]
        rest = rest[:-6]
    residual_ref, n2_ref, hidden_ref, upg_ref, sum_ref = rest[-5:]
    residual = (
        x_ref[...].astype(F32) + (part_a_ref[...].astype(F32) + part_b_ref[...].astype(F32)) + flat(b_out_ref)
    )
    residual_ref[...] = residual.astype(BF16)
    unit, _ = norm_stats(residual)
    normed = (unit * flat(gain_ref) + flat(bias_ref)).astype(BF16)
    n2_ref[...] = normed
    hidden, grad = hidden_pair(mm(normed, up_ref[...], NN) + flat(b_up_ref), cot_down_ref[...].astype(F32))
    up_grad = grad.astype(BF16)
    hidden_ref[...] = hidden
    upg_ref[...] = up_grad
    gather_rows(sum_ref, first, grad)
    if not orders:
        return

    @pl.when(first)
    def _():
        up_acc[...] = jnp.zeros_like(up_acc)
        down_acc[...] = jnp.zeros_like(down_acc)

    up_acc[...] += mm(normed, up_grad, TN)
    down_acc[...] += mm(cot_ref[...], hidden, TN)
    if earlier:
        n2_old, hidden_old, upg_old, cot_old = earlier[-3:] + rest_cot
        up_acc[...] += mm(n2_old[...], upg_old[...], TN)
        down_acc[...] += mm(cot_old[...], hidden_old[...], TN)

    @pl.when(pl.program_id(0) == pl.num_programs(0) - 1)
    def _():
        split_chunks(half_ref[0], orders[0], up_acc, up_keep_ref, up_give_ref)
        split_chunks(half_ref[1], orders[1], down_acc, down_keep_ref, down_give_ref)


def hidden_own(sequence, length, x, part_a, part_b, b_out, gain, bias, up, b_up, cot_down, carried=(), weights=()):
    tokens, d = x.shape
    f = up.shape[1]
    count = 4
    tile = length // count
    tall, wide = rows(tile, d, count * sequence), rows(tile, f, count * sequence)
    near = rows(tile, d)
    specs = [tall, near, near] + [whole((d,))] * 3 + [whole(up.shape), whole((f,)), wide]
    out = [(tall, (tokens, d), BF16, True)] * 2 + [(wide, (tokens, f), BF16, True)] * 2 + [(whole((1, f)), (1, f), F32)]
    args = [x, part_a, part_b, b_out, gain, bias, up, b_up, cot_down]
    orders, scratch, earlier = None, [], ()
    if weights:
        orders, halves, cot = weights
        half_count = len(orders[0][0])
        chunk = (half_count, d // (2 * half_count), f)
        specs += [pl.BlockSpec(memory_space=pltpu.SMEM), tall]
        args += [halves, cot]
        specs.append(rows(tile, d))
        args.append(cot)
        earlier = [pl.BlockSpec(memory_space=pl.ANY), rows(tile, d), rows(tile, f), rows(tile, f)]
        out += [(whole(chunk), chunk, BF16)] * 4
        scratch = [pltpu.VMEM((d, f), F32)] * 2
    return call(
        functools.partial(hidden_kernel, orders), "hidden_own", (count,), specs, out, args, scratch=scratch, carried=carried,
        carried_specs=earlier,
    )


def products_kernel(
    n2_ref, cot_ref, hidden_ref, upg_ref, up_a_ref, down_a_ref, far_ref, bias_ref, *rest
):
    mlp_ref, n2g_ref = rest[-2:]
    d = n2_ref.shape[1]
    up_b, down_b = far_ref[:d, :], far_ref[d:, :]
    z = mm(n2_ref[...], up_b, NN) + bias_of(bias_ref, 0)
    hidden_grad = mm(cot_ref[...], down_b, NT)
    mlp_own = mm(hidden_ref[...], down_a_ref[...], NN)
    n2g_own = mm(upg_ref[...], up_a_ref[...], NT)
    hidden, grad = hidden_pair(z, hidden_grad)
    mlp_ref[...] = (mlp_own + mm(hidden, down_b, NN)).astype(BF16)
    n2g_ref[...] = (n2g_own + mm(grad.astype(BF16), up_b, NT)).astype(BF16)


def products(span, n2, cot, hidden, upg, up, down, far, bias, carried=(), rider=None):
    tokens = n2.shape[0]
    d, f = up.shape
    first, count = span
    tall, wide = rows(TILE, d, first), rows(TILE, f, first)
    return call(
        products_kernel, "feed_forward", (count,),
        [tall, tall, wide, wide, whole(up.shape), whole(down.shape), whole(far.shape), biases(bias)],
        [(tall, (tokens, d), BF16, True), (rows(TILE, d), (count * TILE, d), BF16)],
        (n2, cot, hidden, upg, up, down, far, bias), carried=carried, cover=True, rider=rider,
    )


def middle_kernel(residual_ref, grad_a_ref, grad_b_ref, cot_ref, gain_ref, own_w_ref, far_w_ref, *rest):
    agrad_ref, own_cg_ref, far_cg_ref, sum_ref = rest[-4:]
    unit, scale = norm_stats(residual_ref[...].astype(F32))
    summed = grad_a_ref[...].astype(F32) + grad_b_ref[...].astype(F32)
    rgrad = cot_ref[...].astype(F32) + norm_back(unit, scale, summed * flat(gain_ref))
    agrad = rgrad.astype(BF16)
    agrad_ref[...] = agrad
    own_cg_ref[...] = mm(agrad, own_w_ref[...], NT).astype(BF16)
    far_cg_ref[...] = mm(agrad, far_w_ref[...], NT).astype(BF16)
    gather_rows(sum_ref, pl.program_id(0) == 0, rgrad, summed * unit, summed)


def middle(span, residual, grad_a, grad_b, cot, gain, own_w, far_w, carried=(), rider=None):
    tokens, d = residual.shape
    own = own_w.shape[1] // 4
    first, count = span
    tall, slim, near = rows(TILE, d, first), rows(TILE, own, first), rows(TILE, d)
    return call(
        middle_kernel, "second_norm_back", (count,),
        [tall, near, near, tall, whole((d,)), out_weights(own_w), out_weights(far_w)],
        [(tall, (tokens, d), BF16)] + [(slim, (tokens, own), BF16)] * 2 + [(whole((3, d)), (3, d), F32)],
        (residual, grad_a, grad_b, cot, gain, own_w, far_w), carried=carried, rider=rider,
    )


def output_kernel(residual_ref, mlp_a_ref, mlp_b_ref, b_down_ref, out_ref):
    out_ref[...] = (
        residual_ref[...].astype(F32)
        + ((mlp_a_ref[...].astype(F32) + mlp_b_ref[...].astype(F32)) + flat(b_down_ref))
    ).astype(BF16)


def output(residual, mlp_a, mlp_b, b_down):
    tokens, d = residual.shape
    tall = rows(TILE, d)
    return call(
        output_kernel, "block_output", (tokens // TILE,), [tall] * 3 + [whole((d,))],
        [(tall, (tokens, d), BF16)], (residual, mlp_a, mlp_b, b_down), cover=True,
    )[0]


def first_back_kernel(x_ref, grad_a_ref, grad_b_ref, rgrad_ref, gain_ref, *rest):
    unit, scale = norm_stats(x_ref[...].astype(F32))
    upstream = (grad_a_ref[...].astype(F32) + grad_b_ref[...].astype(F32)) * flat(gain_ref)
    rest[-1][...] = rgrad_ref[...].astype(F32) + norm_back(unit, scale, upstream)


def first_back(span, x, grad_a, grad_b, rgrad, gain, carried=()):
    tokens, d = x.shape
    first, count = span
    tall = rows(TILE // 2, d, 2 * first)
    return call(
        first_back_kernel, "first_norm_back", (2 * count,), [tall] * 4 + [whole((d,))],
        [(tall, (tokens, d), F32)], (x, grad_a, grad_b, rgrad, gain), carried=carried,
    )


def swap(value, axis, size, bit):
    return lax.ppermute(value, axis, [(i, i ^ bit) for i in range(size)])


def tie(value, *others):
    return lax.optimization_barrier((value,) + others)[0]


class ScatterSums:
    def __init__(self, size, *chains):
        self.size = size
        self.keeps, self.gives, bits = [list(part) for part in zip(*chains)]
        self.bits = [list(each) for each in bits]
        self.me = lax.axis_index("dp").astype(jnp.int32)

    def begin(self):
        bits = [each.pop(0) for each in self.bits]
        self.gots = [swap(give, "dp", self.size, 1 << bit) for give, bit in zip(self.gives, bits)]

    def rider(self, *others):
        self.gots = [tie(got, *others) if others else got for got in self.gots]
        mine = jnp.stack([(self.me >> bits[0]) & 1 for bits in self.bits])
        return Rider(mine, self.keeps, self.gots, len({bits[0] for bits in self.bits}) < len(self.bits))

    def take(self, results):
        self.keeps, self.gives = results[: len(self.keeps)], results[len(self.keeps) :]

    def end(self, *others):
        if self.bits[0]:
            self.take(call(alone_kernel, "merge", (1,), [], [], [], rider=self.rider(*others)))
        else:
            self.gots = [tie(got, *others) if others else got for got in self.gots]
        return self.gots

    def finish(self, *widths):
        while self.bits[0]:
            self.begin()
            self.end()
        return last_sum(self.keeps, self.gots, widths)


def body(
    n_dp,
    n_mp,
    block_input,
    segment_ids,
    group_ids,
    padding,
    ln1_gain,
    ln1_bias,
    w_qkv,
    b_qv,
    w_out,
    b_out,
    ln2_gain,
    ln2_bias,
    w_up,
    b_up,
    w_down,
    b_down,
    cotangent,
):
    tokens, d = block_input.shape
    sequences, length = segment_ids.shape
    own = w_qkv.shape[2]
    far = lambda value: swap(value, "mp", n_mp, 2)
    near = lambda value: swap(value, "mp", n_mp, 1)
    levels = n_dp.bit_length() - 1
    bits = list(range(levels))
    other_bits = [1, 0] + bits[2:]
    me = lax.axis_index("dp").astype(jnp.int32)
    halves = jnp.stack([me & 1, (me >> 1) & 1])
    orders = (chunk_order(n_dp, bits), chunk_order(n_dp, other_bits))

    small = jnp.stack([b_up, jnp.pad(b_qv.reshape(-1), (0, d - 2 * own))])
    parts = []
    for _ in range(3):
        parts.append(lax.reduce_precision(small, 8, 7))
        small = small - parts[-1]
    small = jnp.pad(jnp.stack(parts, 1).reshape(6, d).astype(BF16), ((0, 10), (0, 0)))
    pack = jnp.concatenate([jnp.transpose(w_qkv, (1, 2, 0)).reshape(3 * own, d), w_out, small], 0)
    pack_far = far(pack)
    table = tables(segment_ids, group_ids, padding)

    *saved_own, n1 = attend_own(table, block_input, ln1_gain, ln1_bias, pack, b_qv)
    ctx_own = saved_own[0]
    cot_down, sum_cot, mlp_own = upstream(tie(cotangent, n1), w_up, w_down)
    mlp_far = far(mlp_own)
    parts, saved_far = [], ()
    for s in range(sequences):
        *saved_far, part = attend_far(s, table, n1, tie(pack_far, cot_down), ctx_own, pack, saved_far)
        parts.append((part, near(part)))
    carried, sums_up = (), []
    for s, (part, other) in enumerate(parts):
        other = tie(other, carried[0] if carried else parts[-1][0])
        weights = (orders, halves, cotangent) if s == sequences - 1 else ()
        *carried, = hidden_own(
            s, length, block_input, part, other, b_out, ln2_gain, ln2_bias, w_up, b_up, cot_down, carried[:4], weights
        )
        sums_up.append(carried[4])
    residual, n2, hidden, upg, _, up_keep, up_give, down_keep, down_give = carried
    sum_mlp = ScatterSums(n_dp, (up_keep, up_give, bits), (down_keep, down_give, other_bits))
    sum_mlp.begin()
    mlp_far = tie(mlp_far, up_keep)
    tiles = tokens // TILE
    shares, mlp, gate, rider = [], (), (up_keep,), None
    for span in ((0, tiles - 1), (tiles - 1, 1)):
        results = products(
            span, tie(n2, *gate), cotangent, hidden, upg, w_up, w_down, mlp_far, pack_far, mlp, rider
        )
        *mlp, n2g = results[:2]
        shares.append((span, n2g, near(n2g)))
        if rider:
            sum_mlp.take(results[2:])
        else:
            gate, rider = (n2g,), sum_mlp.rider(n2g)
    sum_mlp.begin()
    gate, carried, sums_mid, rider = (n2g,), (), [], None
    for span, n2g, other in shares:
        results = middle(
            span, residual, n2g, tie(other, *gate), cotangent, ln2_gain, pack, pack_far, carried, rider
        )
        *carried, sum_mid = results[:4]
        sums_mid.append(sum_mid)
        if rider:
            sum_mlp.take(results[4:])
        else:
            gate, rider = (carried[0],), sum_mlp.rider(sum_mid)
    sum_mlp.begin()
    agrad, cgrad_own, cgrad_far = carried
    ctx, lse, q, k, v = saved_own
    *own_grads, keep, give, sum_qv = attend_own_back(
        table, halves[:1], orders[0], q, k, v, ctx, cgrad_own, lse, n1, agrad
    )
    mlp_near = near(mlp[0])
    sum_attn = ScatterSums(n_dp, (keep, give, bits))
    sum_attn.begin()
    got = sum_mlp.end(keep)
    up_sum, down_sum = sum_mlp.finish(up_keep.shape[2], up_keep.shape[2])
    ctx, lse, q, k, v = saved_far
    n1g, sum_first = attend_far_back(
        table, q, k, v, ctx, tie(cgrad_far, keep, *got), lse, block_input, own_grads, pack, pack_far
    )
    sum_first = sum_first + near(sum_first)
    n1g_near = near(tie(n1g, sum_first))
    got = sum_attn.end(n1g)
    sum_attn.begin()
    add = lambda values: functools.reduce(jnp.add, values)
    wide_qv = jnp.concatenate([sum_qv.reshape(1, -1), jnp.zeros((1, d - 2 * own), F32)], 1)
    sums = jnp.concatenate([sum_first, add(sums_mid), sum_cot, add(sums_up), wide_qv], 0)
    other = swap(sums, "dp", n_dp, 1)
    block_output = output(tie(residual, n1g, *got, sums), mlp[0], mlp_near, b_down)
    sums = sums + tie(other, block_output)
    other = swap(sums, "dp", n_dp, 2)
    got = sum_attn.end(block_output, sums)
    sum_attn.begin()
    outputs = first_back((0, tiles - 1), block_input, n1g, tie(n1g_near, block_output, *got, sums), agrad, ln1_gain)
    sums = sums + tie(other, *outputs)
    if levels > 2:
        other = swap(sums, "dp", n_dp, 4)
    got = sum_attn.end(*outputs)
    qkv_sum, out_sum = sum_attn.finish(3 * own, own)
    input_grad, = first_back((tiles - 1, 1), block_input, n1g, tie(n1g_near, sums, qkv_sum), agrad, ln1_gain, outputs)
    if levels > 2:
        sums = sums + tie(other, input_grad)
    for bit in range(3, levels):
        sums = sums + swap(sums, "dp", n_dp, 1 << bit)

    piece, tiny = d // n_dp, own // n_dp
    mine = lax.dynamic_slice(sums, (0, me * piece), (sums.shape[0] - 1, piece))
    vectors = [mine[i] for i in range(7)]
    return (
        block_output,
        input_grad,
        vectors[0],
        vectors[1],
        qkv_sum.reshape(piece, 3, own),
        lax.dynamic_slice(sums[7, : 2 * own].reshape(2, own), (0, me * tiny), (2, tiny)),
        out_sum.T,
        vectors[2],
        vectors[3],
        vectors[4],
        up_sum,
        vectors[6],
        down_sum.T,
        vectors[5],
    )


def solution(mesh):
    return jax.shard_map(
        functools.partial(body, mesh.shape["dp"], mesh.shape["mp"]),
        mesh=mesh,
        in_specs=(
            P("dp", None),
            P("dp", None),
            P("dp", None),
            P("dp", None),
            P(),
            P(),
            P(None, None, "mp"),
            P(None, "mp"),
            P("mp", None),
            P(),
            P(),
            P(),
            P(None, "mp"),
            P("mp"),
            P("mp", None),
            P(),
            P("dp", None),
        ),
        out_specs=(
            P("dp", None),
            P("dp", None),
            P("dp"),
            P("dp"),
            P("dp", None, "mp"),
            P(None, ("mp", "dp")),
            P("mp", "dp"),
            P("dp"),
            P("dp"),
            P("dp"),
            P("dp", "mp"),
            P(("mp", "dp")),
            P("mp", "dp"),
            P("dp"),
        ),
        check_vma=False,
    )
```

```python
import functools

import jax
import jax.numpy as jnp
from jax import lax
from jax.experimental import pallas as pl
from jax.experimental.pallas import tpu as pltpu
from jax.sharding import PartitionSpec as P

HD = 64
QB = 128
GRAIN = 64
GRAIN_BITS = 6
GROUP = 2
BACK_GROUP = 2
LONGEST = 256
FREE = dict(
    masks=(), attend_own=(), attend_far=(3, 4, 7), attend_own_back=(7, 10), attend_far_back=(9, 10, 11), upstream=(),
    hidden_own=(1, 2, 8), feed_forward=(4, 5, 6), second_norm_back=(1, 2), block_output=(), first_norm_back=(1, 2),
    merge=range(99), last_sum=range(99),
)
GRANTS = dict(
    masks=4, attend_own=20, attend_far=14, attend_own_back=28, attend_far_back=34, upstream=12, hidden_own=34,
    feed_forward=22, second_norm_back=17, block_output=8, first_norm_back=14, merge=6, last_sum=4,
)
TILE = 512
COVER = 10**12
MASKED = -1e30
EPS = 1e-05
LOG2E = 1.4426950408889634
F32 = jnp.float32
BF16 = jnp.bfloat16
NT = (((1,), (1,)), ((), ()))
NN = (((1,), (0,)), ((), ()))
TN = (((0,), (0,)), ((), ()))


def mm(a, b, dims):
    return lax.dot_general(a, b, dims, preferred_element_type=F32)


def flat(ref):
    return ref[...].reshape(1, -1)


def hosted(kernel, own, taken, carried, given, rider, *refs):
    refs = list(refs[own:])
    cut = lambda count: [refs.pop(0) for _ in range(count)]
    main_in, rider_in, kept, main_out, rider_out = map(cut, (taken, len(rider.args), carried, given, len(rider.out)))
    kernel(*main_in, *kept, *main_out, *refs)

    @pl.when(pl.program_id(0) == 0)
    def _():
        rider.body(rider_in, rider_out)


def call(kernel, name, grid, in_specs, out, args, scratch=(), prefetch=0, carried=(), cover=False, carried_specs=(), rider=None):
    in_specs, out, args = list(in_specs), list(out), list(args)
    pinned = lambda at: at >= prefetch and args[at].size >= 1 << 17 and at not in FREE[name]
    args = [pltpu.with_memory_space_constraint(arg, pltpu.HBM) if pinned(at) else arg for at, arg in enumerate(args)]
    if rider:
        first = [] if rider.halves is None else [rider.halves]
        kernel = functools.partial(hosted, kernel, len(first), len(args), len(carried), len(out), rider)
        in_specs, out, args, prefetch = in_specs + rider.specs, out + rider.out, first + args + rider.args, prefetch + len(first)
    return pl.pallas_call(
        kernel,
        grid_spec=pltpu.PrefetchScalarGridSpec(
            num_scalar_prefetch=prefetch,
            grid=grid,
            in_specs=in_specs + list(carried_specs or [pl.BlockSpec(memory_space=pl.ANY)] * len(carried)),
            out_specs=[entry[0] for entry in out],
            scratch_shapes=list(scratch),
        ),
        out_shape=[pltpu.HBM(*entry[1:3]) if entry[3:] else jax.ShapeDtypeStruct(*entry[1:3]) for entry in out],
        input_output_aliases={len(args) + i: i for i in range(len(carried))},
        compiler_params=pltpu.CompilerParams(vmem_limit_bytes=GRANTS[name] * 1024 * 1024),
        cost_estimate=pl.CostEstimate(flops=COVER if cover else 0, bytes_accessed=1024, transcendentals=0),
        name=name,
    )(*args, *carried)


def whole(shape):
    return pl.BlockSpec(shape, lambda *ids: (0,) * len(shape))


def rows(tile, width, skip=0):
    return pl.BlockSpec((tile, width), lambda i, *rest: (i + skip, 0))


def norm_stats(values):
    average = jnp.mean(values, -1, keepdims=True)
    centered = values - average
    variance = jnp.mean(centered * centered, -1, keepdims=True)
    scale = lax.rsqrt(variance + EPS)
    return centered * scale, scale


def norm_back(unit, scale, upstream):
    first = jnp.mean(upstream, -1, keepdims=True)
    second = jnp.mean(upstream * unit, -1, keepdims=True)
    return scale * (upstream - first - unit * second)


def total(values):
    return jnp.sum(values.astype(F32), 0, keepdims=True)


def gather_rows(ref, first, *values):
    @pl.when(first)
    def _():
        ref[...] = jnp.zeros_like(ref)

    for at, value in enumerate(values):
        ref[at : at + 1, :] += total(value)


def masks_kernel(segment_ref, group_ref, padding_ref, bounds_ref, code_ref):
    sequences, length = segment_ref.shape
    blocks = length // QB
    low = segment_ref[...] * 4
    high = low + group_ref[...]
    codes = jnp.where(padding_ref[...] == 0, high, -1)
    place = lax.broadcasted_iota(jnp.int32, (1, sequences * blocks), 1)
    key_from = jnp.zeros((1, sequences * blocks), jnp.int32)
    key_to = jnp.zeros((1, sequences * blocks), jnp.int32)
    for s in range(sequences):
        for at, rows_of in enumerate((codes, low, high)):
            code_ref[s, at : at + 1, :] = rows_of[s : s + 1, :]
        row = segment_ref[s : s + 1, :]
        for block in range(blocks):
            earliest = row[:, block * QB : block * QB + 1]
            latest = row[:, (block + 1) * QB - 1 : (block + 1) * QB]
            before = jnp.sum((row < earliest).astype(F32), 1, keepdims=True).astype(jnp.int32)
            until = jnp.sum((row <= latest).astype(F32), 1, keepdims=True).astype(jnp.int32)
            here = place == s * blocks + block
            key_from = jnp.where(here, before, key_from)
            key_to = jnp.where(here, until, key_to)
    key_from = key_from & -16
    grains = jnp.maximum((key_to - key_from + (GRAIN - 1)) >> GRAIN_BITS, QB // GRAIN)
    bounds_ref[0:1, :] = jnp.minimum(key_from, length - grains * GRAIN)
    bounds_ref[1:2, :] = grains


def tables(segment_ids, group_ids, padding):
    sequences, length = segment_ids.shape
    bounds = (2, sequences * (length // QB))
    codes = (sequences, 3, length)
    return call(
        masks_kernel, "masks", (1,), [whole(segment_ids.shape)] * 3,
        [(whole(bounds), bounds, jnp.int32), (whole(codes), codes, jnp.int32)], (segment_ids, group_ids, padding),
    )


def extents(length):
    most = min(QB + 2 * LONGEST, length) // GRAIN
    return [extent for extent in (3, 4, 5, 6, 8) if extent < most] + [most]


def head_groups(width):
    return [slice(at, min(at + 2 * HD, width)) for at in range(0, width, 2 * HD)]


def stack_heads(values):
    if values.shape[1] == HD:
        return values
    lane = lax.broadcasted_iota(jnp.int32, values.shape, 1)
    zero = jnp.zeros_like(values)
    return jnp.concatenate(
        [jnp.where(lane < HD, values, zero), jnp.where(lane >= HD, values, zero)], 0
    )


def join_heads(values):
    if values.shape[1] == HD:
        return values
    lane = lax.broadcasted_iota(jnp.int32, (QB, 2 * HD), 1)
    return jnp.where(lane < HD, values[:QB], values[QB:])


def spread_codes(code_ref, column_ref):
    for at in range(0, column_ref.shape[0], QB):
        column_ref[at : at + QB, :] = jnp.broadcast_to(code_ref[0:1, at : at + QB], (QB, QB)).T


def mask_bias(column_ref, code_ref, start, extent, block):
    mine = pl.ds(pl.multiple_of(block * QB, QB), QB)
    codes = column_ref[pl.ds(start, extent), :]
    shape = (extent, QB)
    apart = lax.broadcasted_iota(jnp.int32, shape, 0) - lax.broadcasted_iota(jnp.int32, shape, 1)
    allowed = ((codes >= code_ref[1:2, mine]) & (codes <= code_ref[2:3, mine])) | (
        apart == block * QB - start
    )
    return jnp.where(allowed, jnp.float32(0), jnp.float32(MASKED))


def widen(bias, cols):
    return jnp.concatenate([bias, bias], 1) if cols.stop - cols.start > HD else bias


def each_block(bound_ref, length, group, sequence, run):
    turns = length // QB // group

    def step(turn, carry):
        place = (sequence * turns + turn) * group
        grains = functools.reduce(jnp.maximum, [bound_ref[1, place + i] for i in range(group)])
        blocks = [turn * group + i for i in range(group)]
        least = 0
        for extent in extents(length):
            starts = [
                pl.multiple_of(jnp.minimum(bound_ref[0, place + i], length - extent * GRAIN), 16) for i in range(group)
            ]
            pl.when((grains > least) & (grains <= extent))(functools.partial(run, extent * GRAIN, blocks, starts))
            least = extent
        return carry

    lax.fori_loop(0, turns, step, 0)


def project(normed, wt_ref, q_bias, v_bias, q_ref, k_ref, v_ref):
    own = q_ref.shape[1]
    q_ref[...] = (mm(normed, wt_ref[:own, :], NT) + q_bias).astype(BF16)
    k_ref[...] = mm(normed, wt_ref[own : 2 * own, :], NT).astype(BF16)
    v_ref[...] = (mm(normed, wt_ref[2 * own :, :], NT) + v_bias).astype(BF16)


def attend(sequence, bound_ref, code_ref, column_ref, q_ref, k_ref, v_ref, ctx_ref, lse_ref):
    length, width = q_ref.shape
    heads = head_groups(width)
    spread_codes(code_ref, column_ref)

    def run(extent, blocks, starts):
        units, scores, probs, totals, biases = [], [], [], [], []
        for i, (block, start) in enumerate(zip(blocks, starts)):
            here = pl.ds(start, extent)
            mine = pl.ds(pl.multiple_of(block * QB, QB), QB)
            for p, cols in enumerate(heads):
                units.append((i, block, here, mine, p, cols))
                scores.append(mm(k_ref[here, cols], stack_heads(q_ref[mine, cols]), NT))
            biases.append(mask_bias(column_ref, code_ref, start, extent, block))
        for (i, block, here, mine, p, cols), score in zip(units, scores):
            score = score * (0.125 * LOG2E) + widen(biases[i], cols)
            top = jnp.max(score, 0, keepdims=True)
            weights = jnp.exp2(score - top)
            summed = jnp.sum(weights, 0, keepdims=True)
            lse_ref[block, p : p + 1, : score.shape[1]] = top + jnp.log2(summed)
            totals.append(1.0 / summed)
            probs.append(weights.astype(BF16))
        for (i, block, here, mine, p, cols), prob, scale in zip(units, probs, totals):
            turned = v_ref[here, cols].T
            both = [
                mm(turned[at * HD : (at + 1) * HD], prob[:, at * QB : (at + 1) * QB], NN)
                * scale[:, at * QB : (at + 1) * QB]
                for at in range(prob.shape[1] // QB)
            ]
            ctx_ref[mine, cols] = jnp.concatenate(both, 0).T.astype(BF16)

    each_block(bound_ref, length, GROUP, sequence, run)


def begin_copies(pairs, sems):
    copies = [pltpu.make_async_copy(source, target, sems.at[at]) for at, (source, target) in enumerate(pairs)]
    for copy in copies:
        copy.start()

    def finish():
        for copy in copies:
            copy.wait()

    return finish


def own_kernel(
    bound_ref, code_ref, x_ref, gain_ref, bias_ref, wt_ref, qv_ref,
    ctx_ref, lse_ref, q_hbm, k_hbm, v_hbm, n1_hbm, column_ref, q_ref, k_ref, v_ref, n1_ref, sems,
):
    length = x_ref.shape[0]
    here = pl.ds(pl.multiple_of(pl.program_id(0) * length, length), length)
    chunks = [pl.ds(at, length // 4) for at in range(0, length, length // 4)]

    def norm(chunk):
        unit, _ = norm_stats(x_ref[chunk, :].astype(F32))
        n1_ref[chunk, :] = (unit * flat(gain_ref) + flat(bias_ref)).astype(BF16)

    norm(chunks[0])
    for at, chunk in enumerate(chunks):
        for following in chunks[at + 1 : at + 2]:
            norm(following)
        project(
            n1_ref[chunk, :], wt_ref, qv_ref[0:1, :], qv_ref[1:2, :], *(ref.at[chunk] for ref in (q_ref, k_ref, v_ref))
        )
    finish = begin_copies(
        [(q_ref, q_hbm.at[here]), (k_ref, k_hbm.at[here]), (v_ref, v_hbm.at[here]), (n1_ref, n1_hbm.at[here])], sems
    )
    attend(pl.program_id(0), bound_ref, code_ref, column_ref, q_ref, k_ref, v_ref, ctx_ref, lse_ref)
    finish()


STAY = pl.BlockSpec(memory_space=pl.ANY)


def attention_outs(tokens, width, length, sequences, skip=0):
    tall = rows(length, width, skip)
    lse = (length // QB, 8, 2 * QB)
    return [
        (tall, (tokens, width), BF16, True),
        (pl.BlockSpec(lse, lambda s, *ids: (s + skip, 0, 0)), (sequences * lse[0],) + lse[1:], F32, True),
    ] + [(STAY, (tokens, width), BF16, True)] * 3


def attention_scratch(length, width):
    return [pltpu.VMEM((length, QB), jnp.int32)] + [pltpu.VMEM((length, width), BF16)] * 3


def projections(pack):
    return pl.BlockSpec((pack.shape[1] // 4 * 3, pack.shape[1]), lambda *ids: (0, 0))


def out_weights(pack):
    return pl.BlockSpec((pack.shape[1] // 4, pack.shape[1]), lambda *ids: (3, 0))


def biases(pack):
    return pl.BlockSpec((16, pack.shape[1]), lambda *ids: (pack.shape[1] // 16, 0))


def bias_of(ref, which):
    part = [ref[3 * which + at : 3 * which + at + 1, :].astype(F32) for at in range(3)]
    return part[0] + (part[1] + part[2])


def codes_spec(codes, skip=0):
    return pl.BlockSpec((None,) + codes.shape[1:], lambda s, *ids: (s + skip, 0, 0))


def attend_own(table, x, gain, bias, wt, b_qv):
    bounds, codes = table
    tokens, d = x.shape
    sequences, _, length = codes.shape
    return call(
        own_kernel, "attend_own", (sequences,),
        [codes_spec(codes), rows(length, d), whole(gain.shape), whole(bias.shape), projections(wt), whole(b_qv.shape)],
        attention_outs(tokens, b_qv.shape[1], length, sequences) + [(STAY, (tokens, d), BF16, True)],
        (bounds, codes, x, gain, bias, wt, b_qv),
        scratch=attention_scratch(length, b_qv.shape[1])
        + [pltpu.VMEM((length, d), BF16), pltpu.SemaphoreType.DMA((4,))],
        prefetch=1,
    )


def far_kernel(
    sequence, bound_ref, code_ref, n1_ref, wt_ref, bias_ref, own_ctx_hbm, pack_hbm, far_hbm, *rest
):
    ctx_ref, lse_ref, q_hbm, k_hbm, v_hbm, part_ref = rest[-14:-8]
    column_ref, q_ref, k_ref, v_ref, own_ctx_ref, own_w_ref, far_w_ref, sems = rest[-8:]
    length, own = q_ref.shape
    here = pl.ds(sequence * length, length)
    weights = pl.ds(3 * own, own)
    late = begin_copies(
        [
            (own_ctx_hbm.at[here], own_ctx_ref),
            (pack_hbm.at[weights], own_w_ref),
            (far_hbm.at[weights], far_w_ref),
        ],
        sems.at[pl.ds(0, 3)],
    )
    bias = bias_of(bias_ref, 1)
    project(n1_ref[...], wt_ref, bias[:, :own], bias[:, own : 2 * own], q_ref, k_ref, v_ref)
    finish = begin_copies(
        [(q_ref, q_hbm.at[here]), (k_ref, k_hbm.at[here]), (v_ref, v_hbm.at[here])], sems.at[pl.ds(3, 3)]
    )
    attend(sequence, bound_ref, code_ref, column_ref, q_ref, k_ref, v_ref, ctx_ref, lse_ref)
    late()
    part_ref[...] = (
        mm(own_ctx_ref[...], own_w_ref[...], NN) + mm(ctx_ref[...], far_w_ref[...], NN)
    ).astype(BF16)
    finish()


def attend_far(sequence, table, n1, far, own_ctx, pack, carried=()):
    bounds, codes = table
    tokens, d = n1.shape
    sequences, _, length = codes.shape
    own = own_ctx.shape[1]
    return call(
        functools.partial(far_kernel, sequence), "attend_far", (1,),
        [codes_spec(codes, sequence), rows(length, d, sequence), projections(far), biases(far)] + [STAY] * 3,
        attention_outs(tokens, own, length, sequences, sequence) + [(rows(length, d), (length, d), BF16)],
        (bounds, codes, n1, far, far, own_ctx, pack, far),
        scratch=attention_scratch(length, own)
        + [pltpu.VMEM((length, own), BF16)]
        + [pltpu.VMEM((own, d), BF16)] * 2
        + [pltpu.SemaphoreType.DMA((6,))],
        prefetch=1, carried=carried,
    )


def attend_back(
    bound_ref, code_ref, column_ref, q_ref, k_ref, v_ref, ctx_ref, grad_ref, lse_ref,
    dq_ref, dk_ref, dv_ref, dk_acc, dv_acc,
):
    length, width = q_ref.shape
    heads = head_groups(width)
    spread_codes(code_ref, column_ref)
    dk_acc[...] = jnp.zeros_like(dk_acc)
    dv_acc[...] = jnp.zeros_like(dv_acc)

    def run(extent, blocks, starts):
        units, stacked, upstream, scores, grads, biases = [], [], [], [], [], []
        for i, (block, start) in enumerate(zip(blocks, starts)):
            here = pl.ds(start, extent)
            mine = pl.ds(pl.multiple_of(block * QB, QB), QB)
            for p, cols in enumerate(heads):
                units.append((i, block, here, mine, p, cols))
                stacked.append(stack_heads(q_ref[mine, cols]))
                upstream.append(stack_heads(grad_ref[mine, cols]))
                scores.append(mm(k_ref[here, cols], stacked[-1], NT))
                grads.append(mm(v_ref[here, cols], upstream[-1], NT))
            biases.append(mask_bias(column_ref, code_ref, start, extent, block))
        probs, score_grads = [], []
        for (i, block, here, mine, p, cols), score, grad in zip(units, scores, grads):
            turned = (ctx_ref[mine, cols].astype(F32) * grad_ref[mine, cols].astype(F32)).T
            delta = jnp.concatenate(
                [
                    jnp.sum(turned[at : at + HD], 0, keepdims=True)
                    for at in range(0, turned.shape[0], HD)
                ],
                1,
            )
            weights = jnp.exp2(
                score * (0.125 * LOG2E) + widen(biases[i], cols) - lse_ref[block, p : p + 1, : score.shape[1]]
            )
            probs.append(weights.astype(BF16))
            score_grads.append((weights * (grad - delta)).astype(BF16))
        for n, (i, block, here, mine, p, cols) in enumerate(units):
            dv_acc[here, cols] += mm(probs[n], upstream[n], NN)
            dk_acc[here, cols] += mm(score_grads[n], stacked[n], NN)
            dq = join_heads(mm(score_grads[n], k_ref[here, cols], TN))
            dq_ref[mine, cols] = (dq * 0.125).astype(BF16)

    each_block(bound_ref, length, BACK_GROUP, pl.program_id(0), run)
    dk_ref[...] = (dk_acc[...] * 0.125).astype(BF16)
    dv_ref[...] = dv_acc[...].astype(BF16)


def own_back_kernel(
    order, bound_ref, half_ref, code_ref, q_ref, k_ref, v_ref, ctx_ref, grad_ref, lse_ref, n1_hbm, agrad_hbm,
    dq_ref, dk_ref, dv_ref, keep_ref, give_ref, sum_ref, dk_acc, dv_acc, column_ref, weight_acc, n1_ref, agrad_ref, sems,
):
    length = q_ref.shape[0]
    here = pl.ds(pl.multiple_of(pl.program_id(0) * length, length), length)
    late = begin_copies([(n1_hbm.at[here], n1_ref), (agrad_hbm.at[here], agrad_ref)], sems)
    attend_back(
        bound_ref, code_ref, column_ref, q_ref, k_ref, v_ref, ctx_ref, grad_ref, lse_ref,
        dq_ref, dk_ref, dv_ref, dk_acc, dv_acc,
    )
    first = pl.program_id(0) == 0

    @pl.when(first)
    def _():
        weight_acc[...] = jnp.zeros_like(weight_acc)
        sum_ref[...] = jnp.zeros_like(sum_ref)

    own = dq_ref.shape[1]
    late()
    normed = n1_ref[...]
    for at, grad in enumerate((dq_ref, dk_ref, dv_ref)):
        weight_acc[:, at * own : (at + 1) * own] += mm(normed, grad[...], TN)
    weight_acc[:, 3 * own :] += mm(agrad_ref[...], ctx_ref[...], TN)
    sum_ref[0:1, :] += total(dq_ref[...])
    sum_ref[1:2, :] += total(dv_ref[...])

    @pl.when(pl.program_id(0) == pl.num_programs(0) - 1)
    def _():
        split_chunks(half_ref[0], order, weight_acc, keep_ref, give_ref)


def attend_own_back(table, half, order, q, k, v, ctx, grad, lse, n1, agrad):
    bounds, codes = table
    tokens, d = n1.shape
    own = q.shape[1]
    sequences, _, length = codes.shape
    tall = rows(length, own)
    lse_spec = pl.BlockSpec((length // QB, 8, 2 * QB), lambda s, *ids: (s, 0, 0))
    count = len(order[0])
    chunk = (count, d // (2 * count), 4 * own)
    return call(
        functools.partial(own_back_kernel, order), "attend_own_back", (sequences,),
        [codes_spec(codes)] + [tall] * 5 + [lse_spec, STAY, STAY],
        [(tall, (tokens, own), BF16)] * 3 + [(whole(chunk), chunk, BF16)] * 2 + [(whole((2, own)), (2, own), F32)],
        (bounds, half, codes, q, k, v, ctx, grad, lse, n1, agrad),
        scratch=[pltpu.VMEM((length, own), F32)] * 2
        + [pltpu.VMEM((length, QB), jnp.int32), pltpu.VMEM((d, 4 * own), F32)]
        + [pltpu.VMEM((length, d), BF16)] * 2
        + [pltpu.SemaphoreType.DMA((2,))],
        prefetch=2, cover=True,
    )


def far_back_kernel(
    bound_ref, code_ref, q_ref, k_ref, v_ref, ctx_ref, grad_ref, lse_ref,
    x_hbm, aq_hbm, ak_hbm, av_hbm, wa_hbm, wb_hbm,
    n1g_ref, sum_ref, dk_acc, dv_acc, column_ref, dq_ref, dk_ref, dv_ref,
    x_ref, aq_ref, ak_ref, av_ref, wa_ref, wb_ref, sems,
):
    length = q_ref.shape[0]
    here = pl.ds(pl.multiple_of(pl.program_id(0) * length, length), length)
    first = pl.ds(0, wa_ref.shape[0])
    late = begin_copies(
        [
            (aq_hbm.at[here], aq_ref),
            (ak_hbm.at[here], ak_ref),
            (av_hbm.at[here], av_ref),
            (wa_hbm.at[first], wa_ref),
            (wb_hbm.at[first], wb_ref),
            (x_hbm.at[here], x_ref),
        ],
        sems,
    )
    attend_back(
        bound_ref, code_ref, column_ref, q_ref, k_ref, v_ref, ctx_ref, grad_ref, lse_ref,
        dq_ref, dk_ref, dv_ref, dk_acc, dv_acc,
    )
    own = aq_ref.shape[1]
    late()
    grad = None
    for w_ref, grads in ((wa_ref, (aq_ref, ak_ref, av_ref)), (wb_ref, (dq_ref, dk_ref, dv_ref))):
        for place, one_ref in enumerate(grads):
            here = mm(one_ref[...], w_ref[place * own : (place + 1) * own, :], NN)
            grad = here if grad is None else grad + here
    n1g_ref[...] = grad.astype(BF16)
    unit, _ = norm_stats(x_ref[...].astype(F32))
    gather_rows(sum_ref, pl.program_id(0) == 0, grad * unit, grad)


def attend_far_back(table, q, k, v, ctx, grad, lse, x, own_grads, own_wt, far_wt, rider):
    bounds, codes = table
    tokens, d = x.shape
    own = q.shape[1]
    sequences, _, length = codes.shape
    tall, high = rows(length, own), rows(length, d)
    lse_spec = pl.BlockSpec((length // QB, 8, 2 * QB), lambda s, *ids: (s, 0, 0))
    return call(
        far_back_kernel, "attend_far_back", (sequences,),
        [codes_spec(codes)] + [tall] * 5 + [lse_spec] + [STAY] * 6,
        [(high, (tokens, d), BF16), (whole((2, d)), (2, d), F32)],
        (bounds, codes, q, k, v, ctx, grad, lse, x, *own_grads, own_wt, far_wt),
        scratch=[pltpu.VMEM((length, own), F32)] * 2
        + attention_scratch(length, own)
        + [pltpu.VMEM((length, d), BF16)]
        + [pltpu.VMEM((length, own), BF16)] * 3
        + [pltpu.VMEM((3 * own, d), BF16)] * 2
        + [pltpu.SemaphoreType.DMA((6,))],
        prefetch=1, cover=True, rider=rider,
    )


def reversed_bits(value, count):
    return sum(((value >> i) & 1) << (count - 1 - i) for i in range(count))


def chunk_order(size, bits):
    inner = range(size // 2)
    spread = lambda low, at: sum(((low >> (len(bits) - 2 - i)) & 1) << bit for i, bit in enumerate(bits[1:])) | at << bits[0]
    return [[spread(low, at) for low in inner] for at in (0, 1)]


def split_chunks(half, order, terms, keep_ref, give_ref):
    piece = keep_ref.shape[1]

    def store(mine):
        for ref, devices in ((keep_ref, order[mine]), (give_ref, order[1 - mine])):
            for at, device in enumerate(devices):
                ref[at] = terms[device * piece : (device + 1) * piece, :].astype(BF16)

    for mine in (0, 1):
        pl.when(half == mine)(functools.partial(store, mine))


class Rider:
    def __init__(self, halves, keeps, gots, joint):
        self.halves, self.joint = halves, joint
        self.specs, self.out, self.args = [], [], []
        for chain, keep in enumerate(keeps):
            count, piece, width = keep.shape
            block = (count // 2, piece, width)
            base = 2 * chain if len(gots) < len(keeps) else 0
            got = gots[0 if base else min(chain, len(gots) - 1)]
            at = lambda mine, first, chain=chain: pl.BlockSpec(
                block, lambda i, ref, *ids: (first + (ref[chain] if mine else 1 - ref[chain]), 0, 0)
            )
            self.specs += [at(True, 0), at(True, base), at(False, 0), at(False, base)]
            self.out.append((whole(block), block, F32, True))
            self.args += [keep, got, keep, got]
        shape = (block[0] * len(keeps),) + block[1:]
        self.out += [(whole(shape), shape, BF16)] if joint else [(whole(block), block, BF16)] * len(keeps)

    def body(self, refs, out):
        chains = len(refs) // 4
        for chain in range(chains):
            keep_a, got_a, keep_b, got_b = refs[4 * chain : 4 * chain + 4]
            out[chain][...] = keep_a[...].astype(F32) + got_a[...].astype(F32)
            give = (keep_b[...].astype(F32) + got_b[...].astype(F32)).astype(BF16)
            if self.joint:
                size = give.shape[0]
                out[chains][chain * size : (chain + 1) * size] = give
            else:
                out[chains + chain][...] = give


def alone_kernel():
    pass


class LastRider:
    halves = None

    def __init__(self, keeps, gots):
        self.count, self.joint = len(keeps), len(gots) < len(keeps)
        self.args = [*keeps, *gots]
        self.specs = [whole(array.shape) for array in self.args]
        self.out = [(whole(keep.shape[1:]), keep.shape[1:], F32) for keep in keeps]

    def body(self, refs, out):
        last_sum_kernel(self.count, self.joint, *refs, *out)


def last_sum_kernel(count, joint, *refs):
    arrived = 1 if joint else count
    keeps, gots, out = refs[:count], refs[count : count + arrived], refs[count + arrived :]
    for chain in range(count):
        value = keeps[chain][0].astype(F32) + (gots[0][chain] if joint else gots[chain][0]).astype(F32)
        at = 0
        while at < value.shape[1]:
            out[0][...] = value[:, at : at + out[0].shape[1]]
            at += out[0].shape[1]
            out = out[1:]


def last_sum(keeps, gots, widths):
    piece = keeps[0].shape[1]
    arrays = [*keeps, *gots]
    return call(
        functools.partial(last_sum_kernel, len(keeps), len(gots) < len(keeps)), "last_sum", (1,),
        [whole(array.shape) for array in arrays],
        [(whole((piece, width)), (piece, width), F32) for width in widths], arrays,
    )


def gelu_parts(z):
    spread = jnp.exp2(z * z * (-0.5 * LOG2E))
    t = 1.0 / (1.0 + (0.3275911 * 0.7071067811865476) * jnp.abs(z))
    poly = t * (0.254829592 + t * (-0.284496736 + t * (1.421413741 + t * (-1.453152027 + t * 1.061405429))))
    tail = 0.5 * poly * spread
    return jnp.where(z >= 0, 1.0 - tail, tail), spread


def hidden_pair(z, hidden_grad):
    phi, spread = gelu_parts(z)
    return (z * phi).astype(BF16), hidden_grad * (phi + z * spread * 0.3989422804014327)


def upstream_kernel(cot_ref, down_ref, up_ref, out_ref, sum_ref, pack_hbm, sems):
    d = up_ref.shape[0]
    copies = [
        pltpu.make_async_copy(up_ref, pack_hbm.at[pl.ds(0, d)], sems.at[0]),
        pltpu.make_async_copy(down_ref, pack_hbm.at[pl.ds(d, down_ref.shape[0])], sems.at[1]),
    ]

    @pl.when(pl.program_id(0) == 0)
    def _():
        for copy in copies:
            copy.start()

    cot = cot_ref[...]
    out_ref[...] = mm(cot, down_ref[...], NT).astype(BF16)
    gather_rows(sum_ref, pl.program_id(0) == 0, cot)

    @pl.when(pl.program_id(0) == pl.num_programs(0) - 1)
    def _():
        for copy in copies:
            copy.wait()


def upstream(cot, up, down):
    tokens, d = cot.shape
    f = down.shape[0]
    tile = tokens // 4
    stay = pl.BlockSpec(memory_space=pl.ANY)
    return call(
        upstream_kernel, "upstream", (4,), [rows(tile, d), whole(down.shape), whole(up.shape)],
        [(rows(tile, f), (tokens, f), BF16), (whole((1, d)), (1, d), F32), (stay, (d + f, d), BF16, True)],
        (cot, down, up), scratch=[pltpu.SemaphoreType.DMA((2,))],
    )


def hidden_kernel(
    orders, x_ref, part_a_ref, part_b_ref, b_out_ref, gain_ref, bias_ref, up_ref, b_up_ref, cot_down_ref, *rest
):
    first = pl.program_id(0) == 0
    if orders:
        half_ref, cot_ref, rest_cot, rest = rest[0], rest[1], rest[2:3], rest[2:]
        earlier, rest = rest[1:-11], rest[-11:]
        up_keep_ref, up_give_ref, down_keep_ref, down_give_ref, up_acc, down_acc = rest[-6:]
        rest = rest[:-6]
    residual_ref, n2_ref, hidden_ref, upg_ref, sum_ref = rest[-5:]
    residual = (
        x_ref[...].astype(F32) + (part_a_ref[...].astype(F32) + part_b_ref[...].astype(F32)) + flat(b_out_ref)
    )
    residual_ref[...] = residual.astype(BF16)
    unit, _ = norm_stats(residual)
    normed = (unit * flat(gain_ref) + flat(bias_ref)).astype(BF16)
    n2_ref[...] = normed
    hidden, grad = hidden_pair(mm(normed, up_ref[...], NN) + flat(b_up_ref), cot_down_ref[...].astype(F32))
    up_grad = grad.astype(BF16)
    hidden_ref[...] = hidden
    upg_ref[...] = up_grad
    gather_rows(sum_ref, first, grad)
    if not orders:
        return

    @pl.when(first)
    def _():
        up_acc[...] = jnp.zeros_like(up_acc)
        down_acc[...] = jnp.zeros_like(down_acc)

    if earlier:
        n2_old, hidden_old, upg_old, cot_old = earlier[-3:] + rest_cot
        both = lambda one, two: jnp.concatenate([one, two], 0)
        up_acc[...] += mm(both(n2_old[...], normed), both(upg_old[...], up_grad), TN)
        down_acc[...] += mm(both(cot_old[...], cot_ref[...]), both(hidden_old[...], hidden), TN)
    else:
        up_acc[...] += mm(normed, up_grad, TN)
        down_acc[...] += mm(cot_ref[...], hidden, TN)

    @pl.when(pl.program_id(0) == pl.num_programs(0) - 1)
    def _():
        split_chunks(half_ref[0], orders[0], up_acc, up_keep_ref, up_give_ref)
        split_chunks(half_ref[1], orders[1], down_acc, down_keep_ref, down_give_ref)


def hidden_own(sequence, length, x, part_a, part_b, b_out, gain, bias, up, b_up, cot_down, carried=(), weights=()):
    tokens, d = x.shape
    f = up.shape[1]
    count = 4
    tile = length // count
    tall, wide = rows(tile, d, count * sequence), rows(tile, f, count * sequence)
    near = rows(tile, d)
    specs = [tall, near, near] + [whole((d,))] * 3 + [whole(up.shape), whole((f,)), wide]
    out = [(tall, (tokens, d), BF16, True)] * 2 + [(wide, (tokens, f), BF16, True)] * 2 + [(whole((1, f)), (1, f), F32)]
    args = [x, part_a, part_b, b_out, gain, bias, up, b_up, cot_down]
    orders, scratch, earlier = None, [], ()
    if weights:
        orders, halves, cot = weights
        half_count = len(orders[0][0])
        chunk = (half_count, d // (2 * half_count), f)
        specs += [pl.BlockSpec(memory_space=pltpu.SMEM), tall]
        args += [halves, cot]
        specs.append(rows(tile, d))
        args.append(cot)
        earlier = [pl.BlockSpec(memory_space=pl.ANY), rows(tile, d), rows(tile, f), rows(tile, f)]
        out += [(whole(chunk), chunk, BF16)] * 4
        scratch = [pltpu.VMEM((d, f), F32)] * 2
    return call(
        functools.partial(hidden_kernel, orders), "hidden_own", (count,), specs, out, args, scratch=scratch, carried=carried,
        carried_specs=earlier,
    )


def products_kernel(
    n2_ref, cot_ref, hidden_ref, upg_ref, up_a_ref, down_a_ref, far_ref, bias_ref, *rest
):
    mlp_ref, n2g_ref = rest[-2:]
    d = n2_ref.shape[1]
    up_b, down_b = far_ref[:d, :], far_ref[d:, :]
    z = mm(n2_ref[...], up_b, NN) + bias_of(bias_ref, 0)
    hidden_grad = mm(cot_ref[...], down_b, NT)
    mlp_own = mm(hidden_ref[...], down_a_ref[...], NN)
    n2g_own = mm(upg_ref[...], up_a_ref[...], NT)
    hidden, grad = hidden_pair(z, hidden_grad)
    mlp_ref[...] = (mlp_own + mm(hidden, down_b, NN)).astype(BF16)
    n2g_ref[...] = (n2g_own + mm(grad.astype(BF16), up_b, NT)).astype(BF16)


def products(span, n2, cot, hidden, upg, up, down, far, bias, carried=(), rider=None):
    tokens = n2.shape[0]
    d, f = up.shape
    first, count = span
    tall, wide = rows(TILE, d, first), rows(TILE, f, first)
    return call(
        products_kernel, "feed_forward", (count,),
        [tall, tall, wide, wide, whole(up.shape), whole(down.shape), whole(far.shape), biases(bias)],
        [(tall, (tokens, d), BF16, True), (rows(TILE, d), (count * TILE, d), BF16)],
        (n2, cot, hidden, upg, up, down, far, bias), carried=carried, cover=True, rider=rider,
    )


def middle_kernel(residual_ref, grad_a_ref, grad_b_ref, cot_ref, gain_ref, own_w_ref, far_w_ref, *rest):
    agrad_ref, own_cg_ref, far_cg_ref, sum_ref = rest[-4:]
    unit, scale = norm_stats(residual_ref[...].astype(F32))
    summed = grad_a_ref[...].astype(F32) + grad_b_ref[...].astype(F32)
    rgrad = cot_ref[...].astype(F32) + norm_back(unit, scale, summed * flat(gain_ref))
    agrad = rgrad.astype(BF16)
    agrad_ref[...] = agrad
    own_cg_ref[...] = mm(agrad, own_w_ref[...], NT).astype(BF16)
    far_cg_ref[...] = mm(agrad, far_w_ref[...], NT).astype(BF16)
    gather_rows(sum_ref, pl.program_id(0) == 0, rgrad, summed * unit, summed)


def middle(span, residual, grad_a, grad_b, cot, gain, own_w, far_w, carried=(), rider=None):
    tokens, d = residual.shape
    own = own_w.shape[1] // 4
    first, count = span
    tall, slim, near = rows(TILE, d, first), rows(TILE, own, first), rows(TILE, d)
    return call(
        middle_kernel, "second_norm_back", (count,),
        [tall, near, near, tall, whole((d,)), out_weights(own_w), out_weights(far_w)],
        [(tall, (tokens, d), BF16), (slim, (tokens, own), BF16), (slim, (tokens, own), BF16, True), (whole((3, d)), (3, d), F32)],
        (residual, grad_a, grad_b, cot, gain, own_w, far_w), carried=carried, rider=rider,
    )


def output_kernel(residual_ref, mlp_a_ref, mlp_b_ref, b_down_ref, out_ref):
    out_ref[...] = (
        residual_ref[...].astype(F32)
        + ((mlp_a_ref[...].astype(F32) + mlp_b_ref[...].astype(F32)) + flat(b_down_ref))
    ).astype(BF16)


def output(residual, mlp_a, mlp_b, b_down):
    tokens, d = residual.shape
    tall = rows(TILE, d)
    return call(
        output_kernel, "block_output", (tokens // TILE,), [tall] * 3 + [whole((d,))],
        [(tall, (tokens, d), BF16)], (residual, mlp_a, mlp_b, b_down), cover=True,
    )[0]


def first_back_kernel(x_ref, grad_a_ref, grad_b_ref, rgrad_ref, gain_ref, *rest):
    unit, scale = norm_stats(x_ref[...].astype(F32))
    upstream = (grad_a_ref[...].astype(F32) + grad_b_ref[...].astype(F32)) * flat(gain_ref)
    rest[-1][...] = rgrad_ref[...].astype(F32) + norm_back(unit, scale, upstream)


def first_back(span, x, grad_a, grad_b, rgrad, gain, carried=()):
    tokens, d = x.shape
    first, count = span
    tall = rows(TILE // 2, d, 2 * first)
    return call(
        first_back_kernel, "first_norm_back", (2 * count,), [tall] * 4 + [whole((d,))],
        [(tall, (tokens, d), F32)], (x, grad_a, grad_b, rgrad, gain), carried=carried,
    )


def swap(value, axis, size, bit):
    return lax.ppermute(value, axis, [(i, i ^ bit) for i in range(size)])


def tie(value, *others):
    return lax.optimization_barrier((value,) + others)[0]


class ScatterSums:
    def __init__(self, size, *chains):
        self.size = size
        self.keeps, self.gives, bits = [list(part) for part in zip(*chains)]
        self.bits = [list(each) for each in bits]
        self.me = lax.axis_index("dp").astype(jnp.int32)

    def begin(self):
        bits = [each.pop(0) for each in self.bits]
        self.gots = [swap(give, "dp", self.size, 1 << bit) for give, bit in zip(self.gives, bits)]

    def rider(self, *others):
        self.gots = [tie(got, *others) if others else got for got in self.gots]
        mine = jnp.stack([(self.me >> bits[0]) & 1 for bits in self.bits])
        return Rider(mine, self.keeps, self.gots, len({bits[0] for bits in self.bits}) < len(self.bits))

    def take(self, results):
        self.keeps, self.gives = results[: len(self.keeps)], results[len(self.keeps) :]

    def end(self, *others):
        if self.bits[0]:
            self.take(call(alone_kernel, "merge", (1,), [], [], [], rider=self.rider(*others)))
        else:
            self.gots = [tie(got, *others) if others else got for got in self.gots]
        return self.gots

    def finish(self, *widths):
        while self.bits[0]:
            self.begin()
            self.end()
        return last_sum(self.keeps, self.gots, widths)


def body(
    n_dp,
    n_mp,
    block_input,
    segment_ids,
    group_ids,
    padding,
    ln1_gain,
    ln1_bias,
    w_qkv,
    b_qv,
    w_out,
    b_out,
    ln2_gain,
    ln2_bias,
    w_up,
    b_up,
    w_down,
    b_down,
    cotangent,
):
    tokens, d = block_input.shape
    sequences, length = segment_ids.shape
    own = w_qkv.shape[2]
    far = lambda value: swap(value, "mp", n_mp, 2)
    near = lambda value: swap(value, "mp", n_mp, 1)
    levels = n_dp.bit_length() - 1
    bits = list(range(levels))
    other_bits = [1, 0] + bits[2:]
    me = lax.axis_index("dp").astype(jnp.int32)
    halves = jnp.stack([me & 1, (me >> 1) & 1])
    orders = (chunk_order(n_dp, bits), chunk_order(n_dp, other_bits))

    small = jnp.stack([b_up, jnp.pad(b_qv.reshape(-1), (0, d - 2 * own))])
    parts = []
    for _ in range(3):
        parts.append(lax.reduce_precision(small, 8, 7))
        small = small - parts[-1]
    small = jnp.pad(jnp.stack(parts, 1).reshape(6, d).astype(BF16), ((0, 10), (0, 0)))
    pack = jnp.concatenate([jnp.transpose(w_qkv, (1, 2, 0)).reshape(3 * own, d), w_out, small], 0)
    pack_far = far(pack)
    table = tables(segment_ids, group_ids, padding)

    *saved_own, n1 = attend_own(table, block_input, ln1_gain, ln1_bias, pack, b_qv)
    ctx_own = saved_own[0]
    cot_down, sum_cot, mlp_own = upstream(tie(cotangent, n1), w_up, w_down)
    mlp_far = far(mlp_own)
    parts, saved_far = [], ()
    for s in range(sequences):
        *saved_far, part = attend_far(s, table, n1, tie(pack_far, cot_down), ctx_own, pack, saved_far)
        parts.append((part, near(part)))
    carried, sums_up = (), []
    for s, (part, other) in enumerate(parts):
        other = tie(other, carried[0] if carried else parts[-1][0])
        weights = (orders, halves, cotangent) if s == sequences - 1 else ()
        *carried, = hidden_own(
            s, length, block_input, part, other, b_out, ln2_gain, ln2_bias, w_up, b_up, cot_down, carried[:4], weights
        )
        sums_up.append(carried[4])
    residual, n2, hidden, upg, _, up_keep, up_give, down_keep, down_give = carried
    sum_mlp = ScatterSums(n_dp, (up_keep, up_give, bits), (down_keep, down_give, other_bits))
    sum_mlp.begin()
    mlp_far = tie(mlp_far, up_keep)
    tiles = tokens // TILE
    shares, mlp, gate, rider = [], (), (up_keep,), None
    for span in ((0, tiles - 1), (tiles - 1, 1)):
        results = products(
            span, tie(n2, *gate), cotangent, hidden, upg, w_up, w_down, mlp_far, pack_far, mlp, rider
        )
        *mlp, n2g = results[:2]
        shares.append((span, n2g, near(n2g)))
        if rider:
            sum_mlp.take(results[2:])
        else:
            gate, rider = (n2g,), sum_mlp.rider(n2g)
    sum_mlp.begin()
    gate, carried, sums_mid, rider = (n2g,), (), [], None
    for span, n2g, other in shares:
        results = middle(
            span, residual, n2g, tie(other, *gate), cotangent, ln2_gain, pack, pack_far, carried, rider
        )
        *carried, sum_mid = results[:4]
        sums_mid.append(sum_mid)
        if rider:
            sum_mlp.take(results[4:])
        else:
            gate, rider = (carried[0],), sum_mlp.rider(sum_mid)
    sum_mlp.begin()
    agrad, cgrad_own, cgrad_far = carried
    ctx, lse, q, k, v = saved_own
    *own_grads, keep, give, sum_qv = attend_own_back(
        table, halves[:1], orders[0], q, k, v, ctx, cgrad_own, lse, n1, agrad
    )
    mlp_near = near(mlp[0])
    sum_attn = ScatterSums(n_dp, (keep, give, bits))
    sum_attn.begin()
    got = sum_mlp.end(keep)
    while sum_mlp.bits[0]:
        sum_mlp.begin()
        sum_mlp.end()
    ctx, lse, q, k, v = saved_far
    n1g, sum_first, up_sum, down_sum = attend_far_back(
        table, q, k, v, ctx, tie(cgrad_far, keep, *got), lse, block_input, own_grads, pack, pack_far,
        LastRider(sum_mlp.keeps, sum_mlp.gots),
    )
    got = sum_attn.end(n1g)
    sum_attn.begin()
    sum_first = tie(sum_first, *sum_attn.gives)
    sum_first = sum_first + near(sum_first)
    n1g_near = near(tie(n1g, sum_first))
    add = lambda values: functools.reduce(jnp.add, values)
    wide_qv = jnp.concatenate([sum_qv.reshape(1, -1), jnp.zeros((1, d - 2 * own), F32)], 1)
    sums = jnp.concatenate([sum_first, add(sums_mid), sum_cot, add(sums_up), wide_qv], 0)
    other = swap(sums, "dp", n_dp, 1)
    block_output = output(tie(residual, n1g, *got, sums), mlp[0], mlp_near, b_down)
    sums = sums + tie(other, block_output)
    other = swap(sums, "dp", n_dp, 2)
    got = sum_attn.end(block_output, sums)
    sum_attn.begin()
    outputs = first_back((0, tiles - 1), block_input, n1g, tie(n1g_near, block_output, *got, sums), agrad, ln1_gain)
    sums = sums + tie(other, *outputs)
    if levels > 2:
        other = swap(sums, "dp", n_dp, 4)
    got = sum_attn.end(*outputs)
    qkv_sum, out_sum = sum_attn.finish(3 * own, own)
    input_grad, = first_back((tiles - 1, 1), block_input, n1g, tie(n1g_near, sums, qkv_sum), agrad, ln1_gain, outputs)
    if levels > 2:
        sums = sums + tie(other, input_grad)
    for bit in range(3, levels):
        sums = sums + swap(sums, "dp", n_dp, 1 << bit)

    piece, tiny = d // n_dp, own // n_dp
    mine = lax.dynamic_slice(sums, (0, me * piece), (sums.shape[0] - 1, piece))
    vectors = [mine[i] for i in range(7)]
    return (
        block_output,
        input_grad,
        vectors[0],
        vectors[1],
        qkv_sum.reshape(piece, 3, own),
        lax.dynamic_slice(sums[7, : 2 * own].reshape(2, own), (0, me * tiny), (2, tiny)),
        out_sum.T,
        vectors[2],
        vectors[3],
        vectors[4],
        up_sum,
        vectors[6],
        down_sum.T,
        vectors[5],
    )


def solution(mesh):
    return jax.shard_map(
        functools.partial(body, mesh.shape["dp"], mesh.shape["mp"]),
        mesh=mesh,
        in_specs=(
            P("dp", None),
            P("dp", None),
            P("dp", None),
            P("dp", None),
            P(),
            P(),
            P(None, None, "mp"),
            P(None, "mp"),
            P("mp", None),
            P(),
            P(),
            P(),
            P(None, "mp"),
            P("mp"),
            P("mp", None),
            P(),
            P("dp", None),
        ),
        out_specs=(
            P("dp", None),
            P("dp", None),
            P("dp"),
            P("dp"),
            P("dp", None, "mp"),
            P(None, ("mp", "dp")),
            P("mp", "dp"),
            P("dp"),
            P("dp"),
            P("dp"),
            P("dp", "mp"),
            P(("mp", "dp")),
            P("mp", "dp"),
            P("dp"),
        ),
        check_vma=False,
    )
```

```python
import functools

import jax
import jax.numpy as jnp
from jax import lax
from jax.experimental import pallas as pl
from jax.experimental.pallas import tpu as pltpu
from jax.sharding import PartitionSpec as P

HD = 64
QB = 128
GRAIN = 64
GRAIN_BITS = 6
GROUP = 2
BACK_GROUP = 2
LONGEST = 256
FREE = dict(
    masks=(), attend_own=(), attend_far=(3, 4, 7), attend_own_back=(7, 10), attend_far_back=(9, 10, 11), upstream=(),
    hidden_own=(1, 2, 8), feed_forward=(4, 5, 6), second_norm_back=(1, 2), block_output=(), first_norm_back=(1, 2),
    merge=range(99), last_sum=range(99),
)
GRANTS = dict(
    masks=4, attend_own=20, attend_far=14, attend_own_back=28, attend_far_back=34, upstream=12, hidden_own=34,
    feed_forward=22, second_norm_back=17, block_output=8, first_norm_back=14, merge=6, last_sum=4,
)
TILE = 512
COVER = 10**12
MASKED = -1e30
EPS = 1e-05
LOG2E = 1.4426950408889634
F32 = jnp.float32
BF16 = jnp.bfloat16
NT = (((1,), (1,)), ((), ()))
NN = (((1,), (0,)), ((), ()))
TN = (((0,), (0,)), ((), ()))


def mm(a, b, dims):
    return lax.dot_general(a, b, dims, preferred_element_type=F32)


def flat(ref):
    return ref[...].reshape(1, -1)


def hosted(kernel, own, taken, carried, given, rider, *refs):
    refs = list(refs[own:])
    cut = lambda count: [refs.pop(0) for _ in range(count)]
    main_in, rider_in, kept, main_out, rider_out = map(cut, (taken, len(rider.args), carried, given, len(rider.out)))
    kernel(*main_in, *kept, *main_out, *refs)

    @pl.when(pl.program_id(0) == 0)
    def _():
        rider.body(rider_in, rider_out)


def call(kernel, name, grid, in_specs, out, args, scratch=(), prefetch=0, carried=(), cover=False, carried_specs=(), rider=None):
    in_specs, out, args = list(in_specs), list(out), list(args)
    pinned = lambda at: at >= prefetch and args[at].size >= 1 << 17 and at not in FREE[name]
    args = [pltpu.with_memory_space_constraint(arg, pltpu.HBM) if pinned(at) else arg for at, arg in enumerate(args)]
    if rider:
        first = [] if rider.halves is None else [rider.halves]
        kernel = functools.partial(hosted, kernel, len(first), len(args), len(carried), len(out), rider)
        in_specs, out, args, prefetch = in_specs + rider.specs, out + rider.out, first + args + rider.args, prefetch + len(first)
    return pl.pallas_call(
        kernel,
        grid_spec=pltpu.PrefetchScalarGridSpec(
            num_scalar_prefetch=prefetch,
            grid=grid,
            in_specs=in_specs + list(carried_specs or [pl.BlockSpec(memory_space=pl.ANY)] * len(carried)),
            out_specs=[entry[0] for entry in out],
            scratch_shapes=list(scratch),
        ),
        out_shape=[pltpu.HBM(*entry[1:3]) if entry[3:] else jax.ShapeDtypeStruct(*entry[1:3]) for entry in out],
        input_output_aliases={len(args) + i: i for i in range(len(carried))},
        compiler_params=pltpu.CompilerParams(vmem_limit_bytes=GRANTS[name] * 1024 * 1024),
        cost_estimate=pl.CostEstimate(flops=COVER if cover else 0, bytes_accessed=1024, transcendentals=0),
        name=name,
    )(*args, *carried)


def whole(shape):
    return pl.BlockSpec(shape, lambda *ids: (0,) * len(shape))


def rows(tile, width, skip=0):
    return pl.BlockSpec((tile, width), lambda i, *rest: (i + skip, 0))


def norm_stats(values):
    average = jnp.mean(values, -1, keepdims=True)
    centered = values - average
    variance = jnp.mean(centered * centered, -1, keepdims=True)
    scale = lax.rsqrt(variance + EPS)
    return centered * scale, scale


def norm_back(unit, scale, upstream):
    first = jnp.mean(upstream, -1, keepdims=True)
    second = jnp.mean(upstream * unit, -1, keepdims=True)
    return scale * (upstream - first - unit * second)


def total(values):
    return jnp.sum(values.astype(F32), 0, keepdims=True)


def gather_rows(ref, first, *values):
    @pl.when(first)
    def _():
        ref[...] = jnp.zeros_like(ref)

    for at, value in enumerate(values):
        ref[at : at + 1, :] += total(value)


def masks_kernel(segment_ref, group_ref, padding_ref, bounds_ref, code_ref):
    sequences, length = segment_ref.shape
    blocks = length // QB
    low = segment_ref[...] * 4
    high = low + group_ref[...]
    codes = jnp.where(padding_ref[...] == 0, high, -1)
    place = lax.broadcasted_iota(jnp.int32, (1, sequences * blocks), 1)
    sorted_rows = [jnp.zeros((1, sequences * blocks), jnp.int32)] * 3
    for s in range(sequences):
        for at, rows_of in enumerate((codes, low, high)):
            code_ref[s, at : at + 1, :] = rows_of[s : s + 1, :]
        row = segment_ref[s : s + 1, :]
        windows = []
        for block in range(blocks):
            earliest = row[:, block * QB : block * QB + 1]
            latest = row[:, (block + 1) * QB - 1 : (block + 1) * QB]
            key_from = jnp.sum((row < earliest).astype(F32), 1, keepdims=True).astype(jnp.int32) & -16
            key_to = jnp.sum((row <= latest).astype(F32), 1, keepdims=True).astype(jnp.int32)
            grains = jnp.maximum((key_to - key_from + (GRAIN - 1)) >> GRAIN_BITS, QB // GRAIN)
            windows.append((jnp.minimum(key_from, length - grains * GRAIN), grains, jnp.full_like(grains, block)))
        for block, window in enumerate(windows):
            smaller = [
                (other[1] < window[1]) | ((other[1] == window[1]) & (at < block)) for at, other in enumerate(windows)
            ]
            rank = functools.reduce(jnp.add, [one.astype(jnp.int32) for one in smaller])
            here = place == s * blocks + rank
            sorted_rows = [jnp.where(here, value, kept) for value, kept in zip(window, sorted_rows)]
    for at, value in enumerate(sorted_rows):
        bounds_ref[at : at + 1, :] = value


def tables(segment_ids, group_ids, padding):
    sequences, length = segment_ids.shape
    bounds = (3, sequences * (length // QB))
    codes = (sequences, 3, length)
    return call(
        masks_kernel, "masks", (1,), [whole(segment_ids.shape)] * 3,
        [(whole(bounds), bounds, jnp.int32), (whole(codes), codes, jnp.int32)], (segment_ids, group_ids, padding),
    )


def extents(length):
    most = min(QB + 2 * LONGEST, length) // GRAIN
    return [extent for extent in (3, 4, 5, 6, 8) if extent < most] + [most]


def head_groups(width):
    return [slice(at, min(at + 2 * HD, width)) for at in range(0, width, 2 * HD)]


def stack_heads(values):
    if values.shape[1] == HD:
        return values
    lane = lax.broadcasted_iota(jnp.int32, values.shape, 1)
    zero = jnp.zeros_like(values)
    return jnp.concatenate(
        [jnp.where(lane < HD, values, zero), jnp.where(lane >= HD, values, zero)], 0
    )


def join_heads(values):
    if values.shape[1] == HD:
        return values
    lane = lax.broadcasted_iota(jnp.int32, (QB, 2 * HD), 1)
    return jnp.where(lane < HD, values[:QB], values[QB:])


def spread_codes(code_ref, column_ref):
    for at in range(0, column_ref.shape[0], QB):
        column_ref[at : at + QB, :] = jnp.broadcast_to(code_ref[0:1, at : at + QB], (QB, QB)).T


def mask_bias(column_ref, code_ref, start, extent, block):
    mine = pl.ds(pl.multiple_of(block * QB, QB), QB)
    codes = column_ref[pl.ds(start, extent), :]
    shape = (extent, QB)
    apart = lax.broadcasted_iota(jnp.int32, shape, 0) - lax.broadcasted_iota(jnp.int32, shape, 1)
    allowed = ((codes >= code_ref[1:2, mine]) & (codes <= code_ref[2:3, mine])) | (
        apart == block * QB - start
    )
    return jnp.where(allowed, jnp.float32(0), jnp.float32(MASKED))


def widen(bias, cols):
    return jnp.concatenate([bias, bias], 1) if cols.stop - cols.start > HD else bias


def each_block(bound_ref, length, group, sequence, run):
    turns = length // QB // group

    def step(turn, carry):
        place = (sequence * turns + turn) * group
        grains = functools.reduce(jnp.maximum, [bound_ref[1, place + i] for i in range(group)])
        blocks = [bound_ref[2, place + i] for i in range(group)]
        least = 0
        for extent in extents(length):
            starts = [
                pl.multiple_of(jnp.minimum(bound_ref[0, place + i], length - extent * GRAIN), 16) for i in range(group)
            ]
            pl.when((grains > least) & (grains <= extent))(functools.partial(run, extent * GRAIN, blocks, starts))
            least = extent
        return carry

    lax.fori_loop(0, turns, step, 0)


def project(normed, wt_ref, q_bias, v_bias, q_ref, k_ref, v_ref):
    own = q_ref.shape[1]
    q_ref[...] = (mm(normed, wt_ref[:own, :], NT) + q_bias).astype(BF16)
    k_ref[...] = mm(normed, wt_ref[own : 2 * own, :], NT).astype(BF16)
    v_ref[...] = (mm(normed, wt_ref[2 * own :, :], NT) + v_bias).astype(BF16)


def attend(sequence, bound_ref, code_ref, column_ref, q_ref, k_ref, v_ref, ctx_ref, lse_ref):
    length, width = q_ref.shape
    heads = head_groups(width)
    spread_codes(code_ref, column_ref)

    def run(extent, blocks, starts):
        units, scores, probs, totals, biases = [], [], [], [], []
        for i, (block, start) in enumerate(zip(blocks, starts)):
            here = pl.ds(start, extent)
            mine = pl.ds(pl.multiple_of(block * QB, QB), QB)
            for p, cols in enumerate(heads):
                units.append((i, block, here, mine, p, cols))
                scores.append(mm(k_ref[here, cols], stack_heads(q_ref[mine, cols]), NT))
            biases.append(mask_bias(column_ref, code_ref, start, extent, block))
        for (i, block, here, mine, p, cols), score in zip(units, scores):
            score = score * (0.125 * LOG2E) + widen(biases[i], cols)
            top = jnp.max(score, 0, keepdims=True)
            weights = jnp.exp2(score - top)
            summed = jnp.sum(weights, 0, keepdims=True)
            lse_ref[block, p : p + 1, : score.shape[1]] = top + jnp.log2(summed)
            totals.append(1.0 / summed)
            probs.append(weights.astype(BF16))
        for (i, block, here, mine, p, cols), prob, scale in zip(units, probs, totals):
            turned = v_ref[here, cols].T
            both = [
                mm(turned[at * HD : (at + 1) * HD], prob[:, at * QB : (at + 1) * QB], NN)
                * scale[:, at * QB : (at + 1) * QB]
                for at in range(prob.shape[1] // QB)
            ]
            ctx_ref[mine, cols] = jnp.concatenate(both, 0).T.astype(BF16)

    each_block(bound_ref, length, GROUP, sequence, run)


def begin_copies(pairs, sems):
    copies = [pltpu.make_async_copy(source, target, sems.at[at]) for at, (source, target) in enumerate(pairs)]
    for copy in copies:
        copy.start()

    def finish():
        for copy in copies:
            copy.wait()

    return finish


def own_kernel(
    bound_ref, code_ref, x_ref, gain_ref, bias_ref, wt_ref, qv_ref,
    ctx_ref, lse_ref, q_hbm, k_hbm, v_hbm, n1_hbm, column_ref, q_ref, k_ref, v_ref, n1_ref, sems,
):
    length = x_ref.shape[0]
    here = pl.ds(pl.multiple_of(pl.program_id(0) * length, length), length)
    chunks = [pl.ds(at, length // 4) for at in range(0, length, length // 4)]

    def norm(chunk):
        unit, _ = norm_stats(x_ref[chunk, :].astype(F32))
        n1_ref[chunk, :] = (unit * flat(gain_ref) + flat(bias_ref)).astype(BF16)

    norm(chunks[0])
    for at, chunk in enumerate(chunks):
        for following in chunks[at + 1 : at + 2]:
            norm(following)
        project(
            n1_ref[chunk, :], wt_ref, qv_ref[0:1, :], qv_ref[1:2, :], *(ref.at[chunk] for ref in (q_ref, k_ref, v_ref))
        )
    finish = begin_copies(
        [(q_ref, q_hbm.at[here]), (k_ref, k_hbm.at[here]), (v_ref, v_hbm.at[here]), (n1_ref, n1_hbm.at[here])], sems
    )
    attend(pl.program_id(0), bound_ref, code_ref, column_ref, q_ref, k_ref, v_ref, ctx_ref, lse_ref)
    finish()


STAY = pl.BlockSpec(memory_space=pl.ANY)


def attention_outs(tokens, width, length, sequences, skip=0):
    tall = rows(length, width, skip)
    lse = (length // QB, 8, 2 * QB)
    return [
        (tall, (tokens, width), BF16, True),
        (pl.BlockSpec(lse, lambda s, *ids: (s + skip, 0, 0)), (sequences * lse[0],) + lse[1:], F32, True),
    ] + [(STAY, (tokens, width), BF16, True)] * 3


def attention_scratch(length, width):
    return [pltpu.VMEM((length, QB), jnp.int32)] + [pltpu.VMEM((length, width), BF16)] * 3


def projections(pack):
    return pl.BlockSpec((pack.shape[1] // 4 * 3, pack.shape[1]), lambda *ids: (0, 0))


def out_weights(pack):
    return pl.BlockSpec((pack.shape[1] // 4, pack.shape[1]), lambda *ids: (3, 0))


def biases(pack):
    return pl.BlockSpec((16, pack.shape[1]), lambda *ids: (pack.shape[1] // 16, 0))


def bias_of(ref, which):
    part = [ref[3 * which + at : 3 * which + at + 1, :].astype(F32) for at in range(3)]
    return part[0] + (part[1] + part[2])


def codes_spec(codes, skip=0):
    return pl.BlockSpec((None,) + codes.shape[1:], lambda s, *ids: (s + skip, 0, 0))


def attend_own(table, x, gain, bias, wt, b_qv):
    bounds, codes = table
    tokens, d = x.shape
    sequences, _, length = codes.shape
    return call(
        own_kernel, "attend_own", (sequences,),
        [codes_spec(codes), rows(length, d), whole(gain.shape), whole(bias.shape), projections(wt), whole(b_qv.shape)],
        attention_outs(tokens, b_qv.shape[1], length, sequences) + [(STAY, (tokens, d), BF16, True)],
        (bounds, codes, x, gain, bias, wt, b_qv),
        scratch=attention_scratch(length, b_qv.shape[1])
        + [pltpu.VMEM((length, d), BF16), pltpu.SemaphoreType.DMA((4,))],
        prefetch=1,
    )


def far_kernel(
    sequence, bound_ref, code_ref, n1_ref, wt_ref, bias_ref, own_ctx_hbm, pack_hbm, far_hbm, *rest
):
    ctx_ref, lse_ref, q_hbm, k_hbm, v_hbm, part_ref = rest[-14:-8]
    column_ref, q_ref, k_ref, v_ref, own_ctx_ref, own_w_ref, far_w_ref, sems = rest[-8:]
    length, own = q_ref.shape
    here = pl.ds(sequence * length, length)
    weights = pl.ds(3 * own, own)
    late = begin_copies(
        [
            (own_ctx_hbm.at[here], own_ctx_ref),
            (pack_hbm.at[weights], own_w_ref),
            (far_hbm.at[weights], far_w_ref),
        ],
        sems.at[pl.ds(0, 3)],
    )
    bias = bias_of(bias_ref, 1)
    project(n1_ref[...], wt_ref, bias[:, :own], bias[:, own : 2 * own], q_ref, k_ref, v_ref)
    finish = begin_copies(
        [(q_ref, q_hbm.at[here]), (k_ref, k_hbm.at[here]), (v_ref, v_hbm.at[here])], sems.at[pl.ds(3, 3)]
    )
    attend(sequence, bound_ref, code_ref, column_ref, q_ref, k_ref, v_ref, ctx_ref, lse_ref)
    late()
    part_ref[...] = (
        mm(own_ctx_ref[...], own_w_ref[...], NN) + mm(ctx_ref[...], far_w_ref[...], NN)
    ).astype(BF16)
    finish()


def attend_far(sequence, table, n1, far, own_ctx, pack, carried=()):
    bounds, codes = table
    tokens, d = n1.shape
    sequences, _, length = codes.shape
    own = own_ctx.shape[1]
    return call(
        functools.partial(far_kernel, sequence), "attend_far", (1,),
        [codes_spec(codes, sequence), rows(length, d, sequence), projections(far), biases(far)] + [STAY] * 3,
        attention_outs(tokens, own, length, sequences, sequence) + [(rows(length, d), (length, d), BF16)],
        (bounds, codes, n1, far, far, own_ctx, pack, far),
        scratch=attention_scratch(length, own)
        + [pltpu.VMEM((length, own), BF16)]
        + [pltpu.VMEM((own, d), BF16)] * 2
        + [pltpu.SemaphoreType.DMA((6,))],
        prefetch=1, carried=carried,
    )


def attend_back(
    bound_ref, code_ref, column_ref, q_ref, k_ref, v_ref, ctx_ref, grad_ref, lse_ref,
    dq_ref, dk_ref, dv_ref, dk_acc, dv_acc,
):
    length, width = q_ref.shape
    heads = head_groups(width)
    spread_codes(code_ref, column_ref)
    dk_acc[...] = jnp.zeros_like(dk_acc)
    dv_acc[...] = jnp.zeros_like(dv_acc)

    def run(extent, blocks, starts):
        units, stacked, upstream, scores, grads, biases = [], [], [], [], [], []
        for i, (block, start) in enumerate(zip(blocks, starts)):
            here = pl.ds(start, extent)
            mine = pl.ds(pl.multiple_of(block * QB, QB), QB)
            for p, cols in enumerate(heads):
                units.append((i, block, here, mine, p, cols))
                stacked.append(stack_heads(q_ref[mine, cols]))
                upstream.append(stack_heads(grad_ref[mine, cols]))
                scores.append(mm(k_ref[here, cols], stacked[-1], NT))
                grads.append(mm(v_ref[here, cols], upstream[-1], NT))
            biases.append(mask_bias(column_ref, code_ref, start, extent, block))
        probs, score_grads = [], []
        for (i, block, here, mine, p, cols), score, grad in zip(units, scores, grads):
            turned = (ctx_ref[mine, cols].astype(F32) * grad_ref[mine, cols].astype(F32)).T
            delta = jnp.concatenate(
                [
                    jnp.sum(turned[at : at + HD], 0, keepdims=True)
                    for at in range(0, turned.shape[0], HD)
                ],
                1,
            )
            weights = jnp.exp2(
                score * (0.125 * LOG2E) + widen(biases[i], cols) - lse_ref[block, p : p + 1, : score.shape[1]]
            )
            probs.append(weights.astype(BF16))
            score_grads.append((weights * (grad - delta)).astype(BF16))
        for n, (i, block, here, mine, p, cols) in enumerate(units):
            dv_acc[here, cols] += mm(probs[n], upstream[n], NN)
            dk_acc[here, cols] += mm(score_grads[n], stacked[n], NN)
            dq = join_heads(mm(score_grads[n], k_ref[here, cols], TN))
            dq_ref[mine, cols] = (dq * 0.125).astype(BF16)

    each_block(bound_ref, length, BACK_GROUP, pl.program_id(0), run)
    dk_ref[...] = (dk_acc[...] * 0.125).astype(BF16)
    dv_ref[...] = dv_acc[...].astype(BF16)


def own_back_kernel(
    order, bound_ref, half_ref, code_ref, q_ref, k_ref, v_ref, ctx_ref, grad_ref, lse_ref, n1_hbm, agrad_hbm,
    dq_ref, dk_ref, dv_ref, keep_ref, give_ref, sum_ref, dk_acc, dv_acc, column_ref, weight_acc, n1_ref, agrad_ref, sems,
):
    length = q_ref.shape[0]
    here = pl.ds(pl.multiple_of(pl.program_id(0) * length, length), length)
    late = begin_copies([(n1_hbm.at[here], n1_ref), (agrad_hbm.at[here], agrad_ref)], sems)
    attend_back(
        bound_ref, code_ref, column_ref, q_ref, k_ref, v_ref, ctx_ref, grad_ref, lse_ref,
        dq_ref, dk_ref, dv_ref, dk_acc, dv_acc,
    )
    first = pl.program_id(0) == 0

    @pl.when(first)
    def _():
        weight_acc[...] = jnp.zeros_like(weight_acc)
        sum_ref[...] = jnp.zeros_like(sum_ref)

    own = dq_ref.shape[1]
    late()
    normed = n1_ref[...]
    for at, grad in enumerate((dq_ref, dk_ref, dv_ref)):
        weight_acc[:, at * own : (at + 1) * own] += mm(normed, grad[...], TN)
    weight_acc[:, 3 * own :] += mm(agrad_ref[...], ctx_ref[...], TN)
    sum_ref[0:1, :] += total(dq_ref[...])
    sum_ref[1:2, :] += total(dv_ref[...])

    @pl.when(pl.program_id(0) == pl.num_programs(0) - 1)
    def _():
        split_chunks(half_ref[0], order, weight_acc, keep_ref, give_ref)


def attend_own_back(table, half, order, q, k, v, ctx, grad, lse, n1, agrad):
    bounds, codes = table
    tokens, d = n1.shape
    own = q.shape[1]
    sequences, _, length = codes.shape
    tall = rows(length, own)
    lse_spec = pl.BlockSpec((length // QB, 8, 2 * QB), lambda s, *ids: (s, 0, 0))
    count = len(order[0])
    chunk = (count, d // (2 * count), 4 * own)
    return call(
        functools.partial(own_back_kernel, order), "attend_own_back", (sequences,),
        [codes_spec(codes)] + [tall] * 5 + [lse_spec, STAY, STAY],
        [(tall, (tokens, own), BF16)] * 3 + [(whole(chunk), chunk, BF16)] * 2 + [(whole((2, own)), (2, own), F32)],
        (bounds, half, codes, q, k, v, ctx, grad, lse, n1, agrad),
        scratch=[pltpu.VMEM((length, own), F32)] * 2
        + [pltpu.VMEM((length, QB), jnp.int32), pltpu.VMEM((d, 4 * own), F32)]
        + [pltpu.VMEM((length, d), BF16)] * 2
        + [pltpu.SemaphoreType.DMA((2,))],
        prefetch=2, cover=True,
    )


def far_back_kernel(
    bound_ref, code_ref, q_ref, k_ref, v_ref, ctx_ref, grad_ref, lse_ref,
    x_hbm, aq_hbm, ak_hbm, av_hbm, wa_hbm, wb_hbm,
    n1g_ref, sum_ref, dk_acc, dv_acc, column_ref, dq_ref, dk_ref, dv_ref,
    x_ref, aq_ref, ak_ref, av_ref, wa_ref, wb_ref, sems,
):
    length = q_ref.shape[0]
    here = pl.ds(pl.multiple_of(pl.program_id(0) * length, length), length)
    first = pl.ds(0, wa_ref.shape[0])
    late = begin_copies(
        [
            (aq_hbm.at[here], aq_ref),
            (ak_hbm.at[here], ak_ref),
            (av_hbm.at[here], av_ref),
            (wa_hbm.at[first], wa_ref),
            (wb_hbm.at[first], wb_ref),
            (x_hbm.at[here], x_ref),
        ],
        sems,
    )
    attend_back(
        bound_ref, code_ref, column_ref, q_ref, k_ref, v_ref, ctx_ref, grad_ref, lse_ref,
        dq_ref, dk_ref, dv_ref, dk_acc, dv_acc,
    )
    own = aq_ref.shape[1]
    late()
    grad = None
    for w_ref, grads in ((wa_ref, (aq_ref, ak_ref, av_ref)), (wb_ref, (dq_ref, dk_ref, dv_ref))):
        for place, one_ref in enumerate(grads):
            here = mm(one_ref[...], w_ref[place * own : (place + 1) * own, :], NN)
            grad = here if grad is None else grad + here
    n1g_ref[...] = grad.astype(BF16)
    unit, _ = norm_stats(x_ref[...].astype(F32))
    gather_rows(sum_ref, pl.program_id(0) == 0, grad * unit, grad)


def attend_far_back(table, q, k, v, ctx, grad, lse, x, own_grads, own_wt, far_wt, rider):
    bounds, codes = table
    tokens, d = x.shape
    own = q.shape[1]
    sequences, _, length = codes.shape
    tall, high = rows(length, own), rows(length, d)
    lse_spec = pl.BlockSpec((length // QB, 8, 2 * QB), lambda s, *ids: (s, 0, 0))
    return call(
        far_back_kernel, "attend_far_back", (sequences,),
        [codes_spec(codes)] + [tall] * 5 + [lse_spec] + [STAY] * 6,
        [(high, (tokens, d), BF16), (whole((2, d)), (2, d), F32)],
        (bounds, codes, q, k, v, ctx, grad, lse, x, *own_grads, own_wt, far_wt),
        scratch=[pltpu.VMEM((length, own), F32)] * 2
        + attention_scratch(length, own)
        + [pltpu.VMEM((length, d), BF16)]
        + [pltpu.VMEM((length, own), BF16)] * 3
        + [pltpu.VMEM((3 * own, d), BF16)] * 2
        + [pltpu.SemaphoreType.DMA((6,))],
        prefetch=1, cover=True, rider=rider,
    )


def reversed_bits(value, count):
    return sum(((value >> i) & 1) << (count - 1 - i) for i in range(count))


def chunk_order(size, bits):
    inner = range(size // 2)
    spread = lambda low, at: sum(((low >> (len(bits) - 2 - i)) & 1) << bit for i, bit in enumerate(bits[1:])) | at << bits[0]
    return [[spread(low, at) for low in inner] for at in (0, 1)]


def split_chunks(half, order, terms, keep_ref, give_ref):
    piece = keep_ref.shape[1]

    def store(mine):
        for ref, devices in ((keep_ref, order[mine]), (give_ref, order[1 - mine])):
            for at, device in enumerate(devices):
                ref[at] = terms[device * piece : (device + 1) * piece, :].astype(BF16)

    for mine in (0, 1):
        pl.when(half == mine)(functools.partial(store, mine))


class Rider:
    def __init__(self, halves, keeps, gots, joint):
        self.halves, self.joint = halves, joint
        self.specs, self.out, self.args = [], [], []
        for chain, keep in enumerate(keeps):
            count, piece, width = keep.shape
            block = (count // 2, piece, width)
            base = 2 * chain if len(gots) < len(keeps) else 0
            got = gots[0 if base else min(chain, len(gots) - 1)]
            at = lambda mine, first, chain=chain: pl.BlockSpec(
                block, lambda i, ref, *ids: (first + (ref[chain] if mine else 1 - ref[chain]), 0, 0)
            )
            self.specs += [at(True, 0), at(True, base), at(False, 0), at(False, base)]
            self.out.append((whole(block), block, F32, True))
            self.args += [keep, got, keep, got]
        shape = (block[0] * len(keeps),) + block[1:]
        self.out += [(whole(shape), shape, BF16)] if joint else [(whole(block), block, BF16)] * len(keeps)

    def body(self, refs, out):
        chains = len(refs) // 4
        for chain in range(chains):
            keep_a, got_a, keep_b, got_b = refs[4 * chain : 4 * chain + 4]
            out[chain][...] = keep_a[...].astype(F32) + got_a[...].astype(F32)
            give = (keep_b[...].astype(F32) + got_b[...].astype(F32)).astype(BF16)
            if self.joint:
                size = give.shape[0]
                out[chains][chain * size : (chain + 1) * size] = give
            else:
                out[chains + chain][...] = give


def alone_kernel():
    pass


class LastRider:
    halves = None

    def __init__(self, keeps, gots):
        self.count, self.joint = len(keeps), len(gots) < len(keeps)
        self.args = [*keeps, *gots]
        self.specs = [whole(array.shape) for array in self.args]
        self.out = [(whole(keep.shape[1:]), keep.shape[1:], F32) for keep in keeps]

    def body(self, refs, out):
        last_sum_kernel(self.count, self.joint, *refs, *out)


def last_sum_kernel(count, joint, *refs):
    arrived = 1 if joint else count
    keeps, gots, out = refs[:count], refs[count : count + arrived], refs[count + arrived :]
    for chain in range(count):
        value = keeps[chain][0].astype(F32) + (gots[0][chain] if joint else gots[chain][0]).astype(F32)
        at = 0
        while at < value.shape[1]:
            out[0][...] = value[:, at : at + out[0].shape[1]]
            at += out[0].shape[1]
            out = out[1:]


def last_sum(keeps, gots, widths):
    piece = keeps[0].shape[1]
    arrays = [*keeps, *gots]
    return call(
        functools.partial(last_sum_kernel, len(keeps), len(gots) < len(keeps)), "last_sum", (1,),
        [whole(array.shape) for array in arrays],
        [(whole((piece, width)), (piece, width), F32) for width in widths], arrays,
    )


def gelu_parts(z):
    spread = jnp.exp2(z * z * (-0.5 * LOG2E))
    t = 1.0 / (1.0 + (0.3275911 * 0.7071067811865476) * jnp.abs(z))
    poly = t * (0.254829592 + t * (-0.284496736 + t * (1.421413741 + t * (-1.453152027 + t * 1.061405429))))
    tail = 0.5 * poly * spread
    return jnp.where(z >= 0, 1.0 - tail, tail), spread


def hidden_pair(z, hidden_grad):
    phi, spread = gelu_parts(z)
    return (z * phi).astype(BF16), hidden_grad * (phi + z * spread * 0.3989422804014327)


def upstream_kernel(cot_ref, down_ref, up_ref, out_ref, sum_ref, pack_hbm, sems):
    d = up_ref.shape[0]
    copies = [
        pltpu.make_async_copy(up_ref, pack_hbm.at[pl.ds(0, d)], sems.at[0]),
        pltpu.make_async_copy(down_ref, pack_hbm.at[pl.ds(d, down_ref.shape[0])], sems.at[1]),
    ]

    @pl.when(pl.program_id(0) == 0)
    def _():
        for copy in copies:
            copy.start()

    cot = cot_ref[...]
    out_ref[...] = mm(cot, down_ref[...], NT).astype(BF16)
    gather_rows(sum_ref, pl.program_id(0) == 0, cot)

    @pl.when(pl.program_id(0) == pl.num_programs(0) - 1)
    def _():
        for copy in copies:
            copy.wait()


def upstream(cot, up, down):
    tokens, d = cot.shape
    f = down.shape[0]
    tile = tokens // 4
    stay = pl.BlockSpec(memory_space=pl.ANY)
    return call(
        upstream_kernel, "upstream", (4,), [rows(tile, d), whole(down.shape), whole(up.shape)],
        [(rows(tile, f), (tokens, f), BF16), (whole((1, d)), (1, d), F32), (stay, (d + f, d), BF16, True)],
        (cot, down, up), scratch=[pltpu.SemaphoreType.DMA((2,))],
    )


def hidden_kernel(
    orders, x_ref, part_a_ref, part_b_ref, b_out_ref, gain_ref, bias_ref, up_ref, b_up_ref, cot_down_ref, *rest
):
    first = pl.program_id(0) == 0
    if orders:
        half_ref, cot_ref, rest_cot, rest = rest[0], rest[1], rest[2:3], rest[2:]
        earlier, rest = rest[1:-11], rest[-11:]
        up_keep_ref, up_give_ref, down_keep_ref, down_give_ref, up_acc, down_acc = rest[-6:]
        rest = rest[:-6]
    residual_ref, n2_ref, hidden_ref, upg_ref, sum_ref = rest[-5:]
    residual = (
        x_ref[...].astype(F32) + (part_a_ref[...].astype(F32) + part_b_ref[...].astype(F32)) + flat(b_out_ref)
    )
    residual_ref[...] = residual.astype(BF16)
    unit, _ = norm_stats(residual)
    normed = (unit * flat(gain_ref) + flat(bias_ref)).astype(BF16)
    n2_ref[...] = normed
    hidden, grad = hidden_pair(mm(normed, up_ref[...], NN) + flat(b_up_ref), cot_down_ref[...].astype(F32))
    up_grad = grad.astype(BF16)
    hidden_ref[...] = hidden
    upg_ref[...] = up_grad
    gather_rows(sum_ref, first, grad)
    if not orders:
        return

    @pl.when(first)
    def _():
        up_acc[...] = jnp.zeros_like(up_acc)
        down_acc[...] = jnp.zeros_like(down_acc)

    if earlier:
        n2_old, hidden_old, upg_old, cot_old = earlier[-3:] + rest_cot
        both = lambda one, two: jnp.concatenate([one, two], 0)
        up_acc[...] += mm(both(n2_old[...], normed), both(upg_old[...], up_grad), TN)
        down_acc[...] += mm(both(cot_old[...], cot_ref[...]), both(hidden_old[...], hidden), TN)
    else:
        up_acc[...] += mm(normed, up_grad, TN)
        down_acc[...] += mm(cot_ref[...], hidden, TN)

    @pl.when(pl.program_id(0) == pl.num_programs(0) - 1)
    def _():
        split_chunks(half_ref[0], orders[0], up_acc, up_keep_ref, up_give_ref)
        split_chunks(half_ref[1], orders[1], down_acc, down_keep_ref, down_give_ref)


def hidden_own(sequence, length, x, part_a, part_b, b_out, gain, bias, up, b_up, cot_down, carried=(), weights=()):
    tokens, d = x.shape
    f = up.shape[1]
    count = 4
    tile = length // count
    tall, wide = rows(tile, d, count * sequence), rows(tile, f, count * sequence)
    near = rows(tile, d)
    specs = [tall, near, near] + [whole((d,))] * 3 + [whole(up.shape), whole((f,)), wide]
    out = [(tall, (tokens, d), BF16, True)] * 2 + [(wide, (tokens, f), BF16, True)] * 2 + [(whole((1, f)), (1, f), F32)]
    args = [x, part_a, part_b, b_out, gain, bias, up, b_up, cot_down]
    orders, scratch, earlier = None, [], ()
    if weights:
        orders, halves, cot = weights
        half_count = len(orders[0][0])
        chunk = (half_count, d // (2 * half_count), f)
        specs += [pl.BlockSpec(memory_space=pltpu.SMEM), tall]
        args += [halves, cot]
        specs.append(rows(tile, d))
        args.append(cot)
        earlier = [pl.BlockSpec(memory_space=pl.ANY), rows(tile, d), rows(tile, f), rows(tile, f)]
        out += [(whole(chunk), chunk, BF16)] * 4
        scratch = [pltpu.VMEM((d, f), F32)] * 2
    return call(
        functools.partial(hidden_kernel, orders), "hidden_own", (count,), specs, out, args, scratch=scratch, carried=carried,
        carried_specs=earlier,
    )


def products_kernel(
    n2_ref, cot_ref, hidden_ref, upg_ref, up_a_ref, down_a_ref, far_ref, bias_ref, *rest
):
    mlp_ref, n2g_ref = rest[-2:]
    d = n2_ref.shape[1]
    up_b, down_b = far_ref[:d, :], far_ref[d:, :]
    z = mm(n2_ref[...], up_b, NN) + bias_of(bias_ref, 0)
    hidden_grad = mm(cot_ref[...], down_b, NT)
    mlp_own = mm(hidden_ref[...], down_a_ref[...], NN)
    n2g_own = mm(upg_ref[...], up_a_ref[...], NT)
    hidden, grad = hidden_pair(z, hidden_grad)
    mlp_ref[...] = (mlp_own + mm(hidden, down_b, NN)).astype(BF16)
    n2g_ref[...] = (n2g_own + mm(grad.astype(BF16), up_b, NT)).astype(BF16)


def products(span, n2, cot, hidden, upg, up, down, far, bias, carried=(), rider=None):
    tokens = n2.shape[0]
    d, f = up.shape
    first, count = span
    tall, wide = rows(TILE, d, first), rows(TILE, f, first)
    return call(
        products_kernel, "feed_forward", (count,),
        [tall, tall, wide, wide, whole(up.shape), whole(down.shape), whole(far.shape), biases(bias)],
        [(tall, (tokens, d), BF16, True), (rows(TILE, d), (count * TILE, d), BF16)],
        (n2, cot, hidden, upg, up, down, far, bias), carried=carried, cover=True, rider=rider,
    )


def middle_kernel(residual_ref, grad_a_ref, grad_b_ref, cot_ref, gain_ref, own_w_ref, far_w_ref, *rest):
    agrad_ref, own_cg_ref, far_cg_ref, sum_ref = rest[-4:]
    unit, scale = norm_stats(residual_ref[...].astype(F32))
    summed = grad_a_ref[...].astype(F32) + grad_b_ref[...].astype(F32)
    rgrad = cot_ref[...].astype(F32) + norm_back(unit, scale, summed * flat(gain_ref))
    agrad = rgrad.astype(BF16)
    agrad_ref[...] = agrad
    own_cg_ref[...] = mm(agrad, own_w_ref[...], NT).astype(BF16)
    far_cg_ref[...] = mm(agrad, far_w_ref[...], NT).astype(BF16)
    gather_rows(sum_ref, pl.program_id(0) == 0, rgrad, summed * unit, summed)


def middle(span, residual, grad_a, grad_b, cot, gain, own_w, far_w, carried=(), rider=None):
    tokens, d = residual.shape
    own = own_w.shape[1] // 4
    first, count = span
    tall, slim, near = rows(TILE, d, first), rows(TILE, own, first), rows(TILE, d)
    return call(
        middle_kernel, "second_norm_back", (count,),
        [tall, near, near, tall, whole((d,)), out_weights(own_w), out_weights(far_w)],
        [(tall, (tokens, d), BF16), (slim, (tokens, own), BF16), (slim, (tokens, own), BF16, True), (whole((3, d)), (3, d), F32)],
        (residual, grad_a, grad_b, cot, gain, own_w, far_w), carried=carried, rider=rider,
    )


def output_kernel(residual_ref, mlp_a_ref, mlp_b_ref, b_down_ref, out_ref):
    out_ref[...] = (
        residual_ref[...].astype(F32)
        + ((mlp_a_ref[...].astype(F32) + mlp_b_ref[...].astype(F32)) + flat(b_down_ref))
    ).astype(BF16)


def output(residual, mlp_a, mlp_b, b_down):
    tokens, d = residual.shape
    tall = rows(TILE, d)
    return call(
        output_kernel, "block_output", (tokens // TILE,), [tall] * 3 + [whole((d,))],
        [(tall, (tokens, d), BF16)], (residual, mlp_a, mlp_b, b_down), cover=True,
    )[0]


def first_back_kernel(x_ref, grad_a_ref, grad_b_ref, rgrad_ref, gain_ref, *rest):
    unit, scale = norm_stats(x_ref[...].astype(F32))
    upstream = (grad_a_ref[...].astype(F32) + grad_b_ref[...].astype(F32)) * flat(gain_ref)
    rest[-1][...] = rgrad_ref[...].astype(F32) + norm_back(unit, scale, upstream)


def first_back(span, x, grad_a, grad_b, rgrad, gain, carried=()):
    tokens, d = x.shape
    first, count = span
    tall = rows(TILE // 2, d, 2 * first)
    return call(
        first_back_kernel, "first_norm_back", (2 * count,), [tall] * 4 + [whole((d,))],
        [(tall, (tokens, d), F32)], (x, grad_a, grad_b, rgrad, gain), carried=carried,
    )


def swap(value, axis, size, bit):
    return lax.ppermute(value, axis, [(i, i ^ bit) for i in range(size)])


def tie(value, *others):
    return lax.optimization_barrier((value,) + others)[0]


class ScatterSums:
    def __init__(self, size, *chains):
        self.size = size
        self.keeps, self.gives, bits = [list(part) for part in zip(*chains)]
        self.bits = [list(each) for each in bits]
        self.me = lax.axis_index("dp").astype(jnp.int32)

    def begin(self):
        bits = [each.pop(0) for each in self.bits]
        self.gots = [swap(give, "dp", self.size, 1 << bit) for give, bit in zip(self.gives, bits)]

    def rider(self, *others):
        self.gots = [tie(got, *others) if others else got for got in self.gots]
        mine = jnp.stack([(self.me >> bits[0]) & 1 for bits in self.bits])
        return Rider(mine, self.keeps, self.gots, len({bits[0] for bits in self.bits}) < len(self.bits))

    def take(self, results):
        self.keeps, self.gives = results[: len(self.keeps)], results[len(self.keeps) :]

    def end(self, *others):
        if self.bits[0]:
            self.take(call(alone_kernel, "merge", (1,), [], [], [], rider=self.rider(*others)))
        else:
            self.gots = [tie(got, *others) if others else got for got in self.gots]
        return self.gots

    def finish(self, *widths):
        while self.bits[0]:
            self.begin()
            self.end()
        return last_sum(self.keeps, self.gots, widths)


def body(
    n_dp,
    n_mp,
    block_input,
    segment_ids,
    group_ids,
    padding,
    ln1_gain,
    ln1_bias,
    w_qkv,
    b_qv,
    w_out,
    b_out,
    ln2_gain,
    ln2_bias,
    w_up,
    b_up,
    w_down,
    b_down,
    cotangent,
):
    tokens, d = block_input.shape
    sequences, length = segment_ids.shape
    own = w_qkv.shape[2]
    far = lambda value: swap(value, "mp", n_mp, 2)
    near = lambda value: swap(value, "mp", n_mp, 1)
    levels = n_dp.bit_length() - 1
    bits = list(range(levels))
    other_bits = [1, 0] + bits[2:]
    me = lax.axis_index("dp").astype(jnp.int32)
    halves = jnp.stack([me & 1, (me >> 1) & 1])
    orders = (chunk_order(n_dp, bits), chunk_order(n_dp, other_bits))

    small = jnp.stack([b_up, jnp.pad(b_qv.reshape(-1), (0, d - 2 * own))])
    parts = []
    for _ in range(3):
        parts.append(lax.reduce_precision(small, 8, 7))
        small = small - parts[-1]
    small = jnp.pad(jnp.stack(parts, 1).reshape(6, d).astype(BF16), ((0, 10), (0, 0)))
    pack = jnp.concatenate([jnp.transpose(w_qkv, (1, 2, 0)).reshape(3 * own, d), w_out, small], 0)
    pack_far = far(pack)
    table = tables(segment_ids, group_ids, padding)

    *saved_own, n1 = attend_own(table, block_input, ln1_gain, ln1_bias, pack, b_qv)
    ctx_own = saved_own[0]
    cot_down, sum_cot, mlp_own = upstream(tie(cotangent, n1), w_up, w_down)
    mlp_far = far(mlp_own)
    parts, saved_far = [], ()
    for s in range(sequences):
        *saved_far, part = attend_far(s, table, n1, tie(pack_far, cot_down), ctx_own, pack, saved_far)
        parts.append((part, near(part)))
    carried, sums_up = (), []
    for s, (part, other) in enumerate(parts):
        other = tie(other, carried[0] if carried else parts[-1][0])
        weights = (orders, halves, cotangent) if s == sequences - 1 else ()
        *carried, = hidden_own(
            s, length, block_input, part, other, b_out, ln2_gain, ln2_bias, w_up, b_up, cot_down, carried[:4], weights
        )
        sums_up.append(carried[4])
    residual, n2, hidden, upg, _, up_keep, up_give, down_keep, down_give = carried
    sum_mlp = ScatterSums(n_dp, (up_keep, up_give, bits), (down_keep, down_give, other_bits))
    sum_mlp.begin()
    mlp_far = tie(mlp_far, up_keep)
    tiles = tokens // TILE
    shares, mlp, gate, rider = [], (), (up_keep,), None
    for span in ((0, tiles - 1), (tiles - 1, 1)):
        results = products(
            span, tie(n2, *gate), cotangent, hidden, upg, w_up, w_down, mlp_far, pack_far, mlp, rider
        )
        *mlp, n2g = results[:2]
        shares.append((span, n2g, near(n2g)))
        if rider:
            sum_mlp.take(results[2:])
        else:
            gate, rider = (n2g,), sum_mlp.rider(n2g)
    sum_mlp.begin()
    gate, carried, sums_mid, rider = (n2g,), (), [], None
    for span, n2g, other in shares:
        results = middle(
            span, residual, n2g, tie(other, *gate), cotangent, ln2_gain, pack, pack_far, carried, rider
        )
        *carried, sum_mid = results[:4]
        sums_mid.append(sum_mid)
        if rider:
            sum_mlp.take(results[4:])
        else:
            gate, rider = (carried[0],), sum_mlp.rider(sum_mid)
    sum_mlp.begin()
    agrad, cgrad_own, cgrad_far = carried
    ctx, lse, q, k, v = saved_own
    *own_grads, keep, give, sum_qv = attend_own_back(
        table, halves[:1], orders[0], q, k, v, ctx, cgrad_own, lse, n1, agrad
    )
    mlp_near = near(mlp[0])
    sum_attn = ScatterSums(n_dp, (keep, give, bits))
    sum_attn.begin()
    got = sum_mlp.end(keep)
    while sum_mlp.bits[0]:
        sum_mlp.begin()
        sum_mlp.end()
    ctx, lse, q, k, v = saved_far
    n1g, sum_first, up_sum, down_sum = attend_far_back(
        table, q, k, v, ctx, tie(cgrad_far, keep, *got), lse, block_input, own_grads, pack, pack_far,
        LastRider(sum_mlp.keeps, sum_mlp.gots),
    )
    got = sum_attn.end(n1g)
    sum_attn.begin()
    sum_first = tie(sum_first, *sum_attn.gives)
    sum_first = sum_first + near(sum_first)
    n1g_near = near(tie(n1g, sum_first))
    add = lambda values: functools.reduce(jnp.add, values)
    wide_qv = jnp.concatenate([sum_qv.reshape(1, -1), jnp.zeros((1, d - 2 * own), F32)], 1)
    sums = jnp.concatenate([sum_first, add(sums_mid), sum_cot, add(sums_up), wide_qv], 0)
    other = swap(sums, "dp", n_dp, 1)
    block_output = output(tie(residual, n1g, *got, sums), mlp[0], mlp_near, b_down)
    sums = sums + tie(other, block_output)
    other = swap(sums, "dp", n_dp, 2)
    got = sum_attn.end(block_output, sums)
    sum_attn.begin()
    outputs = first_back((0, tiles - 1), block_input, n1g, tie(n1g_near, block_output, *got, sums), agrad, ln1_gain)
    sums = sums + tie(other, *outputs)
    if levels > 2:
        other = swap(sums, "dp", n_dp, 4)
    got = sum_attn.end(*outputs)
    qkv_sum, out_sum = sum_attn.finish(3 * own, own)
    input_grad, = first_back((tiles - 1, 1), block_input, n1g, tie(n1g_near, sums, qkv_sum), agrad, ln1_gain, outputs)
    if levels > 2:
        sums = sums + tie(other, input_grad)
    for bit in range(3, levels):
        sums = sums + swap(sums, "dp", n_dp, 1 << bit)

    piece, tiny = d // n_dp, own // n_dp
    mine = lax.dynamic_slice(sums, (0, me * piece), (sums.shape[0] - 1, piece))
    vectors = [mine[i] for i in range(7)]
    return (
        block_output,
        input_grad,
        vectors[0],
        vectors[1],
        qkv_sum.reshape(piece, 3, own),
        lax.dynamic_slice(sums[7, : 2 * own].reshape(2, own), (0, me * tiny), (2, tiny)),
        out_sum.T,
        vectors[2],
        vectors[3],
        vectors[4],
        up_sum,
        vectors[6],
        down_sum.T,
        vectors[5],
    )


def solution(mesh):
    return jax.shard_map(
        functools.partial(body, mesh.shape["dp"], mesh.shape["mp"]),
        mesh=mesh,
        in_specs=(
            P("dp", None),
            P("dp", None),
            P("dp", None),
            P("dp", None),
            P(),
            P(),
            P(None, None, "mp"),
            P(None, "mp"),
            P("mp", None),
            P(),
            P(),
            P(),
            P(None, "mp"),
            P("mp"),
            P("mp", None),
            P(),
            P("dp", None),
        ),
        out_specs=(
            P("dp", None),
            P("dp", None),
            P("dp"),
            P("dp"),
            P("dp", None, "mp"),
            P(None, ("mp", "dp")),
            P("mp", "dp"),
            P("dp"),
            P("dp"),
            P("dp"),
            P("dp", "mp"),
            P(("mp", "dp")),
            P("mp", "dp"),
            P("dp"),
        ),
        check_vma=False,
    )
```
